128 devices in a mesh: image: 8 (over x, core), space: 16 (over y, z).
Axes of the slice: x: 4, y: 4, z: 4, core: 2. Of those that a mesh axis runs over, the one named last changes fastest.
Arguments:
- positions: float32 [16, 3, 4096], P('image', None, 'space'), may hold values from -6 to 6
- velocity: float32 [16, 3, 4096], P('image', None, 'space'), may hold values from -4 to 4
- start_state: float32 [3, 4096], P(None, 'space'), may hold values from -6 to 6
- end_state: float32 [3, 4096], P(None, 'space'), may hold values from -6 to 6
- neighbours: int32 [16, 16, 4096], P('image', None, 'space'), may hold values from 0 to 511, as said below
- counts: int32 [16, 4096], P('image', 'space'), may hold values from 1 to 16, as said below
- climb_index: int32 [1], replicated, may hold values from 0 to 15
- radial_a1: float32 [8, 64], replicated, may hold values from -2 to 2
- radial_b1: float32 [64, 128], replicated, may hold values from -0.75 to 0.75
- mix_first: float32 [384, 128], replicated, may hold values from -0.5 to 0.5
- read_first: float32 [128], replicated, may hold values from -0.5 to 0.5
- radial_a2: float32 [8, 64], replicated, may hold values from -2 to 2
- radial_b2: float32 [64, 128], replicated, may hold values from -0.75 to 0.75
- mix_second: float32 [384, 128], replicated, may hold values from -0.5 to 0.5
- read_second: float32 [128], replicated, may hold values from -0.5 to 0.5
Outputs:
- neb_force: float32 [16, 3, 4096], P('image', None, 'space')
- velocity_next: float32 [16, 3, 4096], P('image', None, 'space')
- position_next: float32 [16, 3, 4096], P('image', None, 'space')
- image_energy: float32 [16], P('image')
The draws below stay inside these ranges and needn't reach their ends.
Inputs may be any that keep to these rules, and one draw needn't show every extreme that they name: `neighbours`: A slab's extended atoms are, in order, the last 128 atoms of the slab below, its own 256 atoms, and the first 128 atoms of the slab above; the first and last slabs are beside each other. `counts`: atoms in the middle of the image have a higher least number of live neighbours than those at its ends.
All inputs are finite; a program needn't handle non-finite values.
Results may differ from the reference program's by a relative error of at most 0.0003.
Values sent between devices are 32-bit elements; how exact they have to be, the bound alone decides.
No kernel may reach another device: no remote copies, remote signals or barrier semaphores. Data moves between devices by JAX's collectives and lax.ppermute only.
A program may use at most 64 MiB of HBM per device.

```python
import math
import jax
import jax.numpy as jnp
from jax import lax

CH = 128
RH = 64
NB = 8
NBR = 16
ATOMS_DEV = 256
GHOST = 128
IMAGES = 16
ATOMS = 4096


def draw_neighbours(key, part):
    extent = ATOMS_DEV + 2 * GHOST
    picked = jax.random.randint(key, (IMAGES, NBR, ATOMS), 0, extent).astype(jnp.int32)
    picked = picked.at[:, 0, 0].set(extent - 1)
    return picked.at[:, 1, 0].set(0)


def draw_counts(key, part):
    atom = jnp.arange(ATOMS).astype(jnp.int32)
    lowest = 1 + (NBR - 1) * (ATOMS - jnp.abs(2 * atom - ATOMS)) // ATOMS
    raw = jax.random.randint(jax.random.fold_in(key, 7), (IMAGES, ATOMS), 0, 1 << 20).astype(jnp.int32)
    widths = NBR - lowest + 1
    drawn = (lowest[None] + raw % widths[None]).astype(jnp.int32)
    return drawn.at[:, 0].set(1)


def block_scale(rng, shape, cuts, low, top_value):
    level = 1.0
    for axis_at, parts in cuts:
        draws = jax.random.uniform(jax.random.fold_in(jax.random.fold_in(rng, 6), axis_at), (parts,), jnp.float32, low / len(cuts), top_value / len(cuts))
        level = level * jnp.repeat(jnp.exp(draws), shape[axis_at] // parts).reshape((-1,) + (1,) * (len(shape) - 1 - axis_at))
    return level


def scatter_about(rng, dims, scale, limit, pieces=(), kind=jnp.bfloat16):
    result = scale * jax.random.normal(rng, dims, jnp.float32)
    if pieces:
        result = result * block_scale(rng, dims, pieces, -0.22, 0.18)
    return jnp.clip(result, -limit, limit).astype(kind)


def setup_inputs(seed: int = 0) -> dict:
    arg_keys = jax.random.split(jax.random.key(seed), 16)
    return {
        "positions": scatter_about(arg_keys[0], (IMAGES, 3, ATOMS), 1.0, 6.0, ((0, 8), (2, 16)), jnp.float32),
        "velocity": scatter_about(arg_keys[1], (IMAGES, 3, ATOMS), 0.5, 4.0, ((0, 8), (2, 16)), jnp.float32),
        "start_state": scatter_about(arg_keys[2], (3, ATOMS), 1.0, 6.0, ((1, 16),), jnp.float32),
        "end_state": scatter_about(arg_keys[3], (3, ATOMS), 1.0, 6.0, ((1, 16),), jnp.float32),
        "neighbours": draw_neighbours(jax.random.fold_in(arg_keys[15], 71), 0),
        "counts": draw_counts(jax.random.fold_in(arg_keys[15], 71), 0),
        "climb_index": jax.random.randint(arg_keys[6], (1,), 0, IMAGES).astype(jnp.int32),
        "radial_a1": scatter_about(arg_keys[7], (NB, RH), NB ** -0.5, 2.0, (), jnp.float32),
        "radial_b1": scatter_about(arg_keys[8], (RH, CH), RH ** -0.5, 0.75, (), jnp.float32),
        "mix_first": scatter_about(arg_keys[9], (3 * CH, CH), CH ** -0.5, 0.5, (), jnp.float32),
        "read_first": scatter_about(arg_keys[10], (CH,), CH ** -0.5, 0.5, (), jnp.float32),
        "radial_a2": scatter_about(arg_keys[11], (NB, RH), NB ** -0.5, 2.0, (), jnp.float32),
        "radial_b2": scatter_about(arg_keys[12], (RH, CH), RH ** -0.5, 0.75, (), jnp.float32),
        "mix_second": scatter_about(arg_keys[13], (3 * CH, CH), CH ** -0.5, 0.5, (), jnp.float32),
        "read_second": scatter_about(arg_keys[14], (CH,), CH ** -0.5, 0.5, (), jnp.float32),
    }


highest = lax.Precision.HIGHEST

def harmonics(unit):
    ux = unit[0]
    uy = unit[1]
    uz = unit[2]
    return jnp.stack([jnp.ones_like(ux), ux, uy, uz, ux * uy, uy * uz, ux * uz, 0.5 * (ux * ux - uy * uy), (3.0 * uz * uz - 1.0) / (2.0 * math.sqrt(3.0))])

def layer_out(center, nb_pos, live_mask, radial_a, radial_b, mixing, nb_feat):
    offset = nb_pos - center[:, None, :]
    length = jnp.sqrt(lax.optimization_barrier(jnp.sum(offset * offset, axis=0)) + 1.0)
    angular = harmonics(offset / length[None])
    centres = 0.5 * jnp.arange(radial_a.shape[0]).astype(center.dtype)
    spread = length[None] - centres[:, None, None]
    basis = jnp.exp(-spread * spread / 0.5)
    hidden = jax.nn.silu(jnp.einsum('bka,bh->hka', basis, radial_a, precision=highest))
    radial = jnp.einsum('hka,hc->cka', hidden, radial_b, precision=highest) * live_mask[None]
    if nb_feat is not None:
        radial = radial * nb_feat
    moments = jnp.einsum('cka,lka->cla', radial, angular, precision=highest) / live_mask.shape[0]
    invariants = jnp.concatenate([moments[:, 0], lax.optimization_barrier(jnp.sum(moments[:, 1:4] * moments[:, 1:4], axis=1)), lax.optimization_barrier(jnp.sum(moments[:, 4:9] * moments[:, 4:9], axis=1))], axis=0)
    return jax.nn.silu(jnp.einsum('fa,fc->ca', invariants, mixing, precision=highest))

def reference(positions, velocity, start_state, end_state, neighbours, counts, climb_index, radial_a1, radial_b1, mix_first, read_first, radial_a2, radial_b2, mix_second, read_second):

    def total_energy(image_pos, nb_idx, live_mask):
        atoms = image_pos.shape[1]
        slab = jnp.arange(atoms).astype(jnp.int32) // ATOMS_DEV
        global_nb = ((slab[None] * ATOMS_DEV + nb_idx - GHOST) % atoms).astype(jnp.int32)
        nb_pos = image_pos[:, global_nb]
        first = layer_out(image_pos, nb_pos, live_mask, radial_a1, radial_b1, mix_first, None)
        second = layer_out(image_pos, nb_pos, live_mask, radial_a2, radial_b2, mix_second, first[:, global_nb])
        return jnp.sum(read_first[:, None] * first) + jnp.sum(read_second[:, None] * second)

    def per_image(items):
        image_pos, nb_idx, live_count = items
        slots = lax.broadcasted_iota(jnp.int32, nb_idx.shape, 0)
        live_mask = (slots < live_count[None]).astype(image_pos.dtype)
        energy, grad_pos = jax.value_and_grad(total_energy)(image_pos, nb_idx, live_mask)
        return (energy, -grad_pos)
    energies, forces = lax.map(per_image, (positions, neighbours, counts))
    prev_pos = jnp.concatenate([start_state[None], positions[:-1]], axis=0)
    next_pos = jnp.concatenate([positions[1:], end_state[None]], axis=0)
    spread = next_pos - prev_pos
    ahead = next_pos - positions
    behind = positions - prev_pos
    dist_ahead = lax.optimization_barrier(jnp.sum(ahead * ahead, axis=(1, 2)))
    dist_behind = lax.optimization_barrier(jnp.sum(behind * behind, axis=(1, 2)))
    spread_sq = lax.optimization_barrier(jnp.sum(spread * spread, axis=(1, 2)))
    tangent = spread / jnp.sqrt(spread_sq + 1e-06)[:, None, None]
    along = lax.optimization_barrier(jnp.sum(forces * tangent, axis=(1, 2)))
    spring = 5.0 * (jnp.sqrt(dist_ahead) - jnp.sqrt(dist_behind))
    climbing = (jnp.arange(positions.shape[0]).astype(jnp.int32) == climb_index[0]).astype(positions.dtype)
    coef = -(1.0 + climbing) * along + (1.0 - climbing) * spring
    neb_force = forces + coef[:, None, None] * tangent
    vel_sq = jnp.sum(velocity * velocity)
    force_sq = jnp.sum(neb_force * neb_force)
    velocity_next = 0.9 * velocity + 0.1 * jnp.sqrt(vel_sq / (force_sq + 1e-06)) * neb_force + 0.1 * neb_force
    position_next = positions + 0.1 * velocity_next
    return (neb_force, velocity_next, position_next, energies / positions.shape[2])
```

```python
import functools
import math

import jax
import jax.numpy as jnp
from jax import lax
from jax.experimental import pallas as pl
from jax.experimental.pallas import tpu as pltpu
from jax.sharding import PartitionSpec as P

f32 = jnp.float32
bf16 = jnp.bfloat16
RT3 = math.sqrt(3.0)
NL = 9


def split(x):
    hi = x.astype(bf16)
    lo = (x - hi.astype(f32)).astype(bf16)
    return hi, lo


def dot(a, b):
    return lax.dot_general(a, b, (((1,), (0,)), ((), ())), preferred_element_type=f32)


def dot_nt(a, b):
    return lax.dot_general(a, b, (((1,), (1,)), ((), ())), preferred_element_type=f32)


def pack_left(w):
    hi, lo = split(w)
    return jnp.concatenate([hi, hi, lo], axis=1)


def pack_right(x):
    hi, lo = split(x)
    return jnp.concatenate([hi, lo, hi], axis=0)


def one_hot(row, extent):
    ids = lax.broadcasted_iota(jnp.int32, (extent, row.shape[1]), 0)
    return jnp.where(ids == row, 1.0, 0.0).astype(bf16)


def silu_parts(z):
    s = 0.5 + 0.5 * jnp.tanh(0.5 * z)
    h = z * s
    return h, s + h * (1.0 - s)


def basis_of(row, nb):
    centres = 0.5 * lax.broadcasted_iota(jnp.int32, (nb, row.shape[1]), 0).astype(f32)
    spread = row - centres
    basis = jnp.exp(-2.0 * spread * spread)
    return basis, -4.0 * spread * basis


def moments_into(edge_tile, yb_ref, m_ref, chans, slots, atoms):
    def tile(t, carry):
        c0 = pl.multiple_of(t * 16, 16)
        for a0 in range(0, atoms, 128):
            acc = [jnp.zeros((16, 128), f32) for _ in range(NL)]
            for k in range(slots):
                e = edge_tile(k, c0, a0)
                for l in range(NL):
                    y = yb_ref[k, l, :, a0 : a0 + 128]
                    acc[l] = acc[l] + e * jnp.concatenate([y, y], axis=0)
            for l in range(NL):
                m_ref[l, pl.ds(c0, 16), a0 : a0 + 128] = acc[l]
        return carry

    lax.fori_loop(0, chans // 16, tile, 0)


def store_yb(yb_ref, ylive, slots, atoms):
    for k in range(slots):
        for l in range(NL):
            yb_ref[k, l] = jnp.broadcast_to(ylive[l][k : k + 1], (8, atoms))


def invariants_of(m_ref):
    m = [m_ref[l] for l in range(NL)]
    one = m[1] * m[1] + m[2] * m[2] + m[3] * m[3]
    two = m[4] * m[4] + m[5] * m[5] + m[6] * m[6] + m[7] * m[7] + m[8] * m[8]
    return jnp.concatenate([m[0], one, two], axis=0)


def moment_grads_into(m_ref, dinv, chans):
    m_ref[0] = dinv[:chans]
    d1 = 2.0 * dinv[chans : 2 * chans]
    d2 = 2.0 * dinv[2 * chans :]
    for l in range(1, NL):
        m_ref[l] = m_ref[l] * (d1 if l < 4 else d2)


def first_kernel(
    pos_ref, plo_ref, pup_ref, idx_ref, cnt_ref, a_ref, b_ref, mix_ref, read_ref,
    head_ref, tail_ref, geo_ref, hid_ref, ds_ref, mom_ref, dpre_ref, en_ref,
    yb_ref, g_ref, nb_ref,
):
    slots, atoms = idx_ref.shape[1:]
    ghost = plo_ref.shape[2]
    nb, rh = a_ref.shape
    ch = b_ref.shape[1]
    pos = pos_ref[0]
    ext = jnp.concatenate([plo_ref[0], pos, pup_ref[0]], axis=1)
    extent = ext.shape[1]
    p1 = ext.astype(bf16)
    rest = ext - p1.astype(f32)
    p2 = rest.astype(bf16)
    p3 = (rest - p2.astype(f32)).astype(bf16)
    pad = jnp.zeros((5, extent), f32)
    pieces = jnp.concatenate(
        [jnp.concatenate([p.astype(f32), pad], axis=0) for p in (p1, p2, p3)], axis=0
    ).astype(bf16)
    for k in range(slots):
        oh = one_hot(idx_ref[0, k : k + 1, :], extent)
        got = dot(pieces, oh)
        for x in range(3):
            nb_ref[x, k : k + 1, :] = (
                got[x : x + 1] + got[8 + x : 9 + x] + got[16 + x : 17 + x]
            )
    off = [nb_ref[x] - pos[x : x + 1] for x in range(3)]
    length = jnp.sqrt(off[0] * off[0] + off[1] * off[1] + off[2] * off[2] + 1.0)
    ux, uy, uz = [o / length for o in off]
    ids = lax.broadcasted_iota(jnp.int32, (slots, atoms), 0)
    live = jnp.where(ids < cnt_ref[0], 1.0 / slots, 0.0).astype(f32)
    ylive = [
        live,
        live * ux,
        live * uy,
        live * uz,
        live * (ux * uy),
        live * (uy * uz),
        live * (ux * uz),
        live * (0.5 * (ux * ux - uy * uy)),
        live * ((3.0 * uz * uz - 1.0) / (2.0 * RT3)),
    ]
    for l in range(NL):
        geo_ref[0, l] = ylive[l]
    geo_ref[0, NL] = ux
    geo_ref[0, NL + 1] = uy
    geo_ref[0, NL + 2] = uz
    geo_ref[0, NL + 3] = length
    store_yb(yb_ref, ylive, slots, atoms)
    a_pack = pack_left(a_ref[...].T)
    for k in range(slots):
        basis, _ = basis_of(length[k : k + 1], nb)
        hid, ds = silu_parts(dot(a_pack, pack_right(basis)))
        hid_ref[0, k] = hid
        ds_ref[0, k] = ds

    def hid_tile(k, c0, a0):
        return hid_ref[0, k, pl.ds(c0, 16), a0 : a0 + 128]

    moments_into(hid_tile, yb_ref, g_ref, rh, slots, atoms)
    b_pack = pack_left(b_ref[...].T)
    for l in range(NL):
        mom_ref[0, l] = dot(b_pack, pack_right(g_ref[l]))
    inv = invariants_of(mom_ref.at[0])
    feat, dpre = silu_parts(dot(pack_left(mix_ref[...].T), pack_right(inv)))
    dpre_ref[0] = dpre
    head_ref[0] = feat[:, :ghost]
    tail_ref[0] = feat[:, atoms - ghost :]
    en = read_ref[...] * feat
    total = jnp.sum(en.reshape(ch // 8, 8, atoms), axis=0)
    en_ref[0] = total[:, :128] + total[:, 128:]


def edge_back(k, edge_tile, sink, yb_ref, m_ref, dy_ref, chans, atoms):
    for a0 in range(0, atoms, 128):
        y = [yb_ref[k, l, :, a0 : a0 + 128] for l in range(NL)]
        y = [jnp.concatenate([v, v], axis=0) for v in y]
        acc = [jnp.zeros((8, 128), f32) for _ in range(NL)]
        for c0 in range(0, chans, 16):
            e = edge_tile(k, c0, a0)
            de = None
            for l in range(NL):
                dm = m_ref[l, c0 : c0 + 16, a0 : a0 + 128]
                term = dm * y[l]
                de = term if de is None else de + term
                p = e * dm
                acc[l] = acc[l] + (p[:8] + p[8:])
            sink(k, c0, a0, de)
        for l in range(NL):
            dy_ref[0, l, k : k + 1, a0 : a0 + 128] = jnp.sum(acc[l], axis=0, keepdims=True)


def second_kernel(
    head_ref, tail_ref, hlo_ref, hup_ref, idx_ref, geo_ref, a_ref, b_ref, mix_ref, read_ref,
    dfh_ref, dft_ref, dlo_ref, dup_ref, dy_ref, dlen_ref, en_ref,
    yb_ref, hf_ref, oh_ref, q_ref, rad_ref, ds_ref, m_ref, dq_ref, dr_ref,
):
    slots, atoms = idx_ref.shape[1:]
    ghost = hlo_ref.shape[2]
    nb, rh = a_ref.shape
    ch = b_ref.shape[1]
    extent = atoms + 2 * ghost
    parts = (hlo_ref, head_ref, tail_ref, hup_ref)
    for n, ref in enumerate(parts):
        hi, lo = split(ref[0])
        hf_ref[:ch, n * ghost : (n + 1) * ghost] = hi
        hf_ref[ch:, n * ghost : (n + 1) * ghost] = lo
    store_yb(yb_ref, [geo_ref[0, l] for l in range(NL)], slots, atoms)
    a_pack = pack_left(a_ref[...].T)
    b_pack = pack_left(b_ref[...].T)
    for k in range(slots):
        oh = one_hot(idx_ref[0, k : k + 1, :], extent)
        oh_ref[:, k * atoms : (k + 1) * atoms] = oh
        got = dot(hf_ref[...], oh)
        q_ref[k] = got[:ch] + got[ch:]
        basis, _ = basis_of(geo_ref[0, NL + 3, k : k + 1, :], nb)
        hid, ds = silu_parts(dot(a_pack, pack_right(basis)))
        ds_ref[k] = ds
        rad_ref[k] = dot(b_pack, pack_right(hid))

    def edge_tile(k, c0, a0):
        cs = pl.ds(c0, 16)
        return rad_ref[k, cs, a0 : a0 + 128] * q_ref[k, cs, a0 : a0 + 128]

    moments_into(edge_tile, yb_ref, m_ref, ch, slots, atoms)
    inv = invariants_of(m_ref)
    mix = mix_ref[...]
    feat, dpre = silu_parts(dot(pack_left(mix.T), pack_right(inv)))
    en = read_ref[...] * feat
    total = jnp.sum(en.reshape(ch // 8, 8, atoms), axis=0)
    en_ref[0] = total[:, :128] + total[:, 128:]
    dpre = read_ref[...] * dpre
    dinv = dot(pack_left(mix), pack_right(dpre))
    moment_grads_into(m_ref, dinv, ch)
    bt_pack = pack_left(b_ref[...])
    at_pack = pack_left(a_ref[...])

    def slot(k):
        k0 = k * atoms

        def sink(kk, c0, a0, de):
            cs = slice(c0, c0 + 16)
            hi, lo = split(de * rad_ref[kk, cs, a0 : a0 + 128])
            ls = slice(k0 + a0, k0 + a0 + 128)
            dq_ref[cs, ls] = hi
            dq_ref[ch + c0 : ch + c0 + 16, ls] = lo
            hi, lo = split(de * q_ref[kk, cs, a0 : a0 + 128])
            dr_ref[cs, a0 : a0 + 128] = hi
            dr_ref[ch + c0 : ch + c0 + 16, a0 : a0 + 128] = lo
            dr_ref[2 * ch + c0 : 2 * ch + c0 + 16, a0 : a0 + 128] = hi

        edge_back(k, edge_tile, sink, yb_ref, m_ref, dy_ref, ch, atoms)
        dz = dot(bt_pack, dr_ref[...]) * ds_ref[k]
        dbasis = dot(at_pack, pack_right(dz))
        _, slope = basis_of(geo_ref[0, NL + 3, k : k + 1, :], nb)
        dlen_ref[0, k : k + 1, :] = jnp.sum(dbasis * slope, axis=0, keepdims=True)

    for k in range(slots):
        slot(k)
    back = dot_nt(dq_ref[...], oh_ref[...])
    back = back[:ch] + back[ch:]
    dlo_ref[0] = back[:, :ghost]
    dfh_ref[0] = back[:, ghost : 2 * ghost]
    dft_ref[0] = back[:, 2 * ghost : 3 * ghost]
    dup_ref[0] = back[:, 3 * ghost :]


def third_kernel(
    dfh_ref, dft_ref, rlo_ref, rup_ref, idx_ref, geo_ref, hid_ref, ds_ref, mom_ref, dpre_ref,
    dy2_ref, dlen2_ref, a_ref, b_ref, mix_ref, read_ref,
    own_ref, flo_ref, fup_ref,
    yb_ref, m_ref, dg_ref, dy_ref, dr_ref, dlen_ref, doff_ref,
):
    slots, atoms = idx_ref.shape[1:]
    ghost = rlo_ref.shape[2]
    nb, rh = a_ref.shape
    ch = b_ref.shape[1]
    extent = atoms + 2 * ghost
    store_yb(yb_ref, [geo_ref[0, l] for l in range(NL)], slots, atoms)
    cot = jnp.concatenate([dfh_ref[0] + rlo_ref[0], dft_ref[0] + rup_ref[0]], axis=1)
    dpre = (cot + read_ref[...]) * dpre_ref[0]
    dinv = dot(pack_left(mix_ref[...]), pack_right(dpre))
    for l in range(NL):
        m_ref[l] = mom_ref[0, l]
    moment_grads_into(m_ref, dinv, ch)
    bt_pack = pack_left(b_ref[...])
    at_pack = pack_left(a_ref[...])
    for l in range(NL):
        dg_ref[l] = dot(bt_pack, pack_right(m_ref[l]))

    def edge_tile(k, c0, a0):
        return hid_ref[0, k, pl.ds(c0, 16), a0 : a0 + 128]

    def slot(k):
        def sink(kk, c0, a0, de):
            cs = slice(c0, c0 + 16)
            hi, lo = split(de * ds_ref[0, kk, cs, a0 : a0 + 128])
            dr_ref[cs, a0 : a0 + 128] = hi
            dr_ref[rh + c0 : rh + c0 + 16, a0 : a0 + 128] = lo
            dr_ref[2 * rh + c0 : 2 * rh + c0 + 16, a0 : a0 + 128] = hi

        edge_back(k, edge_tile, sink, yb_ref, dg_ref, dy_ref, rh, atoms)
        dbasis = dot(at_pack, dr_ref[...])
        _, slope = basis_of(geo_ref[0, NL + 3, k : k + 1, :], nb)
        dlen_ref[k : k + 1, :] = jnp.sum(dbasis * slope, axis=0, keepdims=True)

    for k in range(slots):
        slot(k)
    live = geo_ref[0, 0]
    dy = [live * (dy_ref[0, l] + dy2_ref[0, l]) for l in range(NL)]
    ux, uy, uz, length = [geo_ref[0, NL + n] for n in range(4)]
    dux = dy[1] + uy * dy[4] + uz * dy[6] + ux * dy[7]
    duy = dy[2] + ux * dy[4] + uz * dy[5] - uy * dy[7]
    duz = dy[3] + uy * dy[5] + ux * dy[6] + RT3 * uz * dy[8]
    radial = dlen_ref[...] + dlen2_ref[0] - (dux * ux + duy * uy + duz * uz) / length
    doff = [du / length + radial * u for du, u in ((dux, ux), (duy, uy), (duz, uz))]
    centre = jnp.concatenate([jnp.sum(d, axis=0, keepdims=True) for d in doff], axis=0)
    for x in range(3):
        doff_ref[x] = doff[x]
    back = jnp.zeros((16, extent), f32)
    pad = jnp.zeros((5, atoms), f32)
    for k in range(slots):
        rows = jnp.concatenate([doff_ref[x, k : k + 1, :] for x in range(3)] + [pad], axis=0)
        hi = rows.astype(bf16).astype(f32)
        both = jnp.concatenate([hi, rows - hi], axis=0).astype(bf16)
        back = back + dot_nt(both, one_hot(idx_ref[0, k : k + 1, :], extent))
    force = back[8:11] + back[:3]
    own_ref[0] = centre - force[:, ghost : ghost + atoms]
    flo_ref[0] = -force[:, :ghost]
    fup_ref[0] = -force[:, ghost + atoms :]


def lane_row(values):
    lane = lax.broadcasted_iota(jnp.int32, (1, 128), 1)
    row = jnp.zeros((1, 128), f32)
    for n, v in enumerate(values):
        row = jnp.where(lane == n, v, row)
    return row


def total_of(x):
    return jnp.sum(jnp.sum(x, axis=1, keepdims=True), axis=0, keepdims=True)


def chain_of(pos_ref, before_ref, after_ref, start_ref, end_ref, edge_ref):
    count = pos_ref.shape[0]
    before = jnp.where(edge_ref[0] > 0, start_ref[...], before_ref[...])
    after = jnp.where(edge_ref[1] > 0, end_ref[...], after_ref[...])
    prev = [before] + [pos_ref[i] for i in range(count - 1)]
    nxt = [pos_ref[i] for i in range(1, count)] + [after]
    return prev, nxt


def partial_kernel(
    edge_ref, own_ref, rlo_ref, rup_ref, pos_ref, before_ref, after_ref, start_ref, end_ref,
    vel_ref, en1_ref, en2_ref, force_ref, send_ref,
):
    count = pos_ref.shape[0]
    prev, nxt = chain_of(pos_ref, before_ref, after_ref, start_ref, end_ref, edge_ref)
    values = []
    vel = jnp.zeros((1, 1), f32)
    for i in range(count):
        force = own_ref[i] + jnp.concatenate([rlo_ref[i], rup_ref[i]], axis=1)
        force_ref[i] = force
        spread = nxt[i] - prev[i]
        ahead = nxt[i] - pos_ref[i]
        behind = pos_ref[i] - prev[i]
        values += [
            total_of(ahead * ahead),
            total_of(behind * behind),
            total_of(spread * spread),
            total_of(force * force),
            total_of(force * spread),
            total_of(en1_ref[i]) + total_of(en2_ref[i]),
        ]
        v = vel_ref[i]
        vel = vel + total_of(v * v)
    send_ref[...] = jnp.broadcast_to(lane_row(values + [vel]), send_ref.shape)


def final_kernel(
    edge_ref, got_ref, climb_ref, force_ref, pos_ref, before_ref, after_ref, start_ref, end_ref,
    vel_ref, neb_ref, vnext_ref, pnext_ref, en_ref,
    *, images, slabs,
):
    count = pos_ref.shape[0]
    atoms = pos_ref.shape[2]
    me = edge_ref[2]
    prev, nxt = chain_of(pos_ref, before_ref, after_ref, start_ref, end_ref, edge_ref)
    rows = [
        jnp.sum(got_ref[g * slabs : (g + 1) * slabs, :], axis=0, keepdims=True)
        for g in range(images)
    ]
    table = jnp.concatenate(rows, axis=0)
    vel_sq = jnp.sum(table[:, 6 * count : 6 * count + 1], axis=0, keepdims=True)
    group = lax.broadcasted_iota(jnp.int32, (images, 1), 0)
    force_sq = jnp.zeros((1, 1), f32)
    mine = []
    for i in range(count):
        ahead, behind, spread_sq, ff, fd, energy = [
            table[:, 6 * i + n : 6 * i + n + 1] for n in range(6)
        ]
        norm = 1.0 / jnp.sqrt(spread_sq + 1e-06)
        along = fd * norm
        climbing = jnp.where(group * count + i == climb_ref[0], 1.0, 0.0).astype(f32)
        spring = 5.0 * (jnp.sqrt(ahead) - jnp.sqrt(behind))
        coef = -(1.0 + climbing) * along + (1.0 - climbing) * spring
        scale = coef * norm
        part = ff + 2.0 * coef * along + scale * scale * spread_sq
        force_sq = force_sq + jnp.sum(part, axis=0, keepdims=True)
        here = group == me
        mine.append(
            (
                jnp.sum(jnp.where(here, scale, 0.0), axis=0, keepdims=True),
                jnp.sum(jnp.where(here, energy, 0.0), axis=0, keepdims=True),
            )
        )
    gain = 0.1 * jnp.sqrt(vel_sq / (force_sq + 1e-06))
    for i in range(count):
        scale, energy = mine[i]
        neb = force_ref[i] + scale * (nxt[i] - prev[i])
        neb_ref[i] = neb
        vnext = 0.9 * vel_ref[i] + gain * neb + 0.1 * neb
        vnext_ref[i] = vnext
        pnext_ref[i] = pos_ref[i] + 0.1 * vnext
        en_ref[i] = jnp.broadcast_to(energy * (1.0 / (atoms * slabs)), (8, 128))


def per_image(shape):
    rank = len(shape)
    return pl.BlockSpec((1,) + shape, lambda i: (i,) + (0,) * rank)


def whole(shape):
    rank = len(shape)
    return pl.BlockSpec(shape, lambda i: (0,) * rank)


def out(*shape):
    return jax.ShapeDtypeStruct(shape, f32)


VMEM = pl.BlockSpec(memory_space=pltpu.VMEM)
SMEM = pl.BlockSpec(memory_space=pltpu.SMEM)


def neighbours_of(cells, axis):
    count = lax.axis_size(axis)
    up = [(i, (i + 1) % count) for i in range(count)]
    down = [((i + 1) % count, i) for i in range(count)]
    to_below, to_above = cells
    return lax.ppermute(to_above, axis, up), lax.ppermute(to_below, axis, down)


def local(
    positions,
    velocity,
    start_state,
    end_state,
    neighbours,
    counts,
    climb_index,
    radial_a1,
    radial_b1,
    mix_first,
    read_first,
    radial_a2,
    radial_b2,
    mix_second,
    read_second,
):
    images, _, atoms = positions.shape
    slots = neighbours.shape[1]
    ghost = atoms // 2
    nb, rh = radial_a1.shape
    ch = radial_b1.shape[1]
    extent = atoms + 2 * ghost
    space = lax.axis_size("space")
    chain = lax.axis_size("image")
    params = pltpu.CompilerParams(dimension_semantics=("arbitrary",))

    plo, pup = neighbours_of((positions[:, :, :ghost], positions[:, :, ghost:]), "space")
    before = lax.ppermute(positions[images - 1], "image", [(i, i + 1) for i in range(chain - 1)])
    after = lax.ppermute(positions[0], "image", [(i + 1, i) for i in range(chain - 1)])
    counts3 = counts.reshape(images, 1, atoms)
    read1 = read_first.reshape(ch, 1)
    read2 = read_second.reshape(ch, 1)
    geo_n = NL + 4

    head, tail, geo, hid, ds, mom, dpre, en1 = pl.pallas_call(
        first_kernel,
        grid=(images,),
        in_specs=[
            per_image((3, atoms)),
            per_image((3, ghost)),
            per_image((3, ghost)),
            per_image((slots, atoms)),
            per_image((1, atoms)),
            whole((nb, rh)),
            whole((rh, ch)),
            whole((3 * ch, ch)),
            whole((ch, 1)),
        ],
        out_specs=[
            per_image((ch, ghost)),
            per_image((ch, ghost)),
            per_image((geo_n, slots, atoms)),
            per_image((slots, rh, atoms)),
            per_image((slots, rh, atoms)),
            per_image((NL, ch, atoms)),
            per_image((ch, atoms)),
            per_image((8, 128)),
        ],
        out_shape=[
            out(images, ch, ghost),
            out(images, ch, ghost),
            out(images, geo_n, slots, atoms),
            out(images, slots, rh, atoms),
            out(images, slots, rh, atoms),
            out(images, NL, ch, atoms),
            out(images, ch, atoms),
            out(images, 8, 128),
        ],
        scratch_shapes=[
            pltpu.VMEM((slots, NL, 8, atoms), f32),
            pltpu.VMEM((NL, rh, atoms), f32),
            pltpu.VMEM((3, slots, atoms), f32),
        ],
        compiler_params=params,
        name="first",
    )(positions, plo, pup, neighbours, counts3, radial_a1, radial_b1, mix_first, read1)

    hlo, hup = neighbours_of((head, tail), "space")

    dfh, dft, dlo, dup, dy2, dlen2, en2 = pl.pallas_call(
        second_kernel,
        grid=(images,),
        in_specs=[per_image((ch, ghost))] * 4
        + [
            per_image((slots, atoms)),
            per_image((geo_n, slots, atoms)),
            whole((nb, rh)),
            whole((rh, ch)),
            whole((3 * ch, ch)),
            whole((ch, 1)),
        ],
        out_specs=[per_image((ch, ghost))] * 4
        + [
            per_image((NL, slots, atoms)),
            per_image((slots, atoms)),
            per_image((8, 128)),
        ],
        out_shape=[out(images, ch, ghost)] * 4
        + [
            out(images, NL, slots, atoms),
            out(images, slots, atoms),
            out(images, 8, 128),
        ],
        scratch_shapes=[
            pltpu.VMEM((slots, NL, 8, atoms), f32),
            pltpu.VMEM((2 * ch, extent), bf16),
            pltpu.VMEM((extent, slots * atoms), bf16),
            pltpu.VMEM((slots, ch, atoms), f32),
            pltpu.VMEM((slots, ch, atoms), f32),
            pltpu.VMEM((slots, rh, atoms), f32),
            pltpu.VMEM((NL, ch, atoms), f32),
            pltpu.VMEM((2 * ch, slots * atoms), bf16),
            pltpu.VMEM((3 * ch, atoms), bf16),
        ],
        compiler_params=params,
        name="second",
    )(head, tail, hlo, hup, neighbours, geo, radial_a2, radial_b2, mix_second, read2)

    rlo, rup = neighbours_of((dlo, dup), "space")

    own, flo, fup = pl.pallas_call(
        third_kernel,
        grid=(images,),
        in_specs=[per_image((ch, ghost))] * 4
        + [
            per_image((slots, atoms)),
            per_image((geo_n, slots, atoms)),
            per_image((slots, rh, atoms)),
            per_image((slots, rh, atoms)),
            per_image((NL, ch, atoms)),
            per_image((ch, atoms)),
            per_image((NL, slots, atoms)),
            per_image((slots, atoms)),
            whole((nb, rh)),
            whole((rh, ch)),
            whole((3 * ch, ch)),
            whole((ch, 1)),
        ],
        out_specs=[per_image((3, atoms)), per_image((3, ghost)), per_image((3, ghost))],
        out_shape=[out(images, 3, atoms), out(images, 3, ghost), out(images, 3, ghost)],
        scratch_shapes=[
            pltpu.VMEM((slots, NL, 8, atoms), f32),
            pltpu.VMEM((NL, ch, atoms), f32),
            pltpu.VMEM((NL, rh, atoms), f32),
            pltpu.VMEM((1, NL, slots, atoms), f32),
            pltpu.VMEM((3 * rh, atoms), bf16),
            pltpu.VMEM((slots, atoms), f32),
            pltpu.VMEM((3, slots, atoms), f32),
        ],
        compiler_params=params,
        name="third",
    )(
        dfh, dft, rlo, rup, neighbours, geo, hid, ds, mom, dpre, dy2, dlen2,
        radial_a1, radial_b1, mix_first, read1,
    )

    glo, gup = neighbours_of((flo, fup), "space")

    me = lax.axis_index("image")
    edge = jnp.stack([(me == 0).astype(jnp.int32), (me == chain - 1).astype(jnp.int32), me])
    rank = chain * space
    force, send = pl.pallas_call(
        partial_kernel,
        in_specs=[SMEM] + [VMEM] * 11,
        out_specs=[VMEM] * 2,
        out_shape=[out(images, 3, atoms), out(rank, 128)],
        name="partial",
    )(edge, own, glo, gup, positions, before, after, start_state, end_state, velocity, en1, en2)
    got = lax.all_to_all(
        send.reshape(rank, 1, 128), ("image", "space"), split_axis=0, concat_axis=0
    ).reshape(rank, 128)
    neb, vnext, pnext, energy = pl.pallas_call(
        functools.partial(final_kernel, images=chain, slabs=space),
        in_specs=[SMEM, VMEM, SMEM] + [VMEM] * 7,
        out_specs=[VMEM] * 4,
        out_shape=[out(images, 3, atoms)] * 3 + [out(images, 8, 128)],
        name="final",
    )(edge, got, climb_index, force, positions, before, after, start_state, end_state, velocity)
    return (neb, vnext, pnext, energy[:, 0, 0])


def solution(mesh):
    in_specs = (
        P("image", None, "space"),
        P("image", None, "space"),
        P(None, "space"),
        P(None, "space"),
        P("image", None, "space"),
        P("image", "space"),
        P(),
        P(),
        P(),
        P(),
        P(),
        P(),
        P(),
        P(),
        P(),
    )
    out_specs = (
        P("image", None, "space"),
        P("image", None, "space"),
        P("image", None, "space"),
        P("image"),
    )
    return jax.shard_map(local, mesh=mesh, in_specs=in_specs, out_specs=out_specs, check_vma=False)
```

```python
import functools
import math

import jax
import jax.numpy as jnp
from jax import lax
from jax.experimental import pallas as pl
from jax.experimental.pallas import tpu as pltpu
from jax.sharding import PartitionSpec as P

f32 = jnp.float32
bf16 = jnp.bfloat16
RT3 = math.sqrt(3.0)
NL = 9
BIG_VMEM = 36 << 20
SMALL_VMEM = 4 << 20


def split(x):
    hi = x.astype(bf16)
    lo = (x - hi.astype(f32)).astype(bf16)
    return hi, lo


def dot(a, b):
    return lax.dot_general(a, b, (((1,), (0,)), ((), ())), preferred_element_type=f32)


def dot_nt(a, b):
    return lax.dot_general(a, b, (((1,), (1,)), ((), ())), preferred_element_type=f32)


def pack_left(w):
    hi, lo = split(w)
    return jnp.concatenate([hi, hi, lo], axis=1)


def pack_right(x):
    hi, lo = split(x)
    return jnp.concatenate([hi, lo, hi], axis=0)


def one_hot(row, extent):
    step = 256
    wide = (step, row.shape[1])
    ids = lax.broadcasted_iota(jnp.int32, wide, 0).astype(f32).astype(bf16)
    zero, one = jnp.zeros(wide, bf16), jnp.ones(wide, bf16)
    parts = []
    for first in range(0, extent, step):
        here = jnp.broadcast_to((row - first).astype(f32), wide).astype(bf16)
        parts.append(jnp.where(ids == here, one, zero))
    return jnp.concatenate(parts, axis=0)


def lane_gather(row, idx):
    slots, atoms = idx.shape
    extent = row.shape[1]
    lane = idx & 127
    tile = idx >> 7
    blocks = [jnp.broadcast_to(row[:, t : t + 128], (8, 128)) for t in range(0, extent, 128)]
    out_rows = []
    for s0 in range(0, slots, 8):
        cells = []
        for a0 in range(0, atoms, 128):
            at = lane[s0 : s0 + 8, a0 : a0 + 128]
            which = tile[s0 : s0 + 8, a0 : a0 + 128]
            got = None
            for t, block in enumerate(blocks):
                v = jnp.take_along_axis(block, at, axis=1, mode="promise_in_bounds")
                got = v if got is None else jnp.where(which == t, v, got)
            cells.append(got)
        out_rows.append(jnp.concatenate(cells, axis=1))
    return jnp.concatenate(out_rows, axis=0)


def pick(block, i, axis):
    n = block.shape[axis]
    got = lax.index_in_dim(block, 0, axis, keepdims=False)
    for m in range(1, n):
        got = jnp.where(i == m, lax.index_in_dim(block, m, axis, keepdims=False), got)
    return got


def column(row_ref):
    n = row_ref.shape[1]
    return jnp.broadcast_to(row_ref[...], (8, n)).T[:, :1]


def silu_parts(z):
    s = 0.5 + 0.5 * jnp.tanh(0.5 * z)
    h = z * s
    return h, s + h * (1.0 - s)


def basis_of(row, nb):
    centres = 0.5 * lax.broadcasted_iota(jnp.int32, (nb, row.shape[1]), 0).astype(f32)
    spread = row - centres
    basis = jnp.exp(-2.0 * spread * spread)
    return basis, -4.0 * spread * basis


def moments_into(edge_tile, yb_ref, m_ref, chans, slots, atoms):
    def tile(t, carry):
        c0 = pl.multiple_of(t * 16, 16)
        for a0 in range(0, atoms, 128):
            acc = [jnp.zeros((16, 128), f32) for _ in range(NL)]
            for k in range(slots):
                e = edge_tile(k, c0, a0)
                for l in range(NL):
                    y = yb_ref[k, l, :, a0 : a0 + 128]
                    acc[l] = acc[l] + e * jnp.concatenate([y, y], axis=0)
            for l in range(NL):
                m_ref[l, pl.ds(c0, 16), a0 : a0 + 128] = acc[l]
        return carry

    lax.fori_loop(0, chans // 16, tile, 0)


def store_yb(yb_ref, ylive, slots, atoms):
    for k in range(slots):
        for l in range(NL):
            yb_ref[k, l] = jnp.broadcast_to(ylive[l][k : k + 1], (8, atoms))


def invariants_of(m_ref):
    m = [m_ref[l] for l in range(NL)]
    one = m[1] * m[1] + m[2] * m[2] + m[3] * m[3]
    two = m[4] * m[4] + m[5] * m[5] + m[6] * m[6] + m[7] * m[7] + m[8] * m[8]
    return jnp.concatenate([m[0], one, two], axis=0)


def moment_grads_into(m_ref, dinv, chans):
    m_ref[0] = dinv[:chans]
    d1 = 2.0 * dinv[chans : 2 * chans]
    d2 = 2.0 * dinv[2 * chans :]
    for l in range(1, NL):
        m_ref[l] = m_ref[l] * (d1 if l < 4 else d2)


def first_kernel(
    pos_ref, plo_ref, pup_ref, idx_ref, cnt_ref, a_ref, b_ref, mix_ref, read_ref,
    head_ref, tail_ref, geo_ref, hid_ref, dsl_ref, mom_ref, dpre_ref, en_ref,
    yb_ref, g_ref,
):
    slots, atoms = idx_ref.shape[1:]
    ghost = plo_ref.shape[2]
    nb, rh = a_ref.shape
    ch = b_ref.shape[1]
    image = pl.program_id(0)
    idx = idx_ref[0]
    pos = pick(pos_ref[...], image, 1)
    plo = pick(plo_ref[...], image, 1)
    pup = pick(pup_ref[...], image, 1)
    ext = jnp.concatenate([plo, pos, pup], axis=1)
    off = [lane_gather(ext[x : x + 1], idx) - pos[x : x + 1] for x in range(3)]
    length = jnp.sqrt(off[0] * off[0] + off[1] * off[1] + off[2] * off[2] + 1.0)
    ux, uy, uz = [o / length for o in off]
    ids = lax.broadcasted_iota(jnp.int32, (slots, atoms), 0)
    cnt = pick(cnt_ref[...][None], image, 1)
    live = jnp.where(ids < cnt, 1.0 / slots, 0.0).astype(f32)
    ylive = [
        live,
        live * ux,
        live * uy,
        live * uz,
        live * (ux * uy),
        live * (uy * uz),
        live * (ux * uz),
        live * (0.5 * (ux * ux - uy * uy)),
        live * ((3.0 * uz * uz - 1.0) / (2.0 * RT3)),
    ]
    for l in range(NL):
        geo_ref[0, l] = ylive[l]
    geo_ref[0, NL] = ux
    geo_ref[0, NL + 1] = uy
    geo_ref[0, NL + 2] = uz
    geo_ref[0, NL + 3] = length
    store_yb(yb_ref, ylive, slots, atoms)
    a_pack = pack_left(a_ref[...].T)
    for k in range(slots):
        basis, slope = basis_of(length[k : k + 1], nb)
        hid, ds = silu_parts(dot(a_pack, pack_right(basis)))
        hid_ref[0, k] = hid
        dsl_ref[0, k] = ds * dot(a_pack, pack_right(slope))

    def hid_tile(k, c0, a0):
        return hid_ref[0, k, pl.ds(c0, 16), a0 : a0 + 128]

    moments_into(hid_tile, yb_ref, g_ref, rh, slots, atoms)
    b_pack = pack_left(b_ref[...].T)
    for l in range(NL):
        mom_ref[0, l] = dot(b_pack, pack_right(g_ref[l]))
    inv = invariants_of(mom_ref.at[0])
    feat, dpre = silu_parts(dot(pack_left(mix_ref[...].T), pack_right(inv)))
    dpre_ref[0] = dpre
    head_ref[0] = feat[:, :ghost]
    tail_ref[0] = feat[:, atoms - ghost :]
    en = column(read_ref) * feat
    total = jnp.sum(en.reshape(ch // 8, 8, atoms), axis=0)
    en_ref[0] = total[:, :128] + total[:, 128:]


def edge_back(k, edge_tile, sink, yb_ref, m_ref, dy_ref, dlen_ref, chans, atoms):
    for a0 in range(0, atoms, 128):
        y = [yb_ref[k, l, :, a0 : a0 + 128] for l in range(NL)]
        y = [jnp.concatenate([v, v], axis=0) for v in y]
        acc = [jnp.zeros((8, 128), f32) for _ in range(NL + 1)]
        for c0 in range(0, chans, 16):
            e = edge_tile(k, c0, a0)
            de = None
            for l in range(NL):
                dm = m_ref[l, c0 : c0 + 16, a0 : a0 + 128]
                term = dm * y[l]
                de = term if de is None else de + term
                p = e * dm
                acc[l] = acc[l] + (p[:8] + p[8:])
            p = sink(k, c0, a0, de)
            acc[NL] = acc[NL] + (p[:8] + p[8:])
        for l in range(NL):
            dy_ref[0, l, k : k + 1, a0 : a0 + 128] = jnp.sum(acc[l], axis=0, keepdims=True)
        dlen_ref[0, k : k + 1, a0 : a0 + 128] = jnp.sum(acc[NL], axis=0, keepdims=True)


def second_kernel(
    head_ref, tail_ref, hlo_ref, hup_ref, idx_ref, geo_ref, a_ref, b_ref, mix_ref, read_ref,
    dfh_ref, dft_ref, dlo_ref, dup_ref, dy_ref, dlen_ref, en_ref,
    yb_ref, hf_ref, oh_ref, q_ref, rad_ref, radl_ref, m_ref, dq_ref,
):
    slots, atoms = idx_ref.shape[1:]
    ghost = hlo_ref.shape[2]
    nb, rh = a_ref.shape
    ch = b_ref.shape[1]
    extent = atoms + 2 * ghost
    parts = (hlo_ref, head_ref, tail_ref, hup_ref)
    for n, ref in enumerate(parts):
        hi, lo = split(ref[0])
        hf_ref[:ch, n * ghost : (n + 1) * ghost] = hi
        hf_ref[ch:, n * ghost : (n + 1) * ghost] = lo
    store_yb(yb_ref, [geo_ref[0, l] for l in range(NL)], slots, atoms)
    a_pack = pack_left(a_ref[...].T)
    b_pack = pack_left(b_ref[...].T)
    for k in range(slots):
        oh = one_hot(idx_ref[0, k : k + 1, :], extent)
        oh_ref[:, k * atoms : (k + 1) * atoms] = oh
        got = dot(hf_ref[...], oh)
        q_ref[k] = got[:ch] + got[ch:]
        basis, slope = basis_of(geo_ref[0, NL + 3, k : k + 1, :], nb)
        hid, ds = silu_parts(dot(a_pack, pack_right(basis)))
        rad_ref[k] = dot(b_pack, pack_right(hid))
        radl_ref[k] = dot(b_pack, pack_right(ds * dot(a_pack, pack_right(slope))))

    def edge_tile(k, c0, a0):
        cs = pl.ds(c0, 16)
        return rad_ref[k, cs, a0 : a0 + 128] * q_ref[k, cs, a0 : a0 + 128]

    moments_into(edge_tile, yb_ref, m_ref, ch, slots, atoms)
    inv = invariants_of(m_ref)
    mix = mix_ref[...]
    feat, dpre = silu_parts(dot(pack_left(mix.T), pack_right(inv)))
    en = column(read_ref) * feat
    total = jnp.sum(en.reshape(ch // 8, 8, atoms), axis=0)
    en_ref[0] = total[:, :128] + total[:, 128:]
    dpre = column(read_ref) * dpre
    dinv = dot(pack_left(mix), pack_right(dpre))
    moment_grads_into(m_ref, dinv, ch)

    def sink(k, c0, a0, de):
        cs = slice(c0, c0 + 16)
        ls = slice(a0, a0 + 128)
        hi, lo = split(de * rad_ref[k, cs, ls])
        ks = slice(k * atoms + a0, k * atoms + a0 + 128)
        dq_ref[cs, ks] = hi
        dq_ref[ch + c0 : ch + c0 + 16, ks] = lo
        return de * q_ref[k, cs, ls] * radl_ref[k, cs, ls]

    for k in range(slots):
        edge_back(k, edge_tile, sink, yb_ref, m_ref, dy_ref, dlen_ref, ch, atoms)
    back = dot_nt(dq_ref[...], oh_ref[...])
    back = back[:ch] + back[ch:]
    dlo_ref[0] = back[:, :ghost]
    dfh_ref[0] = back[:, ghost : 2 * ghost]
    dft_ref[0] = back[:, 2 * ghost : 3 * ghost]
    dup_ref[0] = back[:, 3 * ghost :]


def third_kernel(
    dfh_ref, dft_ref, rlo_ref, rup_ref, idx_ref, geo_ref, hid_ref, dsl_ref, mom_ref, dpre_ref,
    dy2_ref, dlen2_ref, b_ref, mix_ref, read_ref,
    own_ref, flo_ref, fup_ref,
    yb_ref, m_ref, dg_ref, dy_ref, dlen_ref, doff_ref,
):
    slots, atoms = idx_ref.shape[1:]
    ghost = rlo_ref.shape[2]
    rh, ch = b_ref.shape
    extent = atoms + 2 * ghost
    store_yb(yb_ref, [geo_ref[0, l] for l in range(NL)], slots, atoms)
    cot = jnp.concatenate([dfh_ref[0] + rlo_ref[0], dft_ref[0] + rup_ref[0]], axis=1)
    dpre = (cot + column(read_ref)) * dpre_ref[0]
    dinv = dot(pack_left(mix_ref[...]), pack_right(dpre))
    for l in range(NL):
        m_ref[l] = mom_ref[0, l]
    moment_grads_into(m_ref, dinv, ch)
    bt_pack = pack_left(b_ref[...])
    for l in range(NL):
        dg_ref[l] = dot(bt_pack, pack_right(m_ref[l]))

    def edge_tile(k, c0, a0):
        return hid_ref[0, k, pl.ds(c0, 16), a0 : a0 + 128]

    def sink(k, c0, a0, de):
        return de * dsl_ref[0, k, c0 : c0 + 16, a0 : a0 + 128]

    for k in range(slots):
        edge_back(k, edge_tile, sink, yb_ref, dg_ref, dy_ref, dlen_ref, rh, atoms)
    live = geo_ref[0, 0]
    dy = [live * (dy_ref[0, l] + dy2_ref[0, l]) for l in range(NL)]
    ux, uy, uz, length = [geo_ref[0, NL + n] for n in range(4)]
    dux = dy[1] + uy * dy[4] + uz * dy[6] + ux * dy[7]
    duy = dy[2] + ux * dy[4] + uz * dy[5] - uy * dy[7]
    duz = dy[3] + uy * dy[5] + ux * dy[6] + RT3 * uz * dy[8]
    radial = dlen_ref[0] + dlen2_ref[0] - (dux * ux + duy * uy + duz * uz) / length
    doff = [du / length + radial * u for du, u in ((dux, ux), (duy, uy), (duz, uz))]
    centre = jnp.concatenate([jnp.sum(d, axis=0, keepdims=True) for d in doff], axis=0)
    for x in range(3):
        doff_ref[x] = doff[x]
    back = jnp.zeros((16, extent), f32)
    pad = jnp.zeros((5, atoms), f32)
    for k in range(slots):
        rows = jnp.concatenate([doff_ref[x, k : k + 1, :] for x in range(3)] + [pad], axis=0)
        hi = rows.astype(bf16).astype(f32)
        both = jnp.concatenate([hi, rows - hi], axis=0).astype(bf16)
        back = back + dot_nt(both, one_hot(idx_ref[0, k : k + 1, :], extent))
    force = back[8:11] + back[:3]
    for n in range(own_ref.shape[1]):

        @pl.when(pl.program_id(0) == n)
        def _():
            own_ref[:, n, :] = centre - force[:, ghost : ghost + atoms]
            flo_ref[:, n, :] = -force[:, :ghost]
            fup_ref[:, n, :] = -force[:, ghost + atoms :]


def lane_row(values):
    lane = lax.broadcasted_iota(jnp.int32, (1, 128), 1)
    row = jnp.zeros((1, 128), f32)
    for n, v in enumerate(values):
        row = jnp.where(lane == n, v, row)
    return row


def total_of(x):
    return jnp.sum(jnp.sum(x, axis=1, keepdims=True), axis=0, keepdims=True)


def chain_of(pos_ref, before_ref, after_ref, start_ref, end_ref, chain):
    count = pos_ref.shape[1]
    me = lax.axis_index("image")
    before = jnp.where(me == 0, start_ref[...], before_ref[...])
    after = jnp.where(me == chain - 1, end_ref[...], after_ref[...])
    prev = [before] + [pos_ref[:, i, :] for i in range(count - 1)]
    nxt = [pos_ref[:, i, :] for i in range(1, count)] + [after]
    return prev, nxt


def partial_kernel(
    own_ref, rlo_ref, rup_ref, pos_ref, before_ref, after_ref, start_ref, end_ref,
    vel_ref, en1_ref, en2_ref, force_ref, send_ref, *, chain,
):
    count = pos_ref.shape[1]
    prev, nxt = chain_of(pos_ref, before_ref, after_ref, start_ref, end_ref, chain)
    values = []
    vel = jnp.zeros((1, 1), f32)
    for i in range(count):
        pos = pos_ref[:, i, :]
        force = own_ref[:, i, :] + jnp.concatenate([rlo_ref[:, i, :], rup_ref[:, i, :]], axis=1)
        force_ref[:, i, :] = force
        spread = nxt[i] - prev[i]
        ahead = nxt[i] - pos
        behind = pos - prev[i]
        values += [
            total_of(ahead * ahead),
            total_of(behind * behind),
            total_of(spread * spread),
            total_of(force * force),
            total_of(force * spread),
            total_of(en1_ref[i]) + total_of(en2_ref[i]),
        ]
        v = vel_ref[:, i, :]
        vel = vel + total_of(v * v)
    send_ref[...] = jnp.broadcast_to(lane_row(values + [vel]), send_ref.shape)


def final_kernel(
    got_ref, climb_ref, force_ref, pos_ref, before_ref, after_ref, start_ref, end_ref,
    vel_ref, neb_ref, vnext_ref, pnext_ref, en_ref,
    *, chain, slabs,
):
    count = pos_ref.shape[1]
    atoms = pos_ref.shape[2]
    me = lax.axis_index("image")
    prev, nxt = chain_of(pos_ref, before_ref, after_ref, start_ref, end_ref, chain)
    rows = [
        jnp.sum(got_ref[g * slabs : (g + 1) * slabs, :], axis=0, keepdims=True)
        for g in range(chain)
    ]
    table = jnp.concatenate(rows, axis=0)
    vel_sq = jnp.sum(table[:, 6 * count : 6 * count + 1], axis=0, keepdims=True)
    group = lax.broadcasted_iota(jnp.int32, (chain, 1), 0)
    force_sq = jnp.zeros((1, 1), f32)
    mine = []
    for i in range(count):
        ahead, behind, spread_sq, ff, fd, energy = [
            table[:, 6 * i + n : 6 * i + n + 1] for n in range(6)
        ]
        norm = 1.0 / jnp.sqrt(spread_sq + 1e-06)
        along = fd * norm
        climbing = jnp.where(group * count + i == climb_ref[0], 1.0, 0.0).astype(f32)
        spring = 5.0 * (jnp.sqrt(ahead) - jnp.sqrt(behind))
        coef = -(1.0 + climbing) * along + (1.0 - climbing) * spring
        scale = coef * norm
        part = ff + 2.0 * coef * along + scale * scale * spread_sq
        force_sq = force_sq + jnp.sum(part, axis=0, keepdims=True)
        here = group == me
        mine.append(jnp.sum(jnp.where(here, scale, 0.0), axis=0, keepdims=True))
        en_ref[i] = jnp.sum(jnp.where(here, energy, 0.0)) * (1.0 / (atoms * slabs))
    gain = 0.1 * jnp.sqrt(vel_sq / (force_sq + 1e-06))
    for i in range(count):
        neb = force_ref[:, i, :] + mine[i] * (nxt[i] - prev[i])
        neb_ref[:, i, :] = neb
        vnext = 0.9 * vel_ref[:, i, :] + gain * neb + 0.1 * neb
        vnext_ref[:, i, :] = vnext
        pnext_ref[:, i, :] = pos_ref[:, i, :] + 0.1 * vnext


def per_image(shape):
    rank = len(shape)
    return pl.BlockSpec((1,) + shape, lambda i: (i,) + (0,) * rank)


def whole(shape):
    rank = len(shape)
    return pl.BlockSpec(shape, lambda i: (0,) * rank)


def out(*shape):
    return jax.ShapeDtypeStruct(shape, f32)


VMEM = pl.BlockSpec(memory_space=pltpu.VMEM)
SMEM = pl.BlockSpec(memory_space=pltpu.SMEM)


def neighbours_of(cells, axis):
    count = lax.axis_size(axis)
    up = [(i, (i + 1) % count) for i in range(count)]
    down = [((i + 1) % count, i) for i in range(count)]
    to_below, to_above = cells
    return lax.ppermute(to_above, axis, up), lax.ppermute(to_below, axis, down)


def local(
    positions,
    velocity,
    start_state,
    end_state,
    neighbours,
    counts,
    climb_index,
    radial_a1,
    radial_b1,
    mix_first,
    read_first,
    radial_a2,
    radial_b2,
    mix_second,
    read_second,
):
    images, _, atoms = positions.shape
    slots = neighbours.shape[1]
    ghost = atoms // 2
    nb, rh = radial_a1.shape
    ch = radial_b1.shape[1]
    extent = atoms + 2 * ghost
    space = lax.axis_size("space")
    chain = lax.axis_size("image")
    big = pltpu.CompilerParams(dimension_semantics=("arbitrary",), vmem_limit_bytes=BIG_VMEM)
    small = pltpu.CompilerParams(vmem_limit_bytes=SMALL_VMEM)
    pos = positions.transpose(1, 0, 2)
    vel = velocity.transpose(1, 0, 2)

    plo, pup = neighbours_of((pos[:, :, :ghost], pos[:, :, ghost:]), "space")
    before = lax.ppermute(pos[:, images - 1], "image", [(i, i + 1) for i in range(chain - 1)])
    after = lax.ppermute(pos[:, 0], "image", [(i + 1, i) for i in range(chain - 1)])
    read1 = read_first.reshape(1, ch)
    read2 = read_second.reshape(1, ch)
    geo_n = NL + 4

    head, tail, geo, hid, dsl, mom, dpre, en1 = pl.pallas_call(
        first_kernel,
        grid=(images,),
        in_specs=[
            whole((3, images, atoms)),
            whole((3, images, ghost)),
            whole((3, images, ghost)),
            per_image((slots, atoms)),
            whole((images, atoms)),
            whole((nb, rh)),
            whole((rh, ch)),
            whole((3 * ch, ch)),
            whole((1, ch)),
        ],
        out_specs=[
            per_image((ch, ghost)),
            per_image((ch, ghost)),
            per_image((geo_n, slots, atoms)),
            per_image((slots, rh, atoms)),
            per_image((slots, rh, atoms)),
            per_image((NL, ch, atoms)),
            per_image((ch, atoms)),
            per_image((8, 128)),
        ],
        out_shape=[
            out(images, ch, ghost),
            out(images, ch, ghost),
            out(images, geo_n, slots, atoms),
            out(images, slots, rh, atoms),
            out(images, slots, rh, atoms),
            out(images, NL, ch, atoms),
            out(images, ch, atoms),
            out(images, 8, 128),
        ],
        scratch_shapes=[
            pltpu.VMEM((slots, NL, 8, atoms), f32),
            pltpu.VMEM((NL, rh, atoms), f32),
        ],
        compiler_params=big,
        name="first",
    )(pos, plo, pup, neighbours, counts, radial_a1, radial_b1, mix_first, read1)

    hlo, hup = neighbours_of((head, tail), "space")

    dfh, dft, dlo, dup, dy2, dlen2, en2 = pl.pallas_call(
        second_kernel,
        grid=(images,),
        in_specs=[per_image((ch, ghost))] * 4
        + [
            per_image((slots, atoms)),
            per_image((geo_n, slots, atoms)),
            whole((nb, rh)),
            whole((rh, ch)),
            whole((3 * ch, ch)),
            whole((1, ch)),
        ],
        out_specs=[per_image((ch, ghost))] * 4
        + [
            per_image((NL, slots, atoms)),
            per_image((slots, atoms)),
            per_image((8, 128)),
        ],
        out_shape=[out(images, ch, ghost)] * 4
        + [
            out(images, NL, slots, atoms),
            out(images, slots, atoms),
            out(images, 8, 128),
        ],
        scratch_shapes=[
            pltpu.VMEM((slots, NL, 8, atoms), f32),
            pltpu.VMEM((2 * ch, extent), bf16),
            pltpu.VMEM((extent, slots * atoms), bf16),
            pltpu.VMEM((slots, ch, atoms), f32),
            pltpu.VMEM((slots, ch, atoms), f32),
            pltpu.VMEM((slots, ch, atoms), f32),
            pltpu.VMEM((NL, ch, atoms), f32),
            pltpu.VMEM((2 * ch, slots * atoms), bf16),
        ],
        compiler_params=big,
        name="second",
    )(head, tail, hlo, hup, neighbours, geo, radial_a2, radial_b2, mix_second, read2)

    rlo, rup = neighbours_of((dlo, dup), "space")

    own, flo, fup = pl.pallas_call(
        third_kernel,
        grid=(images,),
        in_specs=[per_image((ch, ghost))] * 4
        + [
            per_image((slots, atoms)),
            per_image((geo_n, slots, atoms)),
            per_image((slots, rh, atoms)),
            per_image((slots, rh, atoms)),
            per_image((NL, ch, atoms)),
            per_image((ch, atoms)),
            per_image((NL, slots, atoms)),
            per_image((slots, atoms)),
            whole((rh, ch)),
            whole((3 * ch, ch)),
            whole((1, ch)),
        ],
        out_specs=[
            whole((3, images, atoms)),
            whole((3, images, ghost)),
            whole((3, images, ghost)),
        ],
        out_shape=[out(3, images, atoms), out(3, images, ghost), out(3, images, ghost)],
        scratch_shapes=[
            pltpu.VMEM((slots, NL, 8, atoms), f32),
            pltpu.VMEM((NL, ch, atoms), f32),
            pltpu.VMEM((NL, rh, atoms), f32),
            pltpu.VMEM((1, NL, slots, atoms), f32),
            pltpu.VMEM((1, slots, atoms), f32),
            pltpu.VMEM((3, slots, atoms), f32),
        ],
        compiler_params=big,
        name="third",
    )(
        dfh, dft, rlo, rup, neighbours, geo, hid, dsl, mom, dpre, dy2, dlen2,
        radial_b1, mix_first, read1,
    )

    glo, gup = neighbours_of((flo, fup), "space")

    rank = chain * space
    force, send = pl.pallas_call(
        functools.partial(partial_kernel, chain=chain),
        in_specs=[VMEM] * 11,
        out_specs=[VMEM] * 2,
        out_shape=[out(3, images, atoms), out(rank, 128)],
        compiler_params=small,
        name="partial",
    )(own, glo, gup, pos, before, after, start_state, end_state, vel, en1, en2)
    got = lax.all_to_all(
        send.reshape(rank, 1, 128), ("image", "space"), split_axis=0, concat_axis=0
    ).reshape(rank, 128)
    neb, vnext, pnext, energy = pl.pallas_call(
        functools.partial(final_kernel, chain=chain, slabs=space),
        in_specs=[VMEM, SMEM] + [VMEM] * 7,
        out_specs=[VMEM] * 3 + [SMEM],
        out_shape=[out(3, images, atoms)] * 3 + [out(images)],
        compiler_params=small,
        name="final",
    )(got, climb_index, force, pos, before, after, start_state, end_state, vel)
    return (
        neb.transpose(1, 0, 2),
        vnext.transpose(1, 0, 2),
        pnext.transpose(1, 0, 2),
        energy,
    )


def solution(mesh):
    in_specs = (
        P("image", None, "space"),
        P("image", None, "space"),
        P(None, "space"),
        P(None, "space"),
        P("image", None, "space"),
        P("image", "space"),
        P(),
        P(),
        P(),
        P(),
        P(),
        P(),
        P(),
        P(),
        P(),
    )
    out_specs = (
        P("image", None, "space"),
        P("image", None, "space"),
        P("image", None, "space"),
        P("image"),
    )
    return jax.shard_map(local, mesh=mesh, in_specs=in_specs, out_specs=out_specs, check_vma=False)
```

```python
import functools
import math

import jax
import jax.numpy as jnp
from jax import lax
from jax.experimental import pallas as pl
from jax.experimental.pallas import tpu as pltpu
from jax.sharding import PartitionSpec as P

f32 = jnp.float32
bf16 = jnp.bfloat16
RT3 = math.sqrt(3.0)
NL = 9
BIG_VMEM = 24 << 20
SMALL_VMEM = 4 << 20


def split(x):
    hi = x.astype(bf16)
    lo = (x - hi.astype(f32)).astype(bf16)
    return hi, lo


def dot(a, b):
    return lax.dot_general(a, b, (((1,), (0,)), ((), ())), preferred_element_type=f32)


def dot_nt(a, b):
    return lax.dot_general(a, b, (((1,), (1,)), ((), ())), preferred_element_type=f32)


def pack_left(w):
    hi, lo = split(w)
    return jnp.concatenate([hi, hi, lo], axis=1)


def pack_right(x):
    hi, lo = split(x)
    return jnp.concatenate([hi, lo, hi], axis=0)


def one_hot(row, extent):
    step = 256
    wide = (step, row.shape[1])
    ids = lax.broadcasted_iota(jnp.int32, wide, 0).astype(f32).astype(bf16)
    zero, one = jnp.zeros(wide, bf16), jnp.ones(wide, bf16)
    parts = []
    for first in range(0, extent, step):
        here = jnp.broadcast_to((row - first).astype(f32), wide).astype(bf16)
        parts.append(jnp.where(ids == here, one, zero))
    return jnp.concatenate(parts, axis=0)


def lane_gather(row, idx):
    slots, atoms = idx.shape
    extent = row.shape[1]
    lane = idx & 127
    tile = idx >> 7
    blocks = [jnp.broadcast_to(row[:, t : t + 128], (8, 128)) for t in range(0, extent, 128)]
    out_rows = []
    for s0 in range(0, slots, 8):
        cells = []
        for a0 in range(0, atoms, 128):
            at = lane[s0 : s0 + 8, a0 : a0 + 128]
            which = tile[s0 : s0 + 8, a0 : a0 + 128]
            got = None
            for t, block in enumerate(blocks):
                v = jnp.take_along_axis(block, at, axis=1, mode="promise_in_bounds")
                got = v if got is None else jnp.where(which == t, v, got)
            cells.append(got)
        out_rows.append(jnp.concatenate(cells, axis=1))
    return jnp.concatenate(out_rows, axis=0)


def pick(block, i, axis):
    n = block.shape[axis]
    got = lax.index_in_dim(block, 0, axis, keepdims=False)
    for m in range(1, n):
        got = jnp.where(i == m, lax.index_in_dim(block, m, axis, keepdims=False), got)
    return got


def silu_parts(z):
    s = 0.5 + 0.5 * jnp.tanh(0.5 * z)
    h = z * s
    return h, s + h * (1.0 - s)


def basis_of(row):
    nb = 8
    centres = 0.5 * lax.broadcasted_iota(jnp.int32, (nb, row.shape[1]), 0).astype(f32)
    spread = row - centres
    basis = jnp.exp(-2.0 * spread * spread)
    return basis, -4.0 * spread * basis


def moments_into(edge_tile, yb_ref, m_ref, chans, slots, atoms):
    def tile(t, carry):
        c0 = pl.multiple_of(t * 16, 16)
        for a0 in range(0, atoms, 128):
            acc = [jnp.zeros((16, 128), f32) for _ in range(NL)]
            for k in range(slots):
                e = edge_tile(k, c0, a0)
                acc[0] = acc[0] + e
                for l in range(1, NL):
                    y = yb_ref[k, l - 1, :, a0 : a0 + 128]
                    acc[l] = acc[l] + e * jnp.concatenate([y, y], axis=0)
            for l in range(NL):
                m_ref[l, pl.ds(c0, 16), a0 : a0 + 128] = acc[l]
        return carry

    lax.fori_loop(0, chans // 16, tile, 0)


def store_yb(yb_ref, angular, slots, atoms):
    for k in range(slots):
        for l in range(NL - 1):
            yb_ref[k, l] = jnp.broadcast_to(angular[l][k : k + 1], (8, atoms))


def invariants_of(m_ref):
    m = [m_ref[l] for l in range(NL)]
    one = m[1] * m[1] + m[2] * m[2] + m[3] * m[3]
    two = m[4] * m[4] + m[5] * m[5] + m[6] * m[6] + m[7] * m[7] + m[8] * m[8]
    return jnp.concatenate([m[0], one, two], axis=0)


def moment_grads_into(m_ref, dinv, chans):
    m_ref[0] = dinv[:chans]
    d1 = 2.0 * dinv[chans : 2 * chans]
    d2 = 2.0 * dinv[2 * chans :]
    for l in range(1, NL):
        m_ref[l] = m_ref[l] * (d1 if l < 4 else d2)


def prep_kernel(*refs):
    n = 10
    hbm, outs, bufs, sems = refs[:n], refs[n : n + 13], refs[n + 13 : -1], refs[-1]
    (
        idx_out, cnt_out, a1_out, b1_out, m1t_out, m1_out, b1t_out, r1_out,
        a2_out, b2_out, m2t_out, m2_out, r2_out,
    ) = outs
    a1, b1, m1, r1, a2, b2, m2, r2 = bufs
    targets = (idx_out, cnt_out) + bufs
    copies = [pltpu.make_async_copy(h, t, sems.at[q]) for q, (h, t) in enumerate(zip(hbm, targets))]
    for c in copies:
        c.start()
    for c in copies:
        c.wait()
    a1_out[...] = pack_left(a1[...].T)
    b1_out[...] = pack_left(b1[...].T)
    m1t_out[...] = pack_left(m1[...].T)
    m1_out[...] = pack_left(m1[...])
    b1t_out[...] = pack_left(b1[...])
    r1_out[...] = jnp.broadcast_to(r1[...], r1_out.shape[::-1]).T
    a2_out[...] = pack_left(a2[...].T)
    b2_out[...] = pack_left(b2[...].T)
    m2t_out[...] = pack_left(m2[...].T)
    m2_out[...] = pack_left(m2[...])
    r2_out[...] = jnp.broadcast_to(r2[...], r2_out.shape[::-1]).T


def energy_rows(read_ref, feat):
    ch, atoms = feat.shape
    read = read_ref[...]
    en = jnp.concatenate([read] * (atoms // 128), axis=1) * feat
    total = jnp.sum(en.reshape(ch // 8, 8, atoms), axis=0)
    return sum(total[:, a0 : a0 + 128] for a0 in range(0, atoms, 128))


def wide(read_ref, atoms):
    return jnp.concatenate([read_ref[...]] * (atoms // 128), axis=1)


def each_image(body):
    def kernel(*refs, images):
        def step(i, carry):
            body(i, *refs)
            return carry

        lax.fori_loop(0, images, step, 0)

    return kernel


@each_image
def first_kernel(
    i, pos_ref, plo_ref, pup_ref, before_ref, after_ref, idx_ref, cnt_ref, a_ref, b_ref, mixt_ref,
    read_ref, head_ref, tail_ref, geo_ref, hid_ref, dsl_ref, mom_ref, dpre_ref, en_ref,
    yb_ref, g_ref,
):
    slots, atoms = idx_ref.shape[1:]
    ghost = plo_ref.shape[2]
    idx = idx_ref[i]
    pos = pick(pos_ref[...], i, 1)
    plo = pick(plo_ref[...], i, 1)
    pup = pick(pup_ref[...], i, 1)
    ext = jnp.concatenate([plo, pos, pup], axis=1)
    off = [lane_gather(ext[x : x + 1], idx) - pos[x : x + 1] for x in range(3)]
    length = jnp.sqrt(off[0] * off[0] + off[1] * off[1] + off[2] * off[2] + 1.0)
    ux, uy, uz = [o / length for o in off]
    ids = lax.broadcasted_iota(jnp.int32, (slots, atoms), 0)
    cnt = pick(cnt_ref[...][None], i, 1)
    live = jnp.where(ids < cnt, 1.0 / slots, 0.0).astype(f32)
    angular = [
        ux,
        uy,
        uz,
        ux * uy,
        uy * uz,
        ux * uz,
        0.5 * (ux * ux - uy * uy),
        (3.0 * uz * uz - 1.0) / (2.0 * RT3),
    ]
    for l in range(NL - 1):
        geo_ref[i, l] = angular[l]
    geo_ref[i, NL - 1] = length
    geo_ref[i, NL] = live
    store_yb(yb_ref, angular, slots, atoms)
    for k in range(slots):
        basis, slope = basis_of(length[k : k + 1])
        hid, ds = silu_parts(dot(a_ref[...], pack_right(basis)))
        row = live[k : k + 1]
        hid_ref[i, k] = hid * row
        dsl_ref[i, k] = ds * row * dot(a_ref[...], pack_right(slope))

    def hid_tile(k, c0, a0):
        return hid_ref[i, k, pl.ds(c0, 16), a0 : a0 + 128]

    moments_into(hid_tile, yb_ref, g_ref, hid_ref.shape[2], slots, atoms)
    for l in range(NL):
        mom_ref[i, l] = dot(b_ref[...], pack_right(g_ref[l]))
    inv = invariants_of(mom_ref.at[i])
    feat, dpre = silu_parts(dot(mixt_ref[...], pack_right(inv)))
    dpre_ref[i] = dpre
    head_ref[i] = feat[:, :ghost]
    tail_ref[i] = feat[:, atoms - ghost :]
    en_ref[i] = energy_rows(read_ref, feat)


def edge_back(k, edge_tile, sink, yb_ref, m_ref, dy_ref, dlen_ref, chans, atoms):
    for a0 in range(0, atoms, 128):
        y = [yb_ref[k, l, :, a0 : a0 + 128] for l in range(NL - 1)]
        y = [jnp.concatenate([v, v], axis=0) for v in y]
        acc = [jnp.zeros((8, 128), f32) for _ in range(NL)]
        for c0 in range(0, chans, 16):
            e = edge_tile(k, c0, a0)
            de = m_ref[0, c0 : c0 + 16, a0 : a0 + 128]
            for l in range(1, NL):
                dm = m_ref[l, c0 : c0 + 16, a0 : a0 + 128]
                de = de + dm * y[l - 1]
                p = e * dm
                acc[l] = acc[l] + (p[:8] + p[8:])
            p = sink(k, c0, a0, de)
            acc[0] = acc[0] + (p[:8] + p[8:])
        for l in range(1, NL):
            dy_ref[l - 1, k : k + 1, a0 : a0 + 128] = jnp.sum(acc[l], axis=0, keepdims=True)
        dlen_ref[k : k + 1, a0 : a0 + 128] = jnp.sum(acc[0], axis=0, keepdims=True)


@each_image
def second_kernel(
    i, head_ref, tail_ref, hlo_ref, hup_ref, idx_ref, geo_ref, a_ref, b_ref, mixt_ref, mix_ref,
    read_ref, dfh_ref, dft_ref, dlo_ref, dup_ref, dy_ref, dlen_ref, en_ref,
    yb_ref, hf_ref, oh_ref, q_ref, rad_ref, radl_ref, m_ref, dq_ref,
):
    slots, atoms = idx_ref.shape[1:]
    ghost = hlo_ref.shape[2]
    ch = hlo_ref.shape[1]
    extent = atoms + 2 * ghost
    for n, ref in enumerate((hlo_ref, head_ref, tail_ref, hup_ref)):
        hi, lo = split(ref[i])
        hf_ref[:ch, n * ghost : (n + 1) * ghost] = hi
        hf_ref[ch:, n * ghost : (n + 1) * ghost] = lo
    store_yb(yb_ref, [geo_ref[i, l] for l in range(NL - 1)], slots, atoms)
    for k in range(slots):
        oh = one_hot(idx_ref[i, k : k + 1, :], extent)
        oh_ref[:, k * atoms : (k + 1) * atoms] = oh
        got = dot(hf_ref[...], oh)
        q_ref[k] = got[:ch] + got[ch:]
        basis, slope = basis_of(geo_ref[i, NL - 1, k : k + 1, :])
        row = geo_ref[i, NL, k : k + 1, :]
        hid, ds = silu_parts(dot(a_ref[...], pack_right(basis)))
        rad_ref[k] = dot(b_ref[...], pack_right(hid * row))
        dsl = ds * row * dot(a_ref[...], pack_right(slope))
        radl_ref[k] = dot(b_ref[...], pack_right(dsl))

    def edge_tile(k, c0, a0):
        cs = pl.ds(c0, 16)
        return rad_ref[k, cs, a0 : a0 + 128] * q_ref[k, cs, a0 : a0 + 128]

    moments_into(edge_tile, yb_ref, m_ref, ch, slots, atoms)
    inv = invariants_of(m_ref)
    feat, dpre = silu_parts(dot(mixt_ref[...], pack_right(inv)))
    en_ref[i] = energy_rows(read_ref, feat)
    dinv = dot(mix_ref[...], pack_right(wide(read_ref, atoms) * dpre))
    moment_grads_into(m_ref, dinv, ch)

    def sink(k, c0, a0, de):
        cs = slice(c0, c0 + 16)
        ls = slice(a0, a0 + 128)
        hi, lo = split(de * rad_ref[k, cs, ls])
        ks = slice(k * atoms + a0, k * atoms + a0 + 128)
        dq_ref[cs, ks] = hi
        dq_ref[ch + c0 : ch + c0 + 16, ks] = lo
        return de * q_ref[k, cs, ls] * radl_ref[k, cs, ls]

    for k in range(slots):
        edge_back(k, edge_tile, sink, yb_ref, m_ref, dy_ref.at[i], dlen_ref.at[i], ch, atoms)
    back = dot_nt(dq_ref[...], oh_ref[...])
    back = back[:ch] + back[ch:]
    dlo_ref[i] = back[:, :ghost]
    dfh_ref[i] = back[:, ghost : 2 * ghost]
    dft_ref[i] = back[:, 2 * ghost : 3 * ghost]
    dup_ref[i] = back[:, 3 * ghost :]


@each_image
def third_kernel(
    i, dfh_ref, dft_ref, rlo_ref, rup_ref, idx_ref, geo_ref, hid_ref, dsl_ref, mom_ref, dpre_ref,
    dy2_ref, dlen2_ref, bt_ref, mix_ref, read_ref,
    own_ref, flo_ref, fup_ref,
    yb_ref, m_ref, dg_ref, dy_ref, dlen_ref, doff_ref,
):
    slots, atoms = idx_ref.shape[1:]
    ch, ghost = rlo_ref.shape[1:]
    rh = hid_ref.shape[2]
    extent = atoms + 2 * ghost
    store_yb(yb_ref, [geo_ref[i, l] for l in range(NL - 1)], slots, atoms)
    cot = jnp.concatenate([dfh_ref[i] + rlo_ref[i], dft_ref[i] + rup_ref[i]], axis=1)
    dpre = (cot + wide(read_ref, atoms)) * dpre_ref[i]
    dinv = dot(mix_ref[...], pack_right(dpre))
    for l in range(NL):
        m_ref[l] = mom_ref[i, l]
    moment_grads_into(m_ref, dinv, ch)
    for l in range(NL):
        dg_ref[l] = dot(bt_ref[...], pack_right(m_ref[l]))

    def edge_tile(k, c0, a0):
        return hid_ref[i, k, pl.ds(c0, 16), a0 : a0 + 128]

    def sink(k, c0, a0, de):
        return de * dsl_ref[i, k, c0 : c0 + 16, a0 : a0 + 128]

    for k in range(slots):
        edge_back(k, edge_tile, sink, yb_ref, dg_ref, dy_ref, dlen_ref, rh, atoms)
    dy = [None] + [dy_ref[l] + dy2_ref[i, l] for l in range(NL - 1)]
    ux, uy, uz = [geo_ref[i, n] for n in range(3)]
    length = geo_ref[i, NL - 1]
    dux = dy[1] + uy * dy[4] + uz * dy[6] + ux * dy[7]
    duy = dy[2] + ux * dy[4] + uz * dy[5] - uy * dy[7]
    duz = dy[3] + uy * dy[5] + ux * dy[6] + RT3 * uz * dy[8]
    radial = dlen_ref[...] + dlen2_ref[i] - (dux * ux + duy * uy + duz * uz) / length
    doff = [du / length + radial * u for du, u in ((dux, ux), (duy, uy), (duz, uz))]
    centre = jnp.concatenate([jnp.sum(d, axis=0, keepdims=True) for d in doff], axis=0)
    for x in range(3):
        doff_ref[x] = doff[x]
    back = jnp.zeros((16, extent), f32)
    pad = jnp.zeros((5, atoms), f32)
    for k in range(slots):
        rows = jnp.concatenate([doff_ref[x, k : k + 1, :] for x in range(3)] + [pad], axis=0)
        hi = rows.astype(bf16).astype(f32)
        both = jnp.concatenate([hi, rows - hi], axis=0).astype(bf16)
        back = back + dot_nt(both, one_hot(idx_ref[i, k : k + 1, :], extent))
    force = back[8:11] + back[:3]
    for n in range(own_ref.shape[1]):

        @pl.when(i == n)
        def _():
            own_ref[:, n, :] = centre - force[:, ghost : ghost + atoms]
            flo_ref[:, n, :] = -force[:, :ghost]
            fup_ref[:, n, :] = -force[:, ghost + atoms :]


def lane_row(values):
    lane = lax.broadcasted_iota(jnp.int32, (1, 128), 1)
    row = jnp.zeros((1, 128), f32)
    for n, v in enumerate(values):
        row = jnp.where(lane == n, v, row)
    return row


def total_of(x):
    return jnp.sum(jnp.sum(x, axis=1, keepdims=True), axis=0, keepdims=True)


def chain_of(pos_ref, before_ref, after_ref, start_ref, end_ref, chain):
    count = pos_ref.shape[1]
    me = lax.axis_index("image")
    before = jnp.where(me == 0, start_ref[...], before_ref[...])
    after = jnp.where(me == chain - 1, end_ref[...], after_ref[...])
    prev = [before] + [pos_ref[:, i, :] for i in range(count - 1)]
    nxt = [pos_ref[:, i, :] for i in range(1, count)] + [after]
    return prev, nxt


def partial_kernel(
    own_ref, rlo_ref, rup_ref, pos_ref, before_ref, after_ref, start_ref, end_ref,
    vel_ref, en1_ref, en2_ref, climb_ref, force_ref, send_ref, *, chain,
):
    count = pos_ref.shape[1]
    prev, nxt = chain_of(pos_ref, before_ref, after_ref, start_ref, end_ref, chain)
    values = []
    vel = jnp.zeros((1, 1), f32)
    for i in range(count):
        pos = pos_ref[:, i, :]
        force = own_ref[:, i, :] + jnp.concatenate([rlo_ref[:, i, :], rup_ref[:, i, :]], axis=1)
        force_ref[:, i, :] = force
        spread = nxt[i] - prev[i]
        ahead = nxt[i] - pos
        behind = pos - prev[i]
        values += [
            total_of(ahead * ahead),
            total_of(behind * behind),
            total_of(spread * spread),
            total_of(force * force),
            total_of(force * spread),
            total_of(en1_ref[i]) + total_of(en2_ref[i]),
        ]
        v = vel_ref[:, i, :]
        vel = vel + total_of(v * v)
    send_ref[...] = jnp.broadcast_to(lane_row(values + [vel, climb_ref[0].astype(f32)]), send_ref.shape)


def final_kernel(
    got_ref, force_ref, pos_ref, before_ref, after_ref, start_ref, end_ref,
    vel_ref, neb_ref, vnext_ref, pnext_ref, en_ref,
    *, chain, slabs,
):
    count = pos_ref.shape[1]
    atoms = pos_ref.shape[2]
    me = lax.axis_index("image")
    prev, nxt = chain_of(pos_ref, before_ref, after_ref, start_ref, end_ref, chain)
    rows = [
        jnp.sum(got_ref[g * slabs : (g + 1) * slabs, :], axis=0, keepdims=True)
        for g in range(chain)
    ]
    table = jnp.concatenate(rows, axis=0)
    climb = got_ref[0:1, 6 * count + 1 : 6 * count + 2]
    vel_sq = jnp.sum(table[:, 6 * count : 6 * count + 1], axis=0, keepdims=True)
    group = lax.broadcasted_iota(jnp.int32, (chain, 1), 0)
    force_sq = jnp.zeros((1, 1), f32)
    mine = []
    for i in range(count):
        ahead, behind, spread_sq, ff, fd, energy = [
            table[:, 6 * i + n : 6 * i + n + 1] for n in range(6)
        ]
        norm = 1.0 / jnp.sqrt(spread_sq + 1e-06)
        along = fd * norm
        climbing = jnp.where((group * count + i).astype(f32) == climb, 1.0, 0.0).astype(f32)
        spring = 5.0 * (jnp.sqrt(ahead) - jnp.sqrt(behind))
        coef = -(1.0 + climbing) * along + (1.0 - climbing) * spring
        scale = coef * norm
        part = ff + 2.0 * coef * along + scale * scale * spread_sq
        force_sq = force_sq + jnp.sum(part, axis=0, keepdims=True)
        here = group == me
        mine.append(jnp.sum(jnp.where(here, scale, 0.0), axis=0, keepdims=True))
        en_ref[i] = jnp.sum(jnp.where(here, energy, 0.0)) * (1.0 / (atoms * slabs))
    gain = 0.1 * jnp.sqrt(vel_sq / (force_sq + 1e-06))
    for i in range(count):
        neb = force_ref[:, i, :] + mine[i] * (nxt[i] - prev[i])
        neb_ref[:, i, :] = neb
        vnext = 0.9 * vel_ref[:, i, :] + gain * neb + 0.1 * neb
        vnext_ref[:, i, :] = vnext
        pnext_ref[:, i, :] = pos_ref[:, i, :] + 0.1 * vnext


def out(*shape):
    return jax.ShapeDtypeStruct(shape, f32)


def half(*shape):
    return jax.ShapeDtypeStruct(shape, bf16)


ANY = pl.BlockSpec(memory_space=pl.ANY)
VMEM = pl.BlockSpec(memory_space=pltpu.VMEM)
SMEM = pl.BlockSpec(memory_space=pltpu.SMEM)


def neighbours_of(cells, axis):
    count = lax.axis_size(axis)
    up = [(i, (i + 1) % count) for i in range(count)]
    down = [((i + 1) % count, i) for i in range(count)]
    to_below, to_above = cells
    return lax.ppermute(to_above, axis, up), lax.ppermute(to_below, axis, down)


def local(
    positions,
    velocity,
    start_state,
    end_state,
    neighbours,
    counts,
    climb_index,
    radial_a1,
    radial_b1,
    mix_first,
    read_first,
    radial_a2,
    radial_b2,
    mix_second,
    read_second,
):
    images, _, atoms = positions.shape
    slots = neighbours.shape[1]
    ghost = atoms // 2
    nb, rh = radial_a1.shape
    ch = radial_b1.shape[1]
    extent = atoms + 2 * ghost
    space = lax.axis_size("space")
    chain = lax.axis_size("image")
    params = pltpu.CompilerParams(vmem_limit_bytes=BIG_VMEM)
    small = pltpu.CompilerParams(vmem_limit_bytes=SMALL_VMEM)
    pos = positions.transpose(1, 0, 2)
    vel = velocity.transpose(1, 0, 2)

    plo, pup = neighbours_of((pos[:, :, :ghost], pos[:, :, ghost:]), "space")
    before = lax.ppermute(pos[:, images - 1], "image", [(i, i + 1) for i in range(chain - 1)])
    after = lax.ppermute(pos[:, 0], "image", [(i + 1, i) for i in range(chain - 1)])
    weights = (
        radial_a1, radial_b1, mix_first, read_first.reshape(1, ch),
        radial_a2, radial_b2, mix_second, read_second.reshape(1, ch),
    )
    idx, cnt, a1, b1, m1t, m1, b1t, r1, a2, b2, m2t, m2, r2 = pl.pallas_call(
        prep_kernel,
        in_specs=[pl.BlockSpec(memory_space=pltpu.HBM)] * 10,
        out_specs=[VMEM] * 13,
        out_shape=[
            jax.ShapeDtypeStruct(neighbours.shape, jnp.int32),
            jax.ShapeDtypeStruct(counts.shape, jnp.int32),
            half(rh, 3 * nb),
            half(ch, 3 * rh),
            half(ch, 9 * ch),
            half(3 * ch, 3 * ch),
            half(rh, 3 * ch),
            out(ch, 128),
            half(rh, 3 * nb),
            half(ch, 3 * rh),
            half(ch, 9 * ch),
            half(3 * ch, 3 * ch),
            out(ch, 128),
        ],
        scratch_shapes=[pltpu.VMEM(w.shape, f32) for w in weights]
        + [pltpu.SemaphoreType.DMA((10,))],
        compiler_params=small,
        cost_estimate=pl.CostEstimate(flops=4000000, bytes_accessed=4000000, transcendentals=0),
        name="prep",
    )(neighbours, counts, *weights)
    geo_n = NL + 1

    head, tail, geo, hid, dsl, mom, dpre, en1 = pl.pallas_call(
        functools.partial(first_kernel, images=images),
        in_specs=[VMEM] * 3 + [ANY] * 2 + [VMEM] * 6,
        out_specs=[VMEM] * 8,
        out_shape=[
            out(images, ch, ghost),
            out(images, ch, ghost),
            out(images, geo_n, slots, atoms),
            out(images, slots, rh, atoms),
            out(images, slots, rh, atoms),
            out(images, NL, ch, atoms),
            out(images, ch, atoms),
            out(images, 8, 128),
        ],
        scratch_shapes=[
            pltpu.VMEM((slots, NL - 1, 8, atoms), f32),
            pltpu.VMEM((NL, rh, atoms), f32),
        ],
        compiler_params=params,
        name="first",
    )(pos, plo, pup, before, after, idx, cnt, a1, b1, m1t, r1)

    hlo, hup = neighbours_of((head, tail), "space")

    dfh, dft, dlo, dup, dy2, dlen2, en2 = pl.pallas_call(
        functools.partial(second_kernel, images=images),
        in_specs=[VMEM] * 11,
        out_specs=[VMEM] * 7,
        out_shape=[out(images, ch, ghost)] * 4
        + [
            out(images, NL - 1, slots, atoms),
            out(images, slots, atoms),
            out(images, 8, 128),
        ],
        scratch_shapes=[
            pltpu.VMEM((slots, NL - 1, 8, atoms), f32),
            pltpu.VMEM((2 * ch, extent), bf16),
            pltpu.VMEM((extent, slots * atoms), bf16),
            pltpu.VMEM((slots, ch, atoms), f32),
            pltpu.VMEM((slots, ch, atoms), f32),
            pltpu.VMEM((slots, ch, atoms), f32),
            pltpu.VMEM((NL, ch, atoms), f32),
            pltpu.VMEM((2 * ch, slots * atoms), bf16),
        ],
        compiler_params=params,
        name="second",
    )(head, tail, hlo, hup, idx, geo, a2, b2, m2t, m2, r2)

    rlo, rup = neighbours_of((dlo, dup), "space")

    own, flo, fup = pl.pallas_call(
        functools.partial(third_kernel, images=images),
        in_specs=[VMEM] * 15,
        out_specs=[VMEM] * 3,
        out_shape=[out(3, images, atoms), out(3, images, ghost), out(3, images, ghost)],
        scratch_shapes=[
            pltpu.VMEM((slots, NL - 1, 8, atoms), f32),
            pltpu.VMEM((NL, ch, atoms), f32),
            pltpu.VMEM((NL, rh, atoms), f32),
            pltpu.VMEM((NL - 1, slots, atoms), f32),
            pltpu.VMEM((slots, atoms), f32),
            pltpu.VMEM((3, slots, atoms), f32),
        ],
        compiler_params=params,
        name="third",
    )(dfh, dft, rlo, rup, idx, geo, hid, dsl, mom, dpre, dy2, dlen2, b1t, m1, r1)

    glo, gup = neighbours_of((flo, fup), "space")

    rank = chain * space
    force, send = pl.pallas_call(
        functools.partial(partial_kernel, chain=chain),
        in_specs=[VMEM] * 11 + [SMEM],
        out_specs=[VMEM] * 2,
        out_shape=[out(3, images, atoms), out(rank, 128)],
        compiler_params=small,
        name="partial",
    )(own, glo, gup, pos, before, after, start_state, end_state, vel, en1, en2, climb_index)
    got = lax.all_to_all(
        send.reshape(rank, 1, 128), ("image", "space"), split_axis=0, concat_axis=0
    ).reshape(rank, 128)
    neb, vnext, pnext, energy = pl.pallas_call(
        functools.partial(final_kernel, chain=chain, slabs=space),
        in_specs=[VMEM] * 8,
        out_specs=[VMEM] * 3 + [SMEM],
        out_shape=[out(3, images, atoms)] * 3 + [out(images)],
        compiler_params=small,
        name="final",
    )(got, force, pos, before, after, start_state, end_state, vel)
    return (
        neb.transpose(1, 0, 2),
        vnext.transpose(1, 0, 2),
        pnext.transpose(1, 0, 2),
        energy,
    )


def solution(mesh):
    in_specs = (
        P("image", None, "space"),
        P("image", None, "space"),
        P(None, "space"),
        P(None, "space"),
        P("image", None, "space"),
        P("image", "space"),
        P(),
        P(),
        P(),
        P(),
        P(),
        P(),
        P(),
        P(),
        P(),
    )
    out_specs = (
        P("image", None, "space"),
        P("image", None, "space"),
        P("image", None, "space"),
        P("image"),
    )
    return jax.shard_map(local, mesh=mesh, in_specs=in_specs, out_specs=out_specs, check_vma=False)
```

```python
import functools
import math

import jax
import jax.numpy as jnp
from jax import lax
from jax.experimental import pallas as pl
from jax.experimental.pallas import tpu as pltpu
from jax.sharding import PartitionSpec as P

f32 = jnp.float32
bf16 = jnp.bfloat16
RT3 = math.sqrt(3.0)
NL = 9
BIG_VMEM = 16 << 20
SMALL_VMEM = 4 << 20


def split(x):
    hi = x.astype(bf16)
    lo = (x - hi.astype(f32)).astype(bf16)
    return hi, lo


def dot(a, b):
    return lax.dot_general(a, b, (((1,), (0,)), ((), ())), preferred_element_type=f32)


def dot_nt(a, b):
    return lax.dot_general(a, b, (((1,), (1,)), ((), ())), preferred_element_type=f32)


def pack_left(w):
    hi, lo = split(w)
    return jnp.concatenate([hi, hi, lo], axis=1)


def pack_right(x):
    hi, lo = split(x)
    return jnp.concatenate([hi, lo, hi], axis=0)


def one_hot(row, extent):
    step = 256
    wide = (step, row.shape[1])
    ids = lax.broadcasted_iota(jnp.int32, wide, 0).astype(f32).astype(bf16)
    zero, one = jnp.zeros(wide, bf16), jnp.ones(wide, bf16)
    parts = []
    for first in range(0, extent, step):
        here = jnp.broadcast_to((row - first).astype(f32), wide).astype(bf16)
        parts.append(jnp.where(ids == here, one, zero))
    return jnp.concatenate(parts, axis=0)


def lane_gather(row, idx):
    slots, atoms = idx.shape
    extent = row.shape[1]
    lane = idx & 127
    tile = idx >> 7
    blocks = [jnp.broadcast_to(row[:, t : t + 128], (8, 128)) for t in range(0, extent, 128)]
    out_rows = []
    for s0 in range(0, slots, 8):
        cells = []
        for a0 in range(0, atoms, 128):
            at = lane[s0 : s0 + 8, a0 : a0 + 128]
            which = tile[s0 : s0 + 8, a0 : a0 + 128]
            got = None
            for t, block in enumerate(blocks):
                v = jnp.take_along_axis(block, at, axis=1, mode="promise_in_bounds")
                got = v if got is None else jnp.where(which == t, v, got)
            cells.append(got)
        out_rows.append(jnp.concatenate(cells, axis=1))
    return jnp.concatenate(out_rows, axis=0)


def pick(block, i, axis):
    n = block.shape[axis]
    got = lax.index_in_dim(block, 0, axis, keepdims=False)
    for m in range(1, n):
        got = jnp.where(i == m, lax.index_in_dim(block, m, axis, keepdims=False), got)
    return got


def silu_parts(z):
    s = 0.5 + 0.5 * jnp.tanh(0.5 * z)
    h = z * s
    return h, s + h * (1.0 - s)


def basis_of(row):
    nb = 8
    centres = 0.5 * lax.broadcasted_iota(jnp.int32, (nb, row.shape[1]), 0).astype(f32)
    spread = row - centres
    basis = jnp.exp(-2.0 * spread * spread)
    return basis, -4.0 * spread * basis


def moments_into(edge_tile, yb_ref, m_ref, chans, slots, atoms):
    def tile(t, carry):
        c0 = pl.multiple_of(t * 16, 16)
        for a0 in range(0, atoms, 128):
            acc = [jnp.zeros((16, 128), f32) for _ in range(NL)]
            for k in range(slots):
                e = edge_tile(k, c0, a0)
                acc[0] = acc[0] + e
                for l in range(1, NL):
                    y = yb_ref[k, l - 1, :, a0 : a0 + 128]
                    acc[l] = acc[l] + e * jnp.concatenate([y, y], axis=0)
            for l in range(NL):
                m_ref[l, pl.ds(c0, 16), a0 : a0 + 128] = acc[l]
        return carry

    lax.fori_loop(0, chans // 16, tile, 0)


def store_yb(yb_ref, angular, slots, atoms):
    for k in range(slots):
        for l in range(NL - 1):
            yb_ref[k, l] = jnp.broadcast_to(angular[l][k : k + 1], (8, atoms))


def invariants_of(m_ref):
    m = [m_ref[l] for l in range(NL)]
    one = m[1] * m[1] + m[2] * m[2] + m[3] * m[3]
    two = m[4] * m[4] + m[5] * m[5] + m[6] * m[6] + m[7] * m[7] + m[8] * m[8]
    return jnp.concatenate([m[0], one, two], axis=0)


def moment_grads_into(m_ref, dinv, chans):
    m_ref[0] = dinv[:chans]
    d1 = 2.0 * dinv[chans : 2 * chans]
    d2 = 2.0 * dinv[2 * chans :]
    for l in range(1, NL):
        m_ref[l] = m_ref[l] * (d1 if l < 4 else d2)


def joined(parts):
    rows = []
    for w in parts:
        rows.append(jnp.pad(w, ((0, -w.shape[0] % 8), (0, 128 - w.shape[1]))))
    return jnp.concatenate(rows, axis=0)


def prep_kernel(
    all_ref, idx_ref, cnt_ref, idx_out, cnt_out, a1_out, b1_out, m1t_out, m1_out, b1t_out, r1_out,
    a2_out, b2_out, m2t_out, m2_out, r2_out,
):
    idx_out[...] = idx_ref[...]
    cnt_out[...] = cnt_ref[...]
    nb = a1_out.shape[1] // 3
    rh = a1_out.shape[0]
    ch = b1_out.shape[0]
    at = 0
    for a_out, b_out, bt_out, mt_out, m_out, r_out in (
        (a1_out, b1_out, b1t_out, m1t_out, m1_out, r1_out),
        (a2_out, b2_out, None, m2t_out, m2_out, r2_out),
    ):
        a_out[...] = pack_left(all_ref[at : at + nb, :].T[:rh])
        at += nb
        b = all_ref[at : at + rh, :]
        b_out[...] = pack_left(b.T)
        if bt_out is not None:
            bt_out[...] = pack_left(b)
        at += rh
        m = all_ref[at : at + 3 * ch, :]
        mt_out[...] = pack_left(m.T)
        m_out[...] = pack_left(m)
        at += 3 * ch
        r_out[...] = jnp.broadcast_to(all_ref[at : at + 1, :], r_out.shape[::-1]).T
        at += 8


def energy_rows(read_ref, feat):
    ch, atoms = feat.shape
    read = read_ref[...]
    en = jnp.concatenate([read] * (atoms // 128), axis=1) * feat
    total = jnp.sum(en.reshape(ch // 8, 8, atoms), axis=0)
    return sum(total[:, a0 : a0 + 128] for a0 in range(0, atoms, 128))


def wide(read_ref, atoms):
    return jnp.concatenate([read_ref[...]] * (atoms // 128), axis=1)


def each_image(body):
    def kernel(*refs, images):
        def step(i, carry):
            body(i, *refs)
            return carry

        lax.fori_loop(0, images, step, 0)

    return kernel


@each_image
def first_kernel(
    i, pos_ref, plo_ref, pup_ref, before_ref, after_ref, idx_ref, cnt_ref, a_ref, b_ref, mixt_ref,
    read_ref, head_ref, tail_ref, geo_ref, hid_ref, dsl_ref, mom_ref, dpre_ref, en_ref,
    yb_ref, g_ref,
):
    slots, atoms = idx_ref.shape[1:]
    ghost = plo_ref.shape[2]
    idx = idx_ref[i]
    pos = pick(pos_ref[...], i, 1)
    plo = pick(plo_ref[...], i, 1)
    pup = pick(pup_ref[...], i, 1)
    ext = jnp.concatenate([plo, pos, pup], axis=1)
    off = [lane_gather(ext[x : x + 1], idx) - pos[x : x + 1] for x in range(3)]
    length = jnp.sqrt(off[0] * off[0] + off[1] * off[1] + off[2] * off[2] + 1.0)
    ux, uy, uz = [o / length for o in off]
    ids = lax.broadcasted_iota(jnp.int32, (slots, atoms), 0)
    cnt = pick(cnt_ref[...][None], i, 1)
    live = jnp.where(ids < cnt, 1.0 / slots, 0.0).astype(f32)
    angular = [
        ux,
        uy,
        uz,
        ux * uy,
        uy * uz,
        ux * uz,
        0.5 * (ux * ux - uy * uy),
        (3.0 * uz * uz - 1.0) / (2.0 * RT3),
    ]
    for l in range(NL - 1):
        geo_ref[i, l] = angular[l]
    geo_ref[i, NL - 1] = length
    geo_ref[i, NL] = live
    store_yb(yb_ref, angular, slots, atoms)
    for k in range(slots):
        basis, slope = basis_of(length[k : k + 1])
        hid, ds = silu_parts(dot(a_ref[...], pack_right(basis)))
        row = live[k : k + 1]
        hid_ref[i, k] = hid * row
        dsl_ref[i, k] = ds * row * dot(a_ref[...], pack_right(slope))

    def hid_tile(k, c0, a0):
        return hid_ref[i, k, pl.ds(c0, 16), a0 : a0 + 128]

    moments_into(hid_tile, yb_ref, g_ref, hid_ref.shape[2], slots, atoms)
    for l in range(NL):
        mom_ref[i, l] = dot(b_ref[...], pack_right(g_ref[l]))
    inv = invariants_of(mom_ref.at[i])
    feat, dpre = silu_parts(dot(mixt_ref[...], pack_right(inv)))
    dpre_ref[i] = dpre
    head_ref[i] = feat[:, :ghost]
    tail_ref[i] = feat[:, atoms - ghost :]
    en_ref[i] = energy_rows(read_ref, feat)


def edge_back(k, edge_tile, sink, yb_ref, m_ref, dy_ref, dlen_ref, chans, atoms):
    for a0 in range(0, atoms, 128):
        y = [yb_ref[k, l, :, a0 : a0 + 128] for l in range(NL - 1)]
        y = [jnp.concatenate([v, v], axis=0) for v in y]
        acc = [jnp.zeros((8, 128), f32) for _ in range(NL)]
        for c0 in range(0, chans, 16):
            e = edge_tile(k, c0, a0)
            de = m_ref[0, c0 : c0 + 16, a0 : a0 + 128]
            for l in range(1, NL):
                dm = m_ref[l, c0 : c0 + 16, a0 : a0 + 128]
                de = de + dm * y[l - 1]
                p = e * dm
                acc[l] = acc[l] + (p[:8] + p[8:])
            p = sink(k, c0, a0, de)
            acc[0] = acc[0] + (p[:8] + p[8:])
        for l in range(1, NL):
            dy_ref[l - 1, k : k + 1, a0 : a0 + 128] = jnp.sum(acc[l], axis=0, keepdims=True)
        dlen_ref[k : k + 1, a0 : a0 + 128] = jnp.sum(acc[0], axis=0, keepdims=True)


@each_image
def radial_kernel(i, geo_ref, a_ref, b_ref, rad_ref, radl_ref):
    for k in range(rad_ref.shape[1]):
        basis, slope = basis_of(geo_ref[i, NL - 1, k : k + 1, :])
        row = geo_ref[i, NL, k : k + 1, :]
        hid, ds = silu_parts(dot(a_ref[...], pack_right(basis)))
        rad_ref[i, k] = dot(b_ref[...], pack_right(hid * row))
        dsl = ds * row * dot(a_ref[...], pack_right(slope))
        radl_ref[i, k] = dot(b_ref[...], pack_right(dsl))


@each_image
def second_kernel(
    i, head_ref, tail_ref, hlo_ref, hup_ref, idx_ref, geo_ref, rad_ref, radl_ref, mixt_ref,
    mix_ref, read_ref, dfh_ref, dft_ref, dlo_ref, dup_ref, dlen_ref, en_ref, q_ref, m_ref,
    yb_ref, hf_ref, oh_ref, dq_ref,
):
    slots, atoms = idx_ref.shape[1:]
    ghost = hlo_ref.shape[2]
    ch = hlo_ref.shape[1]
    extent = atoms + 2 * ghost
    for n, ref in enumerate((hlo_ref, head_ref, tail_ref, hup_ref)):
        hi, lo = split(ref[i])
        hf_ref[:ch, n * ghost : (n + 1) * ghost] = hi
        hf_ref[ch:, n * ghost : (n + 1) * ghost] = lo
    store_yb(yb_ref, [geo_ref[i, l] for l in range(NL - 1)], slots, atoms)
    for k in range(slots):
        oh = one_hot(idx_ref[i, k : k + 1, :], extent)
        oh_ref[:, k * atoms : (k + 1) * atoms] = oh
        got = dot(hf_ref[...], oh)
        q_ref[i, k] = got[:ch] + got[ch:]

    def edge_tile(k, c0, a0):
        cs = pl.ds(c0, 16)
        return rad_ref[i, k, cs, a0 : a0 + 128] * q_ref[i, k, cs, a0 : a0 + 128]

    m = m_ref.at[i]
    moments_into(edge_tile, yb_ref, m, ch, slots, atoms)
    inv = invariants_of(m)
    feat, dpre = silu_parts(dot(mixt_ref[...], pack_right(inv)))
    en_ref[i] = energy_rows(read_ref, feat)
    dinv = dot(mix_ref[...], pack_right(wide(read_ref, atoms) * dpre))
    moment_grads_into(m, dinv, ch)
    for k in range(slots):
        for a0 in range(0, atoms, 128):
            ls = slice(a0, a0 + 128)
            y = [yb_ref[k, l, :, ls] for l in range(NL - 1)]
            y = [jnp.concatenate([v, v], axis=0) for v in y]
            acc = jnp.zeros((8, 128), f32)
            ks = slice(k * atoms + a0, k * atoms + a0 + 128)
            for c0 in range(0, ch, 16):
                cs = slice(c0, c0 + 16)
                de = m[0, cs, ls]
                for l in range(1, NL):
                    de = de + m[l, cs, ls] * y[l - 1]
                hi, lo = split(de * rad_ref[i, k, cs, ls])
                dq_ref[cs, ks] = hi
                dq_ref[ch + c0 : ch + c0 + 16, ks] = lo
                p = de * q_ref[i, k, cs, ls] * radl_ref[i, k, cs, ls]
                acc = acc + (p[:8] + p[8:])
            dlen_ref[i, k : k + 1, ls] = jnp.sum(acc, axis=0, keepdims=True)
    back = dot_nt(dq_ref[...], oh_ref[...])
    back = back[:ch] + back[ch:]
    dlo_ref[i] = back[:, :ghost]
    dfh_ref[i] = back[:, ghost : 2 * ghost]
    dft_ref[i] = back[:, 2 * ghost : 3 * ghost]
    dup_ref[i] = back[:, 3 * ghost :]


@each_image
def angular_kernel(i, rad_ref, q_ref, m_ref, dy_ref):
    slots, ch, atoms = rad_ref.shape[1:]
    for k in range(slots):
        for a0 in range(0, atoms, 128):
            ls = slice(a0, a0 + 128)
            acc = [jnp.zeros((8, 128), f32) for _ in range(NL)]
            for c0 in range(0, ch, 16):
                cs = slice(c0, c0 + 16)
                e = rad_ref[i, k, cs, ls] * q_ref[i, k, cs, ls]
                for l in range(1, NL):
                    p = e * m_ref[i, l, cs, ls]
                    acc[l] = acc[l] + (p[:8] + p[8:])
            for l in range(1, NL):
                dy_ref[i, l - 1, k : k + 1, ls] = jnp.sum(acc[l], axis=0, keepdims=True)


@each_image
def third_kernel(
    i, dfh_ref, dft_ref, rlo_ref, rup_ref, idx_ref, geo_ref, hid_ref, dsl_ref, mom_ref, dpre_ref,
    dy2_ref, dlen2_ref, bt_ref, mix_ref, read_ref,
    own_ref, flo_ref, fup_ref,
    yb_ref, m_ref, dg_ref, dy_ref, dlen_ref, doff_ref,
):
    slots, atoms = idx_ref.shape[1:]
    ch, ghost = rlo_ref.shape[1:]
    rh = hid_ref.shape[2]
    extent = atoms + 2 * ghost
    store_yb(yb_ref, [geo_ref[i, l] for l in range(NL - 1)], slots, atoms)
    cot = jnp.concatenate([dfh_ref[i] + rlo_ref[i], dft_ref[i] + rup_ref[i]], axis=1)
    dpre = (cot + wide(read_ref, atoms)) * dpre_ref[i]
    dinv = dot(mix_ref[...], pack_right(dpre))
    for l in range(NL):
        m_ref[l] = mom_ref[i, l]
    moment_grads_into(m_ref, dinv, ch)
    for l in range(NL):
        dg_ref[l] = dot(bt_ref[...], pack_right(m_ref[l]))

    def edge_tile(k, c0, a0):
        return hid_ref[i, k, pl.ds(c0, 16), a0 : a0 + 128]

    def sink(k, c0, a0, de):
        return de * dsl_ref[i, k, c0 : c0 + 16, a0 : a0 + 128]

    for k in range(slots):
        edge_back(k, edge_tile, sink, yb_ref, dg_ref, dy_ref, dlen_ref, rh, atoms)
    dy = [None] + [dy_ref[l] + dy2_ref[i, l] for l in range(NL - 1)]
    ux, uy, uz = [geo_ref[i, n] for n in range(3)]
    length = geo_ref[i, NL - 1]
    dux = dy[1] + uy * dy[4] + uz * dy[6] + ux * dy[7]
    duy = dy[2] + ux * dy[4] + uz * dy[5] - uy * dy[7]
    duz = dy[3] + uy * dy[5] + ux * dy[6] + RT3 * uz * dy[8]
    radial = dlen_ref[...] + dlen2_ref[i] - (dux * ux + duy * uy + duz * uz) / length
    doff = [du / length + radial * u for du, u in ((dux, ux), (duy, uy), (duz, uz))]
    centre = jnp.concatenate([jnp.sum(d, axis=0, keepdims=True) for d in doff], axis=0)
    for x in range(3):
        doff_ref[x] = doff[x]
    back = jnp.zeros((16, extent), f32)
    pad = jnp.zeros((5, atoms), f32)
    for k in range(slots):
        rows = jnp.concatenate([doff_ref[x, k : k + 1, :] for x in range(3)] + [pad], axis=0)
        hi = rows.astype(bf16).astype(f32)
        both = jnp.concatenate([hi, rows - hi], axis=0).astype(bf16)
        back = back + dot_nt(both, one_hot(idx_ref[i, k : k + 1, :], extent))
    force = back[8:11] + back[:3]
    for n in range(own_ref.shape[1]):

        @pl.when(i == n)
        def _():
            own_ref[:, n, :] = centre - force[:, ghost : ghost + atoms]
            flo_ref[:, n, :] = -force[:, :ghost]
            fup_ref[:, n, :] = -force[:, ghost + atoms :]


def lane_row(values):
    lane = lax.broadcasted_iota(jnp.int32, (1, 128), 1)
    row = jnp.zeros((1, 128), f32)
    for n, v in enumerate(values):
        row = jnp.where(lane == n, v, row)
    return row


def total_of(x):
    return jnp.sum(jnp.sum(x, axis=1, keepdims=True), axis=0, keepdims=True)


def chain_of(pos_ref, before_ref, after_ref, start_ref, end_ref, chain):
    count = pos_ref.shape[1]
    me = lax.axis_index("image")
    before = jnp.where(me == 0, start_ref[...], before_ref[...])
    after = jnp.where(me == chain - 1, end_ref[...], after_ref[...])
    prev = [before] + [pos_ref[:, i, :] for i in range(count - 1)]
    nxt = [pos_ref[:, i, :] for i in range(1, count)] + [after]
    return prev, nxt


def partial_kernel(
    own_ref, rlo_ref, rup_ref, pos_ref, before_ref, after_ref, start_ref, end_ref,
    vel_ref, en1_ref, en2_ref, climb_ref, force_ref, send_ref, *, chain,
):
    count = pos_ref.shape[1]
    prev, nxt = chain_of(pos_ref, before_ref, after_ref, start_ref, end_ref, chain)
    values = []
    vel = jnp.zeros((1, 1), f32)
    for i in range(count):
        pos = pos_ref[:, i, :]
        force = own_ref[:, i, :] + jnp.concatenate([rlo_ref[:, i, :], rup_ref[:, i, :]], axis=1)
        force_ref[:, i, :] = force
        spread = nxt[i] - prev[i]
        ahead = nxt[i] - pos
        behind = pos - prev[i]
        values += [
            total_of(ahead * ahead),
            total_of(behind * behind),
            total_of(spread * spread),
            total_of(force * force),
            total_of(force * spread),
            total_of(en1_ref[i]) + total_of(en2_ref[i]),
        ]
        v = vel_ref[:, i, :]
        vel = vel + total_of(v * v)
    send_ref[...] = jnp.broadcast_to(lane_row(values + [vel, climb_ref[0].astype(f32)]), send_ref.shape)


def final_kernel(
    got_ref, force_ref, pos_ref, before_ref, after_ref, start_ref, end_ref,
    vel_ref, neb_ref, vnext_ref, pnext_ref, en_ref,
    *, chain, slabs,
):
    count = pos_ref.shape[1]
    atoms = pos_ref.shape[2]
    me = lax.axis_index("image")
    prev, nxt = chain_of(pos_ref, before_ref, after_ref, start_ref, end_ref, chain)
    rows = [
        jnp.sum(got_ref[g * slabs : (g + 1) * slabs, :], axis=0, keepdims=True)
        for g in range(chain)
    ]
    table = jnp.concatenate(rows, axis=0)
    climb = got_ref[0:1, 6 * count + 1 : 6 * count + 2]
    vel_sq = jnp.sum(table[:, 6 * count : 6 * count + 1], axis=0, keepdims=True)
    group = lax.broadcasted_iota(jnp.int32, (chain, 1), 0)
    force_sq = jnp.zeros((1, 1), f32)
    mine = []
    for i in range(count):
        ahead, behind, spread_sq, ff, fd, energy = [
            table[:, 6 * i + n : 6 * i + n + 1] for n in range(6)
        ]
        norm = 1.0 / jnp.sqrt(spread_sq + 1e-06)
        along = fd * norm
        climbing = jnp.where((group * count + i).astype(f32) == climb, 1.0, 0.0).astype(f32)
        spring = 5.0 * (jnp.sqrt(ahead) - jnp.sqrt(behind))
        coef = -(1.0 + climbing) * along + (1.0 - climbing) * spring
        scale = coef * norm
        part = ff + 2.0 * coef * along + scale * scale * spread_sq
        force_sq = force_sq + jnp.sum(part, axis=0, keepdims=True)
        here = group == me
        mine.append(jnp.sum(jnp.where(here, scale, 0.0), axis=0, keepdims=True))
        en_ref[i] = jnp.sum(jnp.where(here, energy, 0.0)) * (1.0 / (atoms * slabs))
    gain = 0.1 * jnp.sqrt(vel_sq / (force_sq + 1e-06))
    for i in range(count):
        neb = force_ref[:, i, :] + mine[i] * (nxt[i] - prev[i])
        neb_ref[:, i, :] = neb
        vnext = 0.9 * vel_ref[:, i, :] + gain * neb + 0.1 * neb
        vnext_ref[:, i, :] = vnext
        pnext_ref[:, i, :] = pos_ref[:, i, :] + 0.1 * vnext


def out(*shape):
    return jax.ShapeDtypeStruct(shape, f32)


def half(*shape):
    return jax.ShapeDtypeStruct(shape, bf16)


ANY = pl.BlockSpec(memory_space=pl.ANY)
VMEM = pl.BlockSpec(memory_space=pltpu.VMEM)
SMEM = pl.BlockSpec(memory_space=pltpu.SMEM)


def neighbours_of(cells, axis):
    count = lax.axis_size(axis)
    up = [(i, (i + 1) % count) for i in range(count)]
    down = [((i + 1) % count, i) for i in range(count)]
    to_below, to_above = cells
    return lax.ppermute(to_above, axis, up), lax.ppermute(to_below, axis, down)


def local(
    positions,
    velocity,
    start_state,
    end_state,
    neighbours,
    counts,
    climb_index,
    radial_a1,
    radial_b1,
    mix_first,
    read_first,
    radial_a2,
    radial_b2,
    mix_second,
    read_second,
):
    images, _, atoms = positions.shape
    slots = neighbours.shape[1]
    ghost = atoms // 2
    nb, rh = radial_a1.shape
    ch = radial_b1.shape[1]
    extent = atoms + 2 * ghost
    space = lax.axis_size("space")
    chain = lax.axis_size("image")
    params = pltpu.CompilerParams(vmem_limit_bytes=BIG_VMEM)
    small = pltpu.CompilerParams(vmem_limit_bytes=SMALL_VMEM)
    pos = positions.transpose(1, 0, 2)
    vel = velocity.transpose(1, 0, 2)

    plo, pup = neighbours_of((pos[:, :, :ghost], pos[:, :, ghost:]), "space")
    before = lax.ppermute(pos[:, images - 1], "image", [(i, i + 1) for i in range(chain - 1)])
    after = lax.ppermute(pos[:, 0], "image", [(i + 1, i) for i in range(chain - 1)])
    weights = (
        radial_a1, radial_b1, mix_first, read_first.reshape(1, ch),
        radial_a2, radial_b2, mix_second, read_second.reshape(1, ch),
    )
    idx, cnt, a1, b1, m1t, m1, b1t, r1, a2, b2, m2t, m2, r2 = pl.pallas_call(
        prep_kernel,
        in_specs=[VMEM] * 3,
        out_specs=[VMEM] * 13,
        out_shape=[
            jax.ShapeDtypeStruct(neighbours.shape, jnp.int32),
            jax.ShapeDtypeStruct(counts.shape, jnp.int32),
            half(rh, 3 * nb),
            half(ch, 3 * rh),
            half(ch, 9 * ch),
            half(3 * ch, 3 * ch),
            half(rh, 3 * ch),
            out(ch, 128),
            half(rh, 3 * nb),
            half(ch, 3 * rh),
            half(ch, 9 * ch),
            half(3 * ch, 3 * ch),
            out(ch, 128),
        ],
        compiler_params=small,
        cost_estimate=pl.CostEstimate(flops=4000000, bytes_accessed=4000000, transcendentals=0),
        name="prep",
    )(joined(weights), neighbours, counts)
    geo_n = NL + 1

    head, tail, geo, hid, dsl, mom, dpre, en1 = pl.pallas_call(
        functools.partial(first_kernel, images=images),
        in_specs=[VMEM] * 3 + [ANY] * 2 + [VMEM] * 6,
        out_specs=[VMEM] * 8,
        out_shape=[
            out(images, ch, ghost),
            out(images, ch, ghost),
            out(images, geo_n, slots, atoms),
            out(images, slots, rh, atoms),
            out(images, slots, rh, atoms),
            out(images, NL, ch, atoms),
            out(images, ch, atoms),
            out(images, 8, 128),
        ],
        scratch_shapes=[
            pltpu.VMEM((slots, NL - 1, 8, atoms), f32),
            pltpu.VMEM((NL, rh, atoms), f32),
        ],
        compiler_params=params,
        name="first",
    )(pos, plo, pup, before, after, idx, cnt, a1, b1, m1t, r1)

    hlo, hup = neighbours_of((head, tail), "space")

    rad, radl = pl.pallas_call(
        functools.partial(radial_kernel, images=images),
        in_specs=[VMEM] * 3,
        out_specs=[VMEM] * 2,
        out_shape=[out(images, slots, ch, atoms)] * 2,
        compiler_params=small,
        cost_estimate=pl.CostEstimate(flops=1 << 30, bytes_accessed=1 << 23, transcendentals=1 << 20),
        name="radial",
    )(geo, a2, b2)
    dfh, dft, dlo, dup, dlen2, en2, q, dm = pl.pallas_call(
        functools.partial(second_kernel, images=images),
        in_specs=[VMEM] * 11,
        out_specs=[VMEM] * 8,
        out_shape=[out(images, ch, ghost)] * 4
        + [
            out(images, slots, atoms),
            out(images, 8, 128),
            out(images, slots, ch, atoms),
            out(images, NL, ch, atoms),
        ],
        scratch_shapes=[
            pltpu.VMEM((slots, NL - 1, 8, atoms), f32),
            pltpu.VMEM((2 * ch, extent), bf16),
            pltpu.VMEM((extent, slots * atoms), bf16),
            pltpu.VMEM((2 * ch, slots * atoms), bf16),
        ],
        compiler_params=params,
        name="second",
    )(head, tail, hlo, hup, idx, geo, rad, radl, m2t, m2, r2)

    rlo, rup = neighbours_of((dlo, dup), "space")
    dy2 = pl.pallas_call(
        functools.partial(angular_kernel, images=images),
        in_specs=[VMEM] * 3,
        out_specs=VMEM,
        out_shape=out(images, NL - 1, slots, atoms),
        compiler_params=small,
        cost_estimate=pl.CostEstimate(flops=1 << 30, bytes_accessed=1 << 23, transcendentals=0),
        name="angular",
    )(rad, q, dm)

    own, flo, fup = pl.pallas_call(
        functools.partial(third_kernel, images=images),
        in_specs=[VMEM] * 15,
        out_specs=[VMEM] * 3,
        out_shape=[out(3, images, atoms), out(3, images, ghost), out(3, images, ghost)],
        scratch_shapes=[
            pltpu.VMEM((slots, NL - 1, 8, atoms), f32),
            pltpu.VMEM((NL, ch, atoms), f32),
            pltpu.VMEM((NL, rh, atoms), f32),
            pltpu.VMEM((NL - 1, slots, atoms), f32),
            pltpu.VMEM((slots, atoms), f32),
            pltpu.VMEM((3, slots, atoms), f32),
        ],
        compiler_params=params,
        name="third",
    )(dfh, dft, rlo, rup, idx, geo, hid, dsl, mom, dpre, dy2, dlen2, b1t, m1, r1)

    glo, gup = neighbours_of((flo, fup), "space")

    rank = chain * space
    force, send = pl.pallas_call(
        functools.partial(partial_kernel, chain=chain),
        in_specs=[VMEM] * 11 + [SMEM],
        out_specs=[VMEM] * 2,
        out_shape=[out(3, images, atoms), out(rank, 128)],
        compiler_params=small,
        name="partial",
    )(own, glo, gup, pos, before, after, start_state, end_state, vel, en1, en2, climb_index)
    got = lax.all_to_all(
        send.reshape(rank, 1, 128), ("image", "space"), split_axis=0, concat_axis=0
    ).reshape(rank, 128)
    neb, vnext, pnext, energy = pl.pallas_call(
        functools.partial(final_kernel, chain=chain, slabs=space),
        in_specs=[VMEM] * 8,
        out_specs=[VMEM] * 3 + [SMEM],
        out_shape=[out(3, images, atoms)] * 3 + [out(images)],
        compiler_params=small,
        name="final",
    )(got, force, pos, before, after, start_state, end_state, vel)
    return (
        neb.transpose(1, 0, 2),
        vnext.transpose(1, 0, 2),
        pnext.transpose(1, 0, 2),
        energy,
    )


def solution(mesh):
    in_specs = (
        P("image", None, "space"),
        P("image", None, "space"),
        P(None, "space"),
        P(None, "space"),
        P("image", None, "space"),
        P("image", "space"),
        P(),
        P(),
        P(),
        P(),
        P(),
        P(),
        P(),
        P(),
        P(),
    )
    out_specs = (
        P("image", None, "space"),
        P("image", None, "space"),
        P("image", None, "space"),
        P("image"),
    )
    return jax.shard_map(local, mesh=mesh, in_specs=in_specs, out_specs=out_specs, check_vma=False)
```

```python
import functools
import math

import jax
import jax.numpy as jnp
from jax import lax
from jax.experimental import pallas as pl
from jax.experimental.pallas import tpu as pltpu
from jax.sharding import PartitionSpec as P

f32 = jnp.float32
bf16 = jnp.bfloat16
RT3 = math.sqrt(3.0)
NL = 9
BIG_VMEM = 16 << 20
SMALL_VMEM = 4 << 20


def split(x):
    hi = x.astype(bf16)
    lo = (x - hi.astype(f32)).astype(bf16)
    return hi, lo


def dot(a, b):
    return lax.dot_general(a, b, (((1,), (0,)), ((), ())), preferred_element_type=f32)


def dot_nt(a, b):
    return lax.dot_general(a, b, (((1,), (1,)), ((), ())), preferred_element_type=f32)


def pack_left(w):
    hi, lo = split(w)
    return jnp.concatenate([hi, hi, lo], axis=1)


def pack_right(x):
    hi, lo = split(x)
    return jnp.concatenate([hi, lo, hi], axis=0)


def one_hot(row, extent):
    step = 256
    wide = (step, row.shape[1])
    ids = lax.broadcasted_iota(jnp.int32, wide, 0).astype(f32).astype(bf16)
    zero, one = jnp.zeros(wide, bf16), jnp.ones(wide, bf16)
    parts = []
    for first in range(0, extent, step):
        here = jnp.broadcast_to((row - first).astype(f32), wide).astype(bf16)
        parts.append(jnp.where(ids == here, one, zero))
    return jnp.concatenate(parts, axis=0)


def lane_gather(row, idx):
    slots, atoms = idx.shape
    extent = row.shape[1]
    lane = idx & 127
    tile = idx >> 7
    blocks = [jnp.broadcast_to(row[:, t : t + 128], (8, 128)) for t in range(0, extent, 128)]
    out_rows = []
    for s0 in range(0, slots, 8):
        cells = []
        for a0 in range(0, atoms, 128):
            at = lane[s0 : s0 + 8, a0 : a0 + 128]
            which = tile[s0 : s0 + 8, a0 : a0 + 128]
            got = None
            for t, block in enumerate(blocks):
                v = jnp.take_along_axis(block, at, axis=1, mode="promise_in_bounds")
                got = v if got is None else jnp.where(which == t, v, got)
            cells.append(got)
        out_rows.append(jnp.concatenate(cells, axis=1))
    return jnp.concatenate(out_rows, axis=0)


def pick(block, i, axis):
    n = block.shape[axis]
    got = lax.index_in_dim(block, 0, axis, keepdims=False)
    for m in range(1, n):
        got = jnp.where(i == m, lax.index_in_dim(block, m, axis, keepdims=False), got)
    return got


def silu_parts(z):
    s = 0.5 + 0.5 * jnp.tanh(0.5 * z)
    h = z * s
    return h, s + h * (1.0 - s)


def basis_of(row):
    nb = 8
    centres = 0.5 * lax.broadcasted_iota(jnp.int32, (nb, row.shape[1]), 0).astype(f32)
    spread = row - centres
    basis = jnp.exp(-2.0 * spread * spread)
    return basis, -4.0 * spread * basis


def moments_into(edge_tile, yb_ref, m_ref, chans, slots, atoms):
    def tile(t, carry):
        c0 = pl.multiple_of(t * 16, 16)
        for a0 in range(0, atoms, 128):
            acc = [jnp.zeros((16, 128), f32) for _ in range(NL)]
            for k in range(slots):
                e = edge_tile(k, c0, a0)
                acc[0] = acc[0] + e
                for l in range(1, NL):
                    y = yb_ref[k, l - 1, :, a0 : a0 + 128]
                    acc[l] = acc[l] + e * jnp.concatenate([y, y], axis=0)
            for l in range(NL):
                m_ref[l, pl.ds(c0, 16), a0 : a0 + 128] = acc[l]
        return carry

    lax.fori_loop(0, chans // 16, tile, 0)


def store_yb(yb_ref, angular, slots, atoms):
    for k in range(slots):
        for l in range(NL - 1):
            yb_ref[k, l] = jnp.broadcast_to(angular[l][k : k + 1], (8, atoms))


def invariants_of(m_ref):
    m = [m_ref[l] for l in range(NL)]
    one = m[1] * m[1] + m[2] * m[2] + m[3] * m[3]
    two = m[4] * m[4] + m[5] * m[5] + m[6] * m[6] + m[7] * m[7] + m[8] * m[8]
    return jnp.concatenate([m[0], one, two], axis=0)


def moment_grads_into(m_ref, dinv, chans):
    m_ref[0] = dinv[:chans]
    d1 = 2.0 * dinv[chans : 2 * chans]
    d2 = 2.0 * dinv[2 * chans :]
    for l in range(1, NL):
        m_ref[l] = m_ref[l] * (d1 if l < 4 else d2)


def prep_kernel(*refs):
    n = 10
    hbm, outs, bufs, sems = refs[:n], refs[n : n + 13], refs[n + 13 : -1], refs[-1]
    (
        idx_out, cnt_out, a1_out, b1_out, m1t_out, m1_out, b1t_out, r1_out,
        a2_out, b2_out, m2t_out, m2_out, r2_out,
    ) = outs
    a1, b1, m1, r1, a2, b2, m2, r2 = bufs
    targets = (idx_out, cnt_out) + bufs
    copies = [pltpu.make_async_copy(h, t, sems.at[q]) for q, (h, t) in enumerate(zip(hbm, targets))]
    for c in copies:
        c.start()
    for c in copies:
        c.wait()
    a1_out[...] = pack_left(a1[...].T)
    b1_out[...] = pack_left(b1[...].T)
    m1t_out[...] = pack_left(m1[...].T)
    m1_out[...] = pack_left(m1[...])
    b1t_out[...] = pack_left(b1[...])
    r1_out[...] = jnp.broadcast_to(r1[...], r1_out.shape[::-1]).T
    a2_out[...] = pack_left(a2[...].T)
    b2_out[...] = pack_left(b2[...].T)
    m2t_out[...] = pack_left(m2[...].T)
    m2_out[...] = pack_left(m2[...])
    r2_out[...] = jnp.broadcast_to(r2[...], r2_out.shape[::-1]).T


def energy_rows(read_ref, feat):
    ch, atoms = feat.shape
    read = read_ref[...]
    en = jnp.concatenate([read] * (atoms // 128), axis=1) * feat
    total = jnp.sum(en.reshape(ch // 8, 8, atoms), axis=0)
    return sum(total[:, a0 : a0 + 128] for a0 in range(0, atoms, 128))


def wide(read_ref, atoms):
    return jnp.concatenate([read_ref[...]] * (atoms // 128), axis=1)


def each_image(body):
    def kernel(*refs, images):
        def step(i, carry):
            body(i, *refs)
            return carry

        lax.fori_loop(0, images, step, 0)

    return kernel


@each_image
def first_kernel(
    i, pos_ref, plo_ref, pup_ref, before_ref, after_ref, idx_ref, cnt_ref, a_ref, b_ref, mixt_ref,
    read_ref, head_ref, tail_ref, geo_ref, hid_ref, dsl_ref, mom_ref, dpre_ref, en_ref,
    yb_ref, g_ref,
):
    slots, atoms = idx_ref.shape[1:]
    ghost = plo_ref.shape[2]
    idx = idx_ref[i]
    pos = pick(pos_ref[...], i, 1)
    plo = pick(plo_ref[...], i, 1)
    pup = pick(pup_ref[...], i, 1)
    ext = jnp.concatenate([plo, pos, pup], axis=1)
    off = [lane_gather(ext[x : x + 1], idx) - pos[x : x + 1] for x in range(3)]
    length = jnp.sqrt(off[0] * off[0] + off[1] * off[1] + off[2] * off[2] + 1.0)
    ux, uy, uz = [o / length for o in off]
    ids = lax.broadcasted_iota(jnp.int32, (slots, atoms), 0)
    cnt = pick(cnt_ref[...][None], i, 1)
    live = jnp.where(ids < cnt, 1.0 / slots, 0.0).astype(f32)
    angular = [
        ux,
        uy,
        uz,
        ux * uy,
        uy * uz,
        ux * uz,
        0.5 * (ux * ux - uy * uy),
        (3.0 * uz * uz - 1.0) / (2.0 * RT3),
    ]
    for l in range(NL - 1):
        geo_ref[i, l] = angular[l]
    geo_ref[i, NL - 1] = length
    geo_ref[i, NL] = live
    store_yb(yb_ref, angular, slots, atoms)
    for k in range(slots):
        basis, slope = basis_of(length[k : k + 1])
        hid, ds = silu_parts(dot(a_ref[...], pack_right(basis)))
        row = live[k : k + 1]
        hid_ref[i, k] = hid * row
        dsl_ref[i, k] = ds * row * dot(a_ref[...], pack_right(slope))

    def hid_tile(k, c0, a0):
        return hid_ref[i, k, pl.ds(c0, 16), a0 : a0 + 128]

    moments_into(hid_tile, yb_ref, g_ref, hid_ref.shape[2], slots, atoms)
    for l in range(NL):
        mom_ref[i, l] = dot(b_ref[...], pack_right(g_ref[l]))
    inv = invariants_of(mom_ref.at[i])
    feat, dpre = silu_parts(dot(mixt_ref[...], pack_right(inv)))
    dpre_ref[i] = dpre
    head_ref[i] = feat[:, :ghost]
    tail_ref[i] = feat[:, atoms - ghost :]
    en_ref[i] = energy_rows(read_ref, feat)


def edge_back(k, edge_tile, sink, yb_ref, m_ref, dy_ref, dlen_ref, chans, atoms):
    for a0 in range(0, atoms, 128):
        y = [yb_ref[k, l, :, a0 : a0 + 128] for l in range(NL - 1)]
        y = [jnp.concatenate([v, v], axis=0) for v in y]
        acc = [jnp.zeros((8, 128), f32) for _ in range(NL)]
        for c0 in range(0, chans, 16):
            e = edge_tile(k, c0, a0)
            de = m_ref[0, c0 : c0 + 16, a0 : a0 + 128]
            for l in range(1, NL):
                dm = m_ref[l, c0 : c0 + 16, a0 : a0 + 128]
                de = de + dm * y[l - 1]
                p = e * dm
                acc[l] = acc[l] + (p[:8] + p[8:])
            p = sink(k, c0, a0, de)
            acc[0] = acc[0] + (p[:8] + p[8:])
        for l in range(1, NL):
            dy_ref[l - 1, k : k + 1, a0 : a0 + 128] = jnp.sum(acc[l], axis=0, keepdims=True)
        dlen_ref[k : k + 1, a0 : a0 + 128] = jnp.sum(acc[0], axis=0, keepdims=True)


@each_image
def radial_kernel(i, geo_ref, a_ref, b_ref, rad_ref, radl_ref):
    for k in range(rad_ref.shape[1]):
        basis, slope = basis_of(geo_ref[i, NL - 1, k : k + 1, :])
        row = geo_ref[i, NL, k : k + 1, :]
        hid, ds = silu_parts(dot(a_ref[...], pack_right(basis)))
        rad_ref[i, k] = dot(b_ref[...], pack_right(hid * row))
        dsl = ds * row * dot(a_ref[...], pack_right(slope))
        radl_ref[i, k] = dot(b_ref[...], pack_right(dsl))


@each_image
def second_kernel(
    i, head_ref, tail_ref, hlo_ref, hup_ref, idx_ref, geo_ref, rad_ref, radl_ref, mixt_ref,
    mix_ref, read_ref, dfh_ref, dft_ref, dlo_ref, dup_ref, dlen_ref, en_ref, q_ref, m_ref,
    yb_ref, hf_ref, oh_ref, dq_ref,
):
    slots, atoms = idx_ref.shape[1:]
    ghost = hlo_ref.shape[2]
    ch = hlo_ref.shape[1]
    extent = atoms + 2 * ghost
    for n, ref in enumerate((hlo_ref, head_ref, tail_ref, hup_ref)):
        hi, lo = split(ref[i])
        hf_ref[:ch, n * ghost : (n + 1) * ghost] = hi
        hf_ref[ch:, n * ghost : (n + 1) * ghost] = lo
    store_yb(yb_ref, [geo_ref[i, l] for l in range(NL - 1)], slots, atoms)
    for k in range(slots):
        oh = one_hot(idx_ref[i, k : k + 1, :], extent)
        oh_ref[:, k * atoms : (k + 1) * atoms] = oh
        got = dot(hf_ref[...], oh)
        q_ref[i, k] = got[:ch] + got[ch:]

    def edge_tile(k, c0, a0):
        cs = pl.ds(c0, 16)
        return rad_ref[i, k, cs, a0 : a0 + 128] * q_ref[i, k, cs, a0 : a0 + 128]

    m = m_ref.at[i]
    moments_into(edge_tile, yb_ref, m, ch, slots, atoms)
    inv = invariants_of(m)
    feat, dpre = silu_parts(dot(mixt_ref[...], pack_right(inv)))
    en_ref[i] = energy_rows(read_ref, feat)
    dinv = dot(mix_ref[...], pack_right(wide(read_ref, atoms) * dpre))
    moment_grads_into(m, dinv, ch)
    for k in range(slots):
        for a0 in range(0, atoms, 128):
            ls = slice(a0, a0 + 128)
            y = [yb_ref[k, l, :, ls] for l in range(NL - 1)]
            y = [jnp.concatenate([v, v], axis=0) for v in y]
            acc = jnp.zeros((8, 128), f32)
            ks = slice(k * atoms + a0, k * atoms + a0 + 128)
            for c0 in range(0, ch, 16):
                cs = slice(c0, c0 + 16)
                de = m[0, cs, ls]
                for l in range(1, NL):
                    de = de + m[l, cs, ls] * y[l - 1]
                hi, lo = split(de * rad_ref[i, k, cs, ls])
                dq_ref[cs, ks] = hi
                dq_ref[ch + c0 : ch + c0 + 16, ks] = lo
                p = de * q_ref[i, k, cs, ls] * radl_ref[i, k, cs, ls]
                acc = acc + (p[:8] + p[8:])
            dlen_ref[i, k : k + 1, ls] = jnp.sum(acc, axis=0, keepdims=True)
    back = dot_nt(dq_ref[...], oh_ref[...])
    back = back[:ch] + back[ch:]
    dlo_ref[i] = back[:, :ghost]
    dfh_ref[i] = back[:, ghost : 2 * ghost]
    dft_ref[i] = back[:, 2 * ghost : 3 * ghost]
    dup_ref[i] = back[:, 3 * ghost :]


@each_image
def angular_kernel(i, rad_ref, q_ref, m_ref, dy_ref):
    slots, ch, atoms = rad_ref.shape[1:]
    for k in range(slots):
        for a0 in range(0, atoms, 128):
            ls = slice(a0, a0 + 128)
            acc = [jnp.zeros((8, 128), f32) for _ in range(NL)]
            for c0 in range(0, ch, 16):
                cs = slice(c0, c0 + 16)
                e = rad_ref[i, k, cs, ls] * q_ref[i, k, cs, ls]
                for l in range(1, NL):
                    p = e * m_ref[i, l, cs, ls]
                    acc[l] = acc[l] + (p[:8] + p[8:])
            for l in range(1, NL):
                dy_ref[i, l - 1, k : k + 1, ls] = jnp.sum(acc[l], axis=0, keepdims=True)


@each_image
def third_kernel(
    i, dfh_ref, dft_ref, rlo_ref, rup_ref, idx_ref, geo_ref, hid_ref, dsl_ref, mom_ref, dpre_ref,
    dy2_ref, dlen2_ref, bt_ref, mix_ref, read_ref,
    own_ref, flo_ref, fup_ref,
    yb_ref, m_ref, dg_ref, dy_ref, dlen_ref, doff_ref,
):
    slots, atoms = idx_ref.shape[1:]
    ch, ghost = rlo_ref.shape[1:]
    rh = hid_ref.shape[2]
    extent = atoms + 2 * ghost
    store_yb(yb_ref, [geo_ref[i, l] for l in range(NL - 1)], slots, atoms)
    cot = jnp.concatenate([dfh_ref[i] + rlo_ref[i], dft_ref[i] + rup_ref[i]], axis=1)
    dpre = (cot + wide(read_ref, atoms)) * dpre_ref[i]
    dinv = dot(mix_ref[...], pack_right(dpre))
    for l in range(NL):
        m_ref[l] = mom_ref[i, l]
    moment_grads_into(m_ref, dinv, ch)
    for l in range(NL):
        dg_ref[l] = dot(bt_ref[...], pack_right(m_ref[l]))

    def edge_tile(k, c0, a0):
        return hid_ref[i, k, pl.ds(c0, 16), a0 : a0 + 128]

    def sink(k, c0, a0, de):
        return de * dsl_ref[i, k, c0 : c0 + 16, a0 : a0 + 128]

    for k in range(slots):
        edge_back(k, edge_tile, sink, yb_ref, dg_ref, dy_ref, dlen_ref, rh, atoms)
    dy = [None] + [dy_ref[l] + dy2_ref[i, l] for l in range(NL - 1)]
    ux, uy, uz = [geo_ref[i, n] for n in range(3)]
    length = geo_ref[i, NL - 1]
    dux = dy[1] + uy * dy[4] + uz * dy[6] + ux * dy[7]
    duy = dy[2] + ux * dy[4] + uz * dy[5] - uy * dy[7]
    duz = dy[3] + uy * dy[5] + ux * dy[6] + RT3 * uz * dy[8]
    radial = dlen_ref[...] + dlen2_ref[i] - (dux * ux + duy * uy + duz * uz) / length
    doff = [du / length + radial * u for du, u in ((dux, ux), (duy, uy), (duz, uz))]
    centre = jnp.concatenate([jnp.sum(d, axis=0, keepdims=True) for d in doff], axis=0)
    for x in range(3):
        doff_ref[x] = doff[x]
    back = jnp.zeros((16, extent), f32)
    pad = jnp.zeros((5, atoms), f32)
    for k in range(slots):
        rows = jnp.concatenate([doff_ref[x, k : k + 1, :] for x in range(3)] + [pad], axis=0)
        hi = rows.astype(bf16).astype(f32)
        both = jnp.concatenate([hi, rows - hi], axis=0).astype(bf16)
        back = back + dot_nt(both, one_hot(idx_ref[i, k : k + 1, :], extent))
    force = back[8:11] + back[:3]
    for n in range(own_ref.shape[1]):

        @pl.when(i == n)
        def _():
            own_ref[:, n, :] = centre - force[:, ghost : ghost + atoms]
            flo_ref[:, n, :] = -force[:, :ghost]
            fup_ref[:, n, :] = -force[:, ghost + atoms :]


def lane_row(values):
    lane = lax.broadcasted_iota(jnp.int32, (1, 128), 1)
    row = jnp.zeros((1, 128), f32)
    for n, v in enumerate(values):
        row = jnp.where(lane == n, v, row)
    return row


def total_of(x):
    return jnp.sum(jnp.sum(x, axis=1, keepdims=True), axis=0, keepdims=True)


def chain_of(pos_ref, before_ref, after_ref, start_ref, end_ref, chain):
    count = pos_ref.shape[1]
    me = lax.axis_index("image")
    before = jnp.where(me == 0, start_ref[...], before_ref[...])
    after = jnp.where(me == chain - 1, end_ref[...], after_ref[...])
    prev = [before] + [pos_ref[:, i, :] for i in range(count - 1)]
    nxt = [pos_ref[:, i, :] for i in range(1, count)] + [after]
    return prev, nxt


def partial_kernel(
    own_ref, rlo_ref, rup_ref, pos_ref, before_ref, after_ref, start_ref, end_ref,
    vel_ref, en1_ref, en2_ref, climb_ref, force_ref, send_ref, *, chain,
):
    count = pos_ref.shape[1]
    prev, nxt = chain_of(pos_ref, before_ref, after_ref, start_ref, end_ref, chain)
    values = []
    vel = jnp.zeros((1, 1), f32)
    for i in range(count):
        pos = pos_ref[:, i, :]
        force = own_ref[:, i, :] + jnp.concatenate([rlo_ref[:, i, :], rup_ref[:, i, :]], axis=1)
        force_ref[:, i, :] = force
        spread = nxt[i] - prev[i]
        ahead = nxt[i] - pos
        behind = pos - prev[i]
        values += [
            total_of(ahead * ahead),
            total_of(behind * behind),
            total_of(spread * spread),
            total_of(force * force),
            total_of(force * spread),
            total_of(en1_ref[i]) + total_of(en2_ref[i]),
        ]
        v = vel_ref[:, i, :]
        vel = vel + total_of(v * v)
    send_ref[...] = jnp.broadcast_to(lane_row(values + [vel, climb_ref[0].astype(f32)]), send_ref.shape)


def final_kernel(
    got_ref, force_ref, pos_ref, before_ref, after_ref, start_ref, end_ref,
    vel_ref, neb_ref, vnext_ref, pnext_ref, en_ref,
    *, chain, slabs,
):
    count = pos_ref.shape[1]
    atoms = pos_ref.shape[2]
    me = lax.axis_index("image")
    prev, nxt = chain_of(pos_ref, before_ref, after_ref, start_ref, end_ref, chain)
    rows = [
        jnp.sum(got_ref[g * slabs : (g + 1) * slabs, :], axis=0, keepdims=True)
        for g in range(chain)
    ]
    table = jnp.concatenate(rows, axis=0)
    climb = got_ref[0:1, 6 * count + 1 : 6 * count + 2]
    vel_sq = jnp.sum(table[:, 6 * count : 6 * count + 1], axis=0, keepdims=True)
    group = lax.broadcasted_iota(jnp.int32, (chain, 1), 0)
    force_sq = jnp.zeros((1, 1), f32)
    mine = []
    for i in range(count):
        ahead, behind, spread_sq, ff, fd, energy = [
            table[:, 6 * i + n : 6 * i + n + 1] for n in range(6)
        ]
        norm = 1.0 / jnp.sqrt(spread_sq + 1e-06)
        along = fd * norm
        climbing = jnp.where((group * count + i).astype(f32) == climb, 1.0, 0.0).astype(f32)
        spring = 5.0 * (jnp.sqrt(ahead) - jnp.sqrt(behind))
        coef = -(1.0 + climbing) * along + (1.0 - climbing) * spring
        scale = coef * norm
        part = ff + 2.0 * coef * along + scale * scale * spread_sq
        force_sq = force_sq + jnp.sum(part, axis=0, keepdims=True)
        here = group == me
        mine.append(jnp.sum(jnp.where(here, scale, 0.0), axis=0, keepdims=True))
        en_ref[i] = jnp.sum(jnp.where(here, energy, 0.0)) * (1.0 / (atoms * slabs))
    gain = 0.1 * jnp.sqrt(vel_sq / (force_sq + 1e-06))
    for i in range(count):
        neb = force_ref[:, i, :] + mine[i] * (nxt[i] - prev[i])
        neb_ref[:, i, :] = neb
        vnext = 0.9 * vel_ref[:, i, :] + gain * neb + 0.1 * neb
        vnext_ref[:, i, :] = vnext
        pnext_ref[:, i, :] = pos_ref[:, i, :] + 0.1 * vnext


def out(*shape):
    return jax.ShapeDtypeStruct(shape, f32)


def half(*shape):
    return jax.ShapeDtypeStruct(shape, bf16)


ANY = pl.BlockSpec(memory_space=pl.ANY)
VMEM = pl.BlockSpec(memory_space=pltpu.VMEM)
SMEM = pl.BlockSpec(memory_space=pltpu.SMEM)


def neighbours_of(cells, axis):
    count = lax.axis_size(axis)
    up = [(i, (i + 1) % count) for i in range(count)]
    down = [((i + 1) % count, i) for i in range(count)]
    to_below, to_above = cells
    return lax.ppermute(to_above, axis, up), lax.ppermute(to_below, axis, down)


def local(
    positions,
    velocity,
    start_state,
    end_state,
    neighbours,
    counts,
    climb_index,
    radial_a1,
    radial_b1,
    mix_first,
    read_first,
    radial_a2,
    radial_b2,
    mix_second,
    read_second,
):
    images, _, atoms = positions.shape
    slots = neighbours.shape[1]
    ghost = atoms // 2
    nb, rh = radial_a1.shape
    ch = radial_b1.shape[1]
    extent = atoms + 2 * ghost
    space = lax.axis_size("space")
    chain = lax.axis_size("image")
    params = pltpu.CompilerParams(vmem_limit_bytes=BIG_VMEM)
    small = pltpu.CompilerParams(vmem_limit_bytes=SMALL_VMEM)
    pos = positions.transpose(1, 0, 2)
    vel = velocity.transpose(1, 0, 2)

    plo, pup = neighbours_of((pos[:, :, :ghost], pos[:, :, ghost:]), "space")
    before = lax.ppermute(pos[:, images - 1], "image", [(i, i + 1) for i in range(chain - 1)])
    after = lax.ppermute(pos[:, 0], "image", [(i + 1, i) for i in range(chain - 1)])
    weights = (
        radial_a1, radial_b1, mix_first, read_first.reshape(1, ch),
        radial_a2, radial_b2, mix_second, read_second.reshape(1, ch),
    )
    idx, cnt, a1, b1, m1t, m1, b1t, r1, a2, b2, m2t, m2, r2 = pl.pallas_call(
        prep_kernel,
        in_specs=[pl.BlockSpec(memory_space=pltpu.HBM)] * 10,
        out_specs=[VMEM] * 13,
        out_shape=[
            jax.ShapeDtypeStruct(neighbours.shape, jnp.int32),
            jax.ShapeDtypeStruct(counts.shape, jnp.int32),
            half(rh, 3 * nb),
            half(ch, 3 * rh),
            half(ch, 9 * ch),
            half(3 * ch, 3 * ch),
            half(rh, 3 * ch),
            out(ch, 128),
            half(rh, 3 * nb),
            half(ch, 3 * rh),
            half(ch, 9 * ch),
            half(3 * ch, 3 * ch),
            out(ch, 128),
        ],
        scratch_shapes=[pltpu.VMEM(w.shape, f32) for w in weights]
        + [pltpu.SemaphoreType.DMA((10,))],
        compiler_params=small,
        cost_estimate=pl.CostEstimate(flops=4000000, bytes_accessed=4000000, transcendentals=0),
        name="prep",
    )(*[pltpu.with_memory_space_constraint(w, pltpu.HBM) for w in (neighbours, counts) + weights])
    geo_n = NL + 1

    head, tail, geo, hid, dsl, mom, dpre, en1 = pl.pallas_call(
        functools.partial(first_kernel, images=images),
        in_specs=[VMEM] * 3 + [ANY] * 2 + [VMEM] * 6,
        out_specs=[VMEM] * 8,
        out_shape=[
            out(images, ch, ghost),
            out(images, ch, ghost),
            out(images, geo_n, slots, atoms),
            out(images, slots, rh, atoms),
            out(images, slots, rh, atoms),
            out(images, NL, ch, atoms),
            out(images, ch, atoms),
            out(images, 8, 128),
        ],
        scratch_shapes=[
            pltpu.VMEM((slots, NL - 1, 8, atoms), f32),
            pltpu.VMEM((NL, rh, atoms), f32),
        ],
        compiler_params=params,
        name="first",
    )(pos, plo, pup, before, after, idx, cnt, a1, b1, m1t, r1)

    hlo, hup = neighbours_of((head, tail), "space")

    rad, radl = pl.pallas_call(
        functools.partial(radial_kernel, images=images),
        in_specs=[VMEM] * 3,
        out_specs=[VMEM] * 2,
        out_shape=[out(images, slots, ch, atoms)] * 2,
        compiler_params=small,
        cost_estimate=pl.CostEstimate(flops=1 << 30, bytes_accessed=1 << 23, transcendentals=1 << 20),
        name="radial",
    )(geo, a2, b2)
    dfh, dft, dlo, dup, dlen2, en2, q, dm = pl.pallas_call(
        functools.partial(second_kernel, images=images),
        in_specs=[VMEM] * 11,
        out_specs=[VMEM] * 8,
        out_shape=[out(images, ch, ghost)] * 4
        + [
            out(images, slots, atoms),
            out(images, 8, 128),
            out(images, slots, ch, atoms),
            out(images, NL, ch, atoms),
        ],
        scratch_shapes=[
            pltpu.VMEM((slots, NL - 1, 8, atoms), f32),
            pltpu.VMEM((2 * ch, extent), bf16),
            pltpu.VMEM((extent, slots * atoms), bf16),
            pltpu.VMEM((2 * ch, slots * atoms), bf16),
        ],
        compiler_params=params,
        name="second",
    )(head, tail, hlo, hup, idx, geo, rad, radl, m2t, m2, r2)

    rlo, rup = neighbours_of((dlo, dup), "space")
    dy2 = pl.pallas_call(
        functools.partial(angular_kernel, images=images),
        in_specs=[VMEM] * 3,
        out_specs=VMEM,
        out_shape=out(images, NL - 1, slots, atoms),
        compiler_params=small,
        cost_estimate=pl.CostEstimate(flops=1 << 30, bytes_accessed=1 << 23, transcendentals=0),
        name="angular",
    )(rad, q, dm)

    own, flo, fup = pl.pallas_call(
        functools.partial(third_kernel, images=images),
        in_specs=[VMEM] * 15,
        out_specs=[VMEM] * 3,
        out_shape=[out(3, images, atoms), out(3, images, ghost), out(3, images, ghost)],
        scratch_shapes=[
            pltpu.VMEM((slots, NL - 1, 8, atoms), f32),
            pltpu.VMEM((NL, ch, atoms), f32),
            pltpu.VMEM((NL, rh, atoms), f32),
            pltpu.VMEM((NL - 1, slots, atoms), f32),
            pltpu.VMEM((slots, atoms), f32),
            pltpu.VMEM((3, slots, atoms), f32),
        ],
        compiler_params=params,
        name="third",
    )(dfh, dft, rlo, rup, idx, geo, hid, dsl, mom, dpre, dy2, dlen2, b1t, m1, r1)

    glo, gup = neighbours_of((flo, fup), "space")

    rank = chain * space
    force, send = pl.pallas_call(
        functools.partial(partial_kernel, chain=chain),
        in_specs=[VMEM] * 11 + [SMEM],
        out_specs=[VMEM] * 2,
        out_shape=[out(3, images, atoms), out(rank, 128)],
        compiler_params=small,
        name="partial",
    )(own, glo, gup, pos, before, after, start_state, end_state, vel, en1, en2, climb_index)
    got = lax.all_to_all(
        send.reshape(rank, 1, 128), ("image", "space"), split_axis=0, concat_axis=0
    ).reshape(rank, 128)
    neb, vnext, pnext, energy = pl.pallas_call(
        functools.partial(final_kernel, chain=chain, slabs=space),
        in_specs=[VMEM] * 8,
        out_specs=[VMEM] * 3 + [SMEM],
        out_shape=[out(3, images, atoms)] * 3 + [out(images)],
        compiler_params=small,
        name="final",
    )(got, force, pos, before, after, start_state, end_state, vel)
    return (
        neb.transpose(1, 0, 2),
        vnext.transpose(1, 0, 2),
        pnext.transpose(1, 0, 2),
        energy,
    )


def solution(mesh):
    in_specs = (
        P("image", None, "space"),
        P("image", None, "space"),
        P(None, "space"),
        P(None, "space"),
        P("image", None, "space"),
        P("image", "space"),
        P(),
        P(),
        P(),
        P(),
        P(),
        P(),
        P(),
        P(),
        P(),
    )
    out_specs = (
        P("image", None, "space"),
        P("image", None, "space"),
        P("image", None, "space"),
        P("image"),
    )
    return jax.shard_map(local, mesh=mesh, in_specs=in_specs, out_specs=out_specs, check_vma=False)
```

```python
import functools
import math

import jax
import jax.numpy as jnp
from jax import lax
from jax.experimental import pallas as pl
from jax.experimental.pallas import tpu as pltpu
from jax.sharding import PartitionSpec as P

f32 = jnp.float32
bf16 = jnp.bfloat16
RT3 = math.sqrt(3.0)
NL = 9
GROUP_FIRST = 2
GROUP = 8
PULL = 4
BIG_VMEM = 16 << 20
SMALL_VMEM = 4 << 20


def split(x):
    hi = x.astype(bf16)
    lo = (x - hi.astype(f32)).astype(bf16)
    return hi, lo


def dot(a, b):
    return lax.dot_general(a, b, (((1,), (0,)), ((), ())), preferred_element_type=f32)


def dot_nt(a, b):
    return lax.dot_general(a, b, (((1,), (1,)), ((), ())), preferred_element_type=f32)


def pack_left(w):
    hi, lo = split(w)
    return jnp.concatenate([hi, hi, lo], axis=1)


def pack_right(x):
    hi, lo = split(x)
    return jnp.concatenate([hi, lo, hi], axis=0)


def one_hot(row, extent):
    step = 256
    wide = (step, row.shape[1])
    ids = lax.broadcasted_iota(jnp.int32, wide, 0).astype(f32).astype(bf16)
    zero, one = jnp.zeros(wide, bf16), jnp.ones(wide, bf16)
    parts = []
    for first in range(0, extent, step):
        here = jnp.broadcast_to((row - first).astype(f32), wide).astype(bf16)
        parts.append(jnp.where(ids == here, one, zero))
    return jnp.concatenate(parts, axis=0)


def lane_gather(row, idx):
    slots, atoms = idx.shape
    extent = row.shape[1]
    lane = idx & 127
    tile = idx >> 7
    blocks = [jnp.broadcast_to(row[:, t : t + 128], (8, 128)) for t in range(0, extent, 128)]
    out_rows = []
    for s0 in range(0, slots, 8):
        cells = []
        for a0 in range(0, atoms, 128):
            at = lane[s0 : s0 + 8, a0 : a0 + 128]
            which = tile[s0 : s0 + 8, a0 : a0 + 128]
            got = None
            for t, block in enumerate(blocks):
                v = jnp.take_along_axis(block, at, axis=1, mode="promise_in_bounds")
                got = v if got is None else jnp.where(which == t, v, got)
            cells.append(got)
        out_rows.append(jnp.concatenate(cells, axis=1))
    return jnp.concatenate(out_rows, axis=0)


def pick(block, i, axis):
    n = block.shape[axis]
    got = lax.index_in_dim(block, 0, axis, keepdims=False)
    for m in range(1, n):
        got = jnp.where(i == m, lax.index_in_dim(block, m, axis, keepdims=False), got)
    return got


def silu_parts(z):
    s = 0.5 + 0.5 * jnp.tanh(0.5 * z)
    h = z * s
    return h, s + h * (1.0 - s)


def basis_of(row):
    nb = 8
    centres = 0.5 * lax.broadcasted_iota(jnp.int32, (nb, row.shape[1]), 0).astype(f32)
    spread = row - centres
    basis = jnp.exp(-2.0 * spread * spread)
    return basis, -4.0 * spread * basis


def moments_into(edge_tile, yb_ref, m_ref, chans, slots, atoms):
    def tile(t, carry):
        c0 = pl.multiple_of(t * 16, 16)
        for a0 in range(0, atoms, 128):
            acc = [jnp.zeros((16, 128), f32) for _ in range(NL)]
            for k in range(slots):
                e = edge_tile(k, c0, a0)
                acc[0] = acc[0] + e
                for l in range(1, NL):
                    y = yb_ref[k, l - 1, :, a0 : a0 + 128]
                    acc[l] = acc[l] + e * jnp.concatenate([y, y], axis=0)
            for l in range(NL):
                m_ref[l, pl.ds(c0, 16), a0 : a0 + 128] = acc[l]
        return carry

    lax.fori_loop(0, chans // 16, tile, 0)


def store_yb(yb_ref, angular, slots, atoms):
    for k in range(slots):
        for l in range(NL - 1):
            yb_ref[k, l] = jnp.broadcast_to(angular[l][k : k + 1], (8, atoms))


def invariants_of(m_ref):
    m = [m_ref[l] for l in range(NL)]
    one = m[1] * m[1] + m[2] * m[2] + m[3] * m[3]
    two = m[4] * m[4] + m[5] * m[5] + m[6] * m[6] + m[7] * m[7] + m[8] * m[8]
    return jnp.concatenate([m[0], one, two], axis=0)


def moment_grads_into(m_ref, dinv, chans):
    m_ref[0] = dinv[:chans]
    d1 = 2.0 * dinv[chans : 2 * chans]
    d2 = 2.0 * dinv[2 * chans :]
    for l in range(1, NL):
        m_ref[l] = m_ref[l] * (d1 if l < 4 else d2)


def prep_kernel(*refs):
    n = 10
    hbm, outs, bufs, sems = refs[:n], refs[n : n + 13], refs[n + 13 : -1], refs[-1]
    (
        idx_out, cnt_out, a1_out, b1_out, m1t_out, m1_out, b1t_out, r1_out,
        a2_out, b2_out, m2t_out, m2_out, r2_out,
    ) = outs
    a1, b1, m1, r1, a2, b2, m2, r2 = bufs
    targets = (idx_out, cnt_out) + bufs
    copies = [pltpu.make_async_copy(h, t, sems.at[q]) for q, (h, t) in enumerate(zip(hbm, targets))]
    for c in copies:
        c.start()
    for c in copies:
        c.wait()
    a1_out[...] = pack_left(a1[...].T)
    b1_out[...] = pack_left(b1[...].T)
    m1t_out[...] = pack_left(m1[...].T)
    m1_out[...] = pack_left(m1[...])
    b1t_out[...] = pack_left(b1[...])
    r1_out[...] = jnp.broadcast_to(r1[...], r1_out.shape[::-1]).T
    a2_out[...] = pack_left(a2[...].T)
    b2_out[...] = pack_left(b2[...].T)
    m2t_out[...] = pack_left(m2[...].T)
    m2_out[...] = pack_left(m2[...])
    r2_out[...] = jnp.broadcast_to(r2[...], r2_out.shape[::-1]).T


def lanes(parts):
    return jnp.concatenate(parts, axis=1)


def hidden_of(a_ref, rows, lives):
    pairs = [basis_of(row) for row in rows]
    hid, ds = silu_parts(dot(a_ref[...], lanes([pack_right(p[0]) for p in pairs])))
    back = dot(a_ref[...], lanes([pack_right(p[1]) for p in pairs]))
    live = lanes(lives)
    return hid * live, ds * live * back


def energy_rows(read_ref, feat):
    ch, atoms = feat.shape
    read = read_ref[...]
    en = jnp.concatenate([read] * (atoms // 128), axis=1) * feat
    total = jnp.sum(en.reshape(ch // 8, 8, atoms), axis=0)
    return sum(total[:, a0 : a0 + 128] for a0 in range(0, atoms, 128))


def wide(read_ref, atoms):
    return jnp.concatenate([read_ref[...]] * (atoms // 128), axis=1)


def each_image(body):
    def kernel(*refs, images):
        def step(i, carry):
            body(i, *refs)
            return carry

        lax.fori_loop(0, images, step, 0)

    return kernel


@each_image
def first_kernel(
    i, pos_ref, plo_ref, pup_ref, before_ref, after_ref, idx_ref, cnt_ref, a_ref, b_ref, mixt_ref,
    read_ref, head_ref, tail_ref, geo_ref, hid_ref, dsl_ref, mom_ref, dpre_ref, en_ref,
    yb_ref, g_ref,
):
    slots, atoms = idx_ref.shape[1:]
    ghost = plo_ref.shape[2]
    idx = idx_ref[i]
    pos = pick(pos_ref[...], i, 1)
    plo = pick(plo_ref[...], i, 1)
    pup = pick(pup_ref[...], i, 1)
    ext = jnp.concatenate([plo, pos, pup], axis=1)
    off = [lane_gather(ext[x : x + 1], idx) - pos[x : x + 1] for x in range(3)]
    length = jnp.sqrt(off[0] * off[0] + off[1] * off[1] + off[2] * off[2] + 1.0)
    ux, uy, uz = [o / length for o in off]
    ids = lax.broadcasted_iota(jnp.int32, (slots, atoms), 0)
    cnt = pick(cnt_ref[...][None], i, 1)
    live = jnp.where(ids < cnt, 1.0 / slots, 0.0).astype(f32)
    angular = [
        ux,
        uy,
        uz,
        ux * uy,
        uy * uz,
        ux * uz,
        0.5 * (ux * ux - uy * uy),
        (3.0 * uz * uz - 1.0) / (2.0 * RT3),
    ]
    for l in range(NL - 1):
        geo_ref[i, l] = angular[l]
    geo_ref[i, NL - 1] = length
    geo_ref[i, NL] = live
    store_yb(yb_ref, angular, slots, atoms)
    for k0 in range(0, slots, GROUP_FIRST):
        ks = range(k0, k0 + GROUP_FIRST)
        hid, dsl = hidden_of(
            a_ref, [length[k : k + 1] for k in ks], [live[k : k + 1] for k in ks]
        )
        for k in ks:
            at = slice((k - k0) * atoms, (k - k0 + 1) * atoms)
            hid_ref[i, k] = hid[:, at]
            dsl_ref[i, k] = dsl[:, at]

    def hid_tile(k, c0, a0):
        return hid_ref[i, k, pl.ds(c0, 16), a0 : a0 + 128]

    moments_into(hid_tile, yb_ref, g_ref, hid_ref.shape[2], slots, atoms)
    for l in range(NL):
        mom_ref[i, l] = dot(b_ref[...], pack_right(g_ref[l]))
    inv = invariants_of(mom_ref.at[i])
    feat, dpre = silu_parts(dot(mixt_ref[...], pack_right(inv)))
    dpre_ref[i] = dpre
    head_ref[i] = feat[:, :ghost]
    tail_ref[i] = feat[:, atoms - ghost :]
    en_ref[i] = energy_rows(read_ref, feat)


def edge_back(k, edge_tile, sink, yb_ref, m_ref, dy_ref, dlen_ref, chans, atoms):
    for a0 in range(0, atoms, 128):
        y = [yb_ref[k, l, :, a0 : a0 + 128] for l in range(NL - 1)]
        y = [jnp.concatenate([v, v], axis=0) for v in y]
        acc = [jnp.zeros((8, 128), f32) for _ in range(NL)]
        for c0 in range(0, chans, 16):
            e = edge_tile(k, c0, a0)
            de = m_ref[0, c0 : c0 + 16, a0 : a0 + 128]
            for l in range(1, NL):
                dm = m_ref[l, c0 : c0 + 16, a0 : a0 + 128]
                de = de + dm * y[l - 1]
                p = e * dm
                acc[l] = acc[l] + (p[:8] + p[8:])
            p = sink(k, c0, a0, de)
            acc[0] = acc[0] + (p[:8] + p[8:])
        for l in range(1, NL):
            dy_ref[l - 1, k : k + 1, a0 : a0 + 128] = jnp.sum(acc[l], axis=0, keepdims=True)
        dlen_ref[k : k + 1, a0 : a0 + 128] = jnp.sum(acc[0], axis=0, keepdims=True)


@each_image
def radial_kernel(i, geo_ref, a_ref, b_ref, rad_ref, radl_ref):
    slots, _, atoms = rad_ref.shape[1:]
    for k0 in range(0, slots, GROUP):
        ks = range(k0, k0 + GROUP)
        hid, dsl = hidden_of(
            a_ref,
            [geo_ref[i, NL - 1, k : k + 1, :] for k in ks],
            [geo_ref[i, NL, k : k + 1, :] for k in ks],
        )
        rad = dot(b_ref[...], pack_right(hid))
        radl = dot(b_ref[...], pack_right(dsl))
        for k in ks:
            at = slice((k - k0) * atoms, (k - k0 + 1) * atoms)
            rad_ref[i, k] = rad[:, at]
            radl_ref[i, k] = radl[:, at]


@each_image
def second_kernel(
    i, head_ref, tail_ref, hlo_ref, hup_ref, idx_ref, geo_ref, rad_ref, radl_ref, mixt_ref,
    mix_ref, read_ref, dfh_ref, dft_ref, dlo_ref, dup_ref, dlen_ref, en_ref, q_ref, m_ref,
    yb_ref, hf_ref, oh_ref, dq_ref,
):
    slots, atoms = idx_ref.shape[1:]
    ghost = hlo_ref.shape[2]
    ch = hlo_ref.shape[1]
    extent = atoms + 2 * ghost
    for n, ref in enumerate((hlo_ref, head_ref, tail_ref, hup_ref)):
        hi, lo = split(ref[i])
        hf_ref[:ch, n * ghost : (n + 1) * ghost] = hi
        hf_ref[ch:, n * ghost : (n + 1) * ghost] = lo
    store_yb(yb_ref, [geo_ref[i, l] for l in range(NL - 1)], slots, atoms)
    for k0 in range(0, slots, PULL):
        at = slice(k0 * atoms, (k0 + PULL) * atoms)
        for k in range(k0, k0 + PULL):
            oh_ref[:, k * atoms : (k + 1) * atoms] = one_hot(idx_ref[i, k : k + 1, :], extent)
        got = dot(hf_ref[...], oh_ref[:, at])
        got = got[:ch] + got[ch:]
        for k in range(k0, k0 + PULL):
            q_ref[i, k] = got[:, (k - k0) * atoms : (k - k0 + 1) * atoms]

    def edge_tile(k, c0, a0):
        cs = pl.ds(c0, 16)
        return rad_ref[i, k, cs, a0 : a0 + 128] * q_ref[i, k, cs, a0 : a0 + 128]

    m = m_ref.at[i]
    moments_into(edge_tile, yb_ref, m, ch, slots, atoms)
    inv = invariants_of(m)
    feat, dpre = silu_parts(dot(mixt_ref[...], pack_right(inv)))
    en_ref[i] = energy_rows(read_ref, feat)
    dinv = dot(mix_ref[...], pack_right(wide(read_ref, atoms) * dpre))
    moment_grads_into(m, dinv, ch)
    for k in range(slots):
        for a0 in range(0, atoms, 128):
            ls = slice(a0, a0 + 128)
            y = [yb_ref[k, l, :, ls] for l in range(NL - 1)]
            y = [jnp.concatenate([v, v], axis=0) for v in y]
            acc = jnp.zeros((8, 128), f32)
            ks = slice(k * atoms + a0, k * atoms + a0 + 128)
            for c0 in range(0, ch, 16):
                cs = slice(c0, c0 + 16)
                de = m[0, cs, ls]
                for l in range(1, NL):
                    de = de + m[l, cs, ls] * y[l - 1]
                hi, lo = split(de * rad_ref[i, k, cs, ls])
                dq_ref[cs, ks] = hi
                dq_ref[ch + c0 : ch + c0 + 16, ks] = lo
                p = de * q_ref[i, k, cs, ls] * radl_ref[i, k, cs, ls]
                acc = acc + (p[:8] + p[8:])
            dlen_ref[i, k : k + 1, ls] = jnp.sum(acc, axis=0, keepdims=True)
    back = dot_nt(dq_ref[...], oh_ref[...])
    back = back[:ch] + back[ch:]
    dlo_ref[i] = back[:, :ghost]
    dfh_ref[i] = back[:, ghost : 2 * ghost]
    dft_ref[i] = back[:, 2 * ghost : 3 * ghost]
    dup_ref[i] = back[:, 3 * ghost :]


@each_image
def angular_kernel(i, rad_ref, q_ref, m_ref, dy_ref):
    slots, ch, atoms = rad_ref.shape[1:]
    for k in range(slots):
        for a0 in range(0, atoms, 128):
            ls = slice(a0, a0 + 128)
            acc = [jnp.zeros((8, 128), f32) for _ in range(NL)]
            for c0 in range(0, ch, 16):
                cs = slice(c0, c0 + 16)
                e = rad_ref[i, k, cs, ls] * q_ref[i, k, cs, ls]
                for l in range(1, NL):
                    p = e * m_ref[i, l, cs, ls]
                    acc[l] = acc[l] + (p[:8] + p[8:])
            for l in range(1, NL):
                dy_ref[i, l - 1, k : k + 1, ls] = jnp.sum(acc[l], axis=0, keepdims=True)


@each_image
def third_kernel(
    i, dfh_ref, dft_ref, rlo_ref, rup_ref, idx_ref, geo_ref, hid_ref, dsl_ref, mom_ref, dpre_ref,
    dy2_ref, dlen2_ref, bt_ref, mix_ref, read_ref,
    own_ref, flo_ref, fup_ref,
    yb_ref, m_ref, dg_ref, dy_ref, dlen_ref, doff_ref,
):
    slots, atoms = idx_ref.shape[1:]
    ch, ghost = rlo_ref.shape[1:]
    rh = hid_ref.shape[2]
    extent = atoms + 2 * ghost
    store_yb(yb_ref, [geo_ref[i, l] for l in range(NL - 1)], slots, atoms)
    cot = jnp.concatenate([dfh_ref[i] + rlo_ref[i], dft_ref[i] + rup_ref[i]], axis=1)
    dpre = (cot + wide(read_ref, atoms)) * dpre_ref[i]
    dinv = dot(mix_ref[...], pack_right(dpre))
    for l in range(NL):
        m_ref[l] = mom_ref[i, l]
    moment_grads_into(m_ref, dinv, ch)
    for l in range(NL):
        dg_ref[l] = dot(bt_ref[...], pack_right(m_ref[l]))

    def edge_tile(k, c0, a0):
        return hid_ref[i, k, pl.ds(c0, 16), a0 : a0 + 128]

    def sink(k, c0, a0, de):
        return de * dsl_ref[i, k, c0 : c0 + 16, a0 : a0 + 128]

    for k in range(slots):
        edge_back(k, edge_tile, sink, yb_ref, dg_ref, dy_ref, dlen_ref, rh, atoms)
    dy = [None] + [dy_ref[l] + dy2_ref[i, l] for l in range(NL - 1)]
    ux, uy, uz = [geo_ref[i, n] for n in range(3)]
    length = geo_ref[i, NL - 1]
    dux = dy[1] + uy * dy[4] + uz * dy[6] + ux * dy[7]
    duy = dy[2] + ux * dy[4] + uz * dy[5] - uy * dy[7]
    duz = dy[3] + uy * dy[5] + ux * dy[6] + RT3 * uz * dy[8]
    radial = dlen_ref[...] + dlen2_ref[i] - (dux * ux + duy * uy + duz * uz) / length
    doff = [du / length + radial * u for du, u in ((dux, ux), (duy, uy), (duz, uz))]
    centre = jnp.concatenate([jnp.sum(d, axis=0, keepdims=True) for d in doff], axis=0)
    for x in range(3):
        doff_ref[x] = doff[x]
    back = jnp.zeros((16, extent), f32)
    pad = jnp.zeros((5, atoms), f32)
    for k in range(slots):
        rows = jnp.concatenate([doff_ref[x, k : k + 1, :] for x in range(3)] + [pad], axis=0)
        hi = rows.astype(bf16).astype(f32)
        both = jnp.concatenate([hi, rows - hi], axis=0).astype(bf16)
        back = back + dot_nt(both, one_hot(idx_ref[i, k : k + 1, :], extent))
    force = back[8:11] + back[:3]
    for n in range(own_ref.shape[1]):

        @pl.when(i == n)
        def _():
            own_ref[:, n, :] = centre - force[:, ghost : ghost + atoms]
            flo_ref[:, n, :] = -force[:, :ghost]
            fup_ref[:, n, :] = -force[:, ghost + atoms :]


def lane_row(values):
    lane = lax.broadcasted_iota(jnp.int32, (1, 128), 1)
    row = jnp.zeros((1, 128), f32)
    for n, v in enumerate(values):
        row = jnp.where(lane == n, v, row)
    return row


def total_of(x):
    return jnp.sum(jnp.sum(x, axis=1, keepdims=True), axis=0, keepdims=True)


def chain_of(pos_ref, before_ref, after_ref, start_ref, end_ref, chain):
    count = pos_ref.shape[1]
    me = lax.axis_index("image")
    before = jnp.where(me == 0, start_ref[...], before_ref[...])
    after = jnp.where(me == chain - 1, end_ref[...], after_ref[...])
    prev = [before] + [pos_ref[:, i, :] for i in range(count - 1)]
    nxt = [pos_ref[:, i, :] for i in range(1, count)] + [after]
    return prev, nxt


def partial_kernel(
    own_ref, rlo_ref, rup_ref, pos_ref, before_ref, after_ref, start_ref, end_ref,
    vel_ref, en1_ref, en2_ref, climb_ref, force_ref, send_ref, *, chain,
):
    count = pos_ref.shape[1]
    prev, nxt = chain_of(pos_ref, before_ref, after_ref, start_ref, end_ref, chain)
    values = []
    vel = jnp.zeros((1, 1), f32)
    for i in range(count):
        pos = pos_ref[:, i, :]
        force = own_ref[:, i, :] + jnp.concatenate([rlo_ref[:, i, :], rup_ref[:, i, :]], axis=1)
        force_ref[:, i, :] = force
        spread = nxt[i] - prev[i]
        ahead = nxt[i] - pos
        behind = pos - prev[i]
        values += [
            total_of(ahead * ahead),
            total_of(behind * behind),
            total_of(spread * spread),
            total_of(force * force),
            total_of(force * spread),
            total_of(en1_ref[i]) + total_of(en2_ref[i]),
        ]
        v = vel_ref[:, i, :]
        vel = vel + total_of(v * v)
    send_ref[...] = jnp.broadcast_to(lane_row(values + [vel, climb_ref[0].astype(f32)]), send_ref.shape)


def final_kernel(
    got_ref, force_ref, pos_ref, before_ref, after_ref, start_ref, end_ref,
    vel_ref, neb_ref, vnext_ref, pnext_ref, en_ref,
    *, chain, slabs,
):
    count = pos_ref.shape[1]
    atoms = pos_ref.shape[2]
    me = lax.axis_index("image")
    prev, nxt = chain_of(pos_ref, before_ref, after_ref, start_ref, end_ref, chain)
    rows = [
        jnp.sum(got_ref[g * slabs : (g + 1) * slabs, :], axis=0, keepdims=True)
        for g in range(chain)
    ]
    table = jnp.concatenate(rows, axis=0)
    climb = got_ref[0:1, 6 * count + 1 : 6 * count + 2]
    vel_sq = jnp.sum(table[:, 6 * count : 6 * count + 1], axis=0, keepdims=True)
    group = lax.broadcasted_iota(jnp.int32, (chain, 1), 0)
    force_sq = jnp.zeros((1, 1), f32)
    mine = []
    for i in range(count):
        ahead, behind, spread_sq, ff, fd, energy = [
            table[:, 6 * i + n : 6 * i + n + 1] for n in range(6)
        ]
        norm = 1.0 / jnp.sqrt(spread_sq + 1e-06)
        along = fd * norm
        climbing = jnp.where((group * count + i).astype(f32) == climb, 1.0, 0.0).astype(f32)
        spring = 5.0 * (jnp.sqrt(ahead) - jnp.sqrt(behind))
        coef = -(1.0 + climbing) * along + (1.0 - climbing) * spring
        scale = coef * norm
        part = ff + 2.0 * coef * along + scale * scale * spread_sq
        force_sq = force_sq + jnp.sum(part, axis=0, keepdims=True)
        here = group == me
        mine.append(jnp.sum(jnp.where(here, scale, 0.0), axis=0, keepdims=True))
        en_ref[i] = jnp.sum(jnp.where(here, energy, 0.0)) * (1.0 / (atoms * slabs))
    gain = 0.1 * jnp.sqrt(vel_sq / (force_sq + 1e-06))
    for i in range(count):
        neb = force_ref[:, i, :] + mine[i] * (nxt[i] - prev[i])
        neb_ref[:, i, :] = neb
        vnext = 0.9 * vel_ref[:, i, :] + gain * neb + 0.1 * neb
        vnext_ref[:, i, :] = vnext
        pnext_ref[:, i, :] = pos_ref[:, i, :] + 0.1 * vnext


def out(*shape):
    return jax.ShapeDtypeStruct(shape, f32)


def half(*shape):
    return jax.ShapeDtypeStruct(shape, bf16)


ANY = pl.BlockSpec(memory_space=pl.ANY)
VMEM = pl.BlockSpec(memory_space=pltpu.VMEM)
SMEM = pl.BlockSpec(memory_space=pltpu.SMEM)


def neighbours_of(cells, axis):
    count = lax.axis_size(axis)
    up = [(i, (i + 1) % count) for i in range(count)]
    down = [((i + 1) % count, i) for i in range(count)]
    to_below, to_above = cells
    return lax.ppermute(to_above, axis, up), lax.ppermute(to_below, axis, down)


def local(
    positions,
    velocity,
    start_state,
    end_state,
    neighbours,
    counts,
    climb_index,
    radial_a1,
    radial_b1,
    mix_first,
    read_first,
    radial_a2,
    radial_b2,
    mix_second,
    read_second,
):
    images, _, atoms = positions.shape
    slots = neighbours.shape[1]
    ghost = atoms // 2
    nb, rh = radial_a1.shape
    ch = radial_b1.shape[1]
    extent = atoms + 2 * ghost
    space = lax.axis_size("space")
    chain = lax.axis_size("image")
    params = pltpu.CompilerParams(vmem_limit_bytes=BIG_VMEM)
    small = pltpu.CompilerParams(vmem_limit_bytes=SMALL_VMEM)
    pos = positions.transpose(1, 0, 2)
    vel = velocity.transpose(1, 0, 2)

    plo, pup = neighbours_of((pos[:, :, :ghost], pos[:, :, ghost:]), "space")
    before = lax.ppermute(pos[:, images - 1], "image", [(i, i + 1) for i in range(chain - 1)])
    after = lax.ppermute(pos[:, 0], "image", [(i + 1, i) for i in range(chain - 1)])
    weights = (
        radial_a1, radial_b1, mix_first, read_first.reshape(1, ch),
        radial_a2, radial_b2, mix_second, read_second.reshape(1, ch),
    )
    idx, cnt, a1, b1, m1t, m1, b1t, r1, a2, b2, m2t, m2, r2 = pl.pallas_call(
        prep_kernel,
        in_specs=[pl.BlockSpec(memory_space=pltpu.HBM)] * 10,
        out_specs=[VMEM] * 13,
        out_shape=[
            jax.ShapeDtypeStruct(neighbours.shape, jnp.int32),
            jax.ShapeDtypeStruct(counts.shape, jnp.int32),
            half(rh, 3 * nb),
            half(ch, 3 * rh),
            half(ch, 9 * ch),
            half(3 * ch, 3 * ch),
            half(rh, 3 * ch),
            out(ch, 128),
            half(rh, 3 * nb),
            half(ch, 3 * rh),
            half(ch, 9 * ch),
            half(3 * ch, 3 * ch),
            out(ch, 128),
        ],
        scratch_shapes=[pltpu.VMEM(w.shape, f32) for w in weights]
        + [pltpu.SemaphoreType.DMA((10,))],
        compiler_params=small,
        cost_estimate=pl.CostEstimate(flops=4000000, bytes_accessed=4000000, transcendentals=0),
        name="prep",
    )(*[pltpu.with_memory_space_constraint(w, pltpu.HBM) for w in (neighbours, counts) + weights])
    geo_n = NL + 1

    head, tail, geo, hid, dsl, mom, dpre, en1 = pl.pallas_call(
        functools.partial(first_kernel, images=images),
        in_specs=[VMEM] * 3 + [ANY] * 2 + [VMEM] * 6,
        out_specs=[VMEM] * 8,
        out_shape=[
            out(images, ch, ghost),
            out(images, ch, ghost),
            out(images, geo_n, slots, atoms),
            out(images, slots, rh, atoms),
            out(images, slots, rh, atoms),
            out(images, NL, ch, atoms),
            out(images, ch, atoms),
            out(images, 8, 128),
        ],
        scratch_shapes=[
            pltpu.VMEM((slots, NL - 1, 8, atoms), f32),
            pltpu.VMEM((NL, rh, atoms), f32),
        ],
        compiler_params=params,
        name="first",
    )(pos, plo, pup, before, after, idx, cnt, a1, b1, m1t, r1)

    hlo, hup = neighbours_of((head, tail), "space")

    rad, radl = pl.pallas_call(
        functools.partial(radial_kernel, images=images),
        in_specs=[VMEM] * 3,
        out_specs=[VMEM] * 2,
        out_shape=[out(images, slots, ch, atoms)] * 2,
        compiler_params=small,
        cost_estimate=pl.CostEstimate(flops=1 << 30, bytes_accessed=1 << 23, transcendentals=1 << 20),
        name="radial",
    )(geo, a2, b2)
    dfh, dft, dlo, dup, dlen2, en2, q, dm = pl.pallas_call(
        functools.partial(second_kernel, images=images),
        in_specs=[VMEM] * 11,
        out_specs=[VMEM] * 8,
        out_shape=[out(images, ch, ghost)] * 4
        + [
            out(images, slots, atoms),
            out(images, 8, 128),
            out(images, slots, ch, atoms),
            out(images, NL, ch, atoms),
        ],
        scratch_shapes=[
            pltpu.VMEM((slots, NL - 1, 8, atoms), f32),
            pltpu.VMEM((2 * ch, extent), bf16),
            pltpu.VMEM((extent, slots * atoms), bf16),
            pltpu.VMEM((2 * ch, slots * atoms), bf16),
        ],
        compiler_params=params,
        name="second",
    )(head, tail, hlo, hup, idx, geo, rad, radl, m2t, m2, r2)

    rlo, rup = neighbours_of((dlo, dup), "space")
    dy2 = pl.pallas_call(
        functools.partial(angular_kernel, images=images),
        in_specs=[VMEM] * 3,
        out_specs=VMEM,
        out_shape=out(images, NL - 1, slots, atoms),
        compiler_params=small,
        cost_estimate=pl.CostEstimate(flops=1 << 30, bytes_accessed=1 << 23, transcendentals=0),
        name="angular",
    )(rad, q, dm)

    own, flo, fup = pl.pallas_call(
        functools.partial(third_kernel, images=images),
        in_specs=[VMEM] * 15,
        out_specs=[VMEM] * 3,
        out_shape=[out(3, images, atoms), out(3, images, ghost), out(3, images, ghost)],
        scratch_shapes=[
            pltpu.VMEM((slots, NL - 1, 8, atoms), f32),
            pltpu.VMEM((NL, ch, atoms), f32),
            pltpu.VMEM((NL, rh, atoms), f32),
            pltpu.VMEM((NL - 1, slots, atoms), f32),
            pltpu.VMEM((slots, atoms), f32),
            pltpu.VMEM((3, slots, atoms), f32),
        ],
        compiler_params=params,
        name="third",
    )(dfh, dft, rlo, rup, idx, geo, hid, dsl, mom, dpre, dy2, dlen2, b1t, m1, r1)

    glo, gup = neighbours_of((flo, fup), "space")

    rank = chain * space
    force, send = pl.pallas_call(
        functools.partial(partial_kernel, chain=chain),
        in_specs=[VMEM] * 11 + [SMEM],
        out_specs=[VMEM] * 2,
        out_shape=[out(3, images, atoms), out(rank, 128)],
        compiler_params=small,
        name="partial",
    )(own, glo, gup, pos, before, after, start_state, end_state, vel, en1, en2, climb_index)
    got = lax.all_to_all(
        send.reshape(rank, 1, 128), ("image", "space"), split_axis=0, concat_axis=0
    ).reshape(rank, 128)
    neb, vnext, pnext, energy = pl.pallas_call(
        functools.partial(final_kernel, chain=chain, slabs=space),
        in_specs=[VMEM] * 8,
        out_specs=[VMEM] * 3 + [SMEM],
        out_shape=[out(3, images, atoms)] * 3 + [out(images)],
        compiler_params=small,
        name="final",
    )(got, force, pos, before, after, start_state, end_state, vel)
    return (
        neb.transpose(1, 0, 2),
        vnext.transpose(1, 0, 2),
        pnext.transpose(1, 0, 2),
        energy,
    )


def solution(mesh):
    in_specs = (
        P("image", None, "space"),
        P("image", None, "space"),
        P(None, "space"),
        P(None, "space"),
        P("image", None, "space"),
        P("image", "space"),
        P(),
        P(),
        P(),
        P(),
        P(),
        P(),
        P(),
        P(),
        P(),
    )
    out_specs = (
        P("image", None, "space"),
        P("image", None, "space"),
        P("image", None, "space"),
        P("image"),
    )
    return jax.shard_map(local, mesh=mesh, in_specs=in_specs, out_specs=out_specs, check_vma=False)
```

```python
import functools
import math

import jax
import jax.numpy as jnp
from jax import lax
from jax.experimental import pallas as pl
from jax.experimental.pallas import tpu as pltpu
from jax.sharding import PartitionSpec as P

f32 = jnp.float32
bf16 = jnp.bfloat16
RT3 = math.sqrt(3.0)
NL = 9
GROUP_FIRST = 2
GROUP = 8
PULL = 4
BIG_VMEM = 16 << 20
SMALL_VMEM = 4 << 20


def split(x):
    hi = x.astype(bf16)
    lo = (x - hi.astype(f32)).astype(bf16)
    return hi, lo


def dot(a, b):
    return lax.dot_general(a, b, (((1,), (0,)), ((), ())), preferred_element_type=f32)


def dot_nt(a, b):
    return lax.dot_general(a, b, (((1,), (1,)), ((), ())), preferred_element_type=f32)


def pack_left(w):
    hi, lo = split(w)
    return jnp.concatenate([hi, hi, lo], axis=1)


def pack_right(x):
    hi, lo = split(x)
    return jnp.concatenate([hi, lo, hi], axis=0)


def one_hot(row, extent):
    step = 256
    wide = (step, row.shape[1])
    ids = lax.broadcasted_iota(jnp.int32, wide, 0).astype(f32).astype(bf16)
    zero, one = jnp.zeros(wide, bf16), jnp.ones(wide, bf16)
    parts = []
    for first in range(0, extent, step):
        here = jnp.broadcast_to((row - first).astype(f32), wide).astype(bf16)
        parts.append(jnp.where(ids == here, one, zero))
    return jnp.concatenate(parts, axis=0)


def lane_gather(row, idx):
    slots, atoms = idx.shape
    extent = row.shape[1]
    lane = idx & 127
    tile = idx >> 7
    blocks = [jnp.broadcast_to(row[:, t : t + 128], (8, 128)) for t in range(0, extent, 128)]
    out_rows = []
    for s0 in range(0, slots, 8):
        cells = []
        for a0 in range(0, atoms, 128):
            at = lane[s0 : s0 + 8, a0 : a0 + 128]
            which = tile[s0 : s0 + 8, a0 : a0 + 128]
            got = None
            for t, block in enumerate(blocks):
                v = jnp.take_along_axis(block, at, axis=1, mode="promise_in_bounds")
                got = v if got is None else jnp.where(which == t, v, got)
            cells.append(got)
        out_rows.append(jnp.concatenate(cells, axis=1))
    return jnp.concatenate(out_rows, axis=0)


def pick(block, i, axis):
    n = block.shape[axis]
    got = lax.index_in_dim(block, 0, axis, keepdims=False)
    for m in range(1, n):
        got = jnp.where(i == m, lax.index_in_dim(block, m, axis, keepdims=False), got)
    return got


def silu_parts(z):
    s = 0.5 + 0.5 * jnp.tanh(0.5 * z)
    h = z * s
    return h, s + h * (1.0 - s)


def basis_of(row):
    nb = 8
    centres = 0.5 * lax.broadcasted_iota(jnp.int32, (nb, row.shape[1]), 0).astype(f32)
    spread = row - centres
    basis = jnp.exp(-2.0 * spread * spread)
    return basis, -4.0 * spread * basis


def moments_into(edge_tile, yb_ref, m_ref, chans, slots, atoms):
    def tile(t, carry):
        c0 = pl.multiple_of(t * 16, 16)
        for a0 in range(0, atoms, 128):
            acc = [jnp.zeros((16, 128), f32) for _ in range(NL)]
            for k in range(slots):
                e = edge_tile(k, c0, a0)
                acc[0] = acc[0] + e
                for l in range(1, NL):
                    y = yb_ref[k, l - 1, :, a0 : a0 + 128]
                    acc[l] = acc[l] + e * jnp.concatenate([y, y], axis=0)
            for l in range(NL):
                m_ref[l, pl.ds(c0, 16), a0 : a0 + 128] = acc[l]
        return carry

    lax.fori_loop(0, chans // 16, tile, 0)


def store_yb(yb_ref, angular, slots, atoms):
    for k in range(slots):
        for l in range(NL - 1):
            yb_ref[k, l] = jnp.broadcast_to(angular[l][k : k + 1], (8, atoms))


def invariants_of(m_ref):
    m = [m_ref[l] for l in range(NL)]
    one = m[1] * m[1] + m[2] * m[2] + m[3] * m[3]
    two = m[4] * m[4] + m[5] * m[5] + m[6] * m[6] + m[7] * m[7] + m[8] * m[8]
    return jnp.concatenate([m[0], one, two], axis=0)


def moment_grads_into(m_ref, dinv, chans):
    m_ref[0] = dinv[:chans]
    d1 = 2.0 * dinv[chans : 2 * chans]
    d2 = 2.0 * dinv[2 * chans :]
    for l in range(1, NL):
        m_ref[l] = m_ref[l] * (d1 if l < 4 else d2)


def prep_kernel(*refs):
    n = 10
    hbm, outs, bufs, sems = refs[:n], refs[n : n + 13], refs[n + 13 : -1], refs[-1]
    (
        idx_out, cnt_out, a1_out, b1_out, m1t_out, m1_out, b1t_out, r1_out,
        a2_out, b2_out, m2t_out, m2_out, r2_out,
    ) = outs
    a1, b1, m1, r1, a2, b2, m2, r2 = bufs
    targets = (idx_out, cnt_out) + bufs
    copies = [pltpu.make_async_copy(h, t, sems.at[q]) for q, (h, t) in enumerate(zip(hbm, targets))]
    for c in copies:
        c.start()
    for c in copies:
        c.wait()
    a1_out[...] = pack_left(a1[...].T)
    b1_out[...] = pack_left(b1[...].T)
    m1t_out[...] = pack_left(m1[...].T)
    m1_out[...] = pack_left(m1[...])
    b1t_out[...] = pack_left(b1[...])
    r1_out[...] = jnp.broadcast_to(r1[...], r1_out.shape[::-1]).T
    a2_out[...] = pack_left(a2[...].T)
    b2_out[...] = pack_left(b2[...].T)
    m2t_out[...] = pack_left(m2[...].T)
    m2_out[...] = pack_left(m2[...])
    r2_out[...] = jnp.broadcast_to(r2[...], r2_out.shape[::-1]).T


def lanes(parts):
    return jnp.concatenate(parts, axis=1)


def hidden_of(a_ref, rows, lives):
    pairs = [basis_of(row) for row in rows]
    hid, ds = silu_parts(dot(a_ref[...], lanes([pack_right(p[0]) for p in pairs])))
    back = dot(a_ref[...], lanes([pack_right(p[1]) for p in pairs]))
    live = lanes(lives)
    return hid * live, ds * live * back


def energy_rows(read_ref, feat):
    ch, atoms = feat.shape
    read = read_ref[...]
    en = jnp.concatenate([read] * (atoms // 128), axis=1) * feat
    total = jnp.sum(en.reshape(ch // 8, 8, atoms), axis=0)
    return sum(total[:, a0 : a0 + 128] for a0 in range(0, atoms, 128))


def wide(read_ref, atoms):
    return jnp.concatenate([read_ref[...]] * (atoms // 128), axis=1)


def each_image(body):
    def kernel(*refs, images):
        def step(i, carry):
            body(i, *refs)
            return carry

        lax.fori_loop(0, images, step, 0)

    return kernel


@each_image
def first_kernel(
    i, pos_ref, plo_ref, pup_ref, before_ref, after_ref, idx_ref, cnt_ref, a_ref, b_ref, mixt_ref,
    read_ref, head_ref, tail_ref, geo_ref, hid_ref, dsl_ref, mom_ref, dpre_ref, en_ref, ybs_ref,
    g_ref,
):
    slots, atoms = idx_ref.shape[1:]
    yb_ref = ybs_ref.at[i]
    ghost = plo_ref.shape[2]
    idx = idx_ref[i]
    pos = pick(pos_ref[...], i, 1)
    plo = pick(plo_ref[...], i, 1)
    pup = pick(pup_ref[...], i, 1)
    ext = jnp.concatenate([plo, pos, pup], axis=1)
    off = [lane_gather(ext[x : x + 1], idx) - pos[x : x + 1] for x in range(3)]
    length = jnp.sqrt(off[0] * off[0] + off[1] * off[1] + off[2] * off[2] + 1.0)
    ux, uy, uz = [o / length for o in off]
    ids = lax.broadcasted_iota(jnp.int32, (slots, atoms), 0)
    cnt = pick(cnt_ref[...][None], i, 1)
    live = jnp.where(ids < cnt, 1.0 / slots, 0.0).astype(f32)
    angular = [
        ux,
        uy,
        uz,
        ux * uy,
        uy * uz,
        ux * uz,
        0.5 * (ux * ux - uy * uy),
        (3.0 * uz * uz - 1.0) / (2.0 * RT3),
    ]
    for l in range(NL - 1):
        geo_ref[i, l] = angular[l]
    geo_ref[i, NL - 1] = length
    geo_ref[i, NL] = live
    store_yb(yb_ref, angular, slots, atoms)
    for k0 in range(0, slots, GROUP_FIRST):
        ks = range(k0, k0 + GROUP_FIRST)
        hid, dsl = hidden_of(
            a_ref, [length[k : k + 1] for k in ks], [live[k : k + 1] for k in ks]
        )
        for k in ks:
            at = slice((k - k0) * atoms, (k - k0 + 1) * atoms)
            hid_ref[i, k] = hid[:, at]
            dsl_ref[i, k] = dsl[:, at]

    def hid_tile(k, c0, a0):
        return hid_ref[i, k, pl.ds(c0, 16), a0 : a0 + 128]

    moments_into(hid_tile, yb_ref, g_ref, hid_ref.shape[2], slots, atoms)
    for l in range(NL):
        mom_ref[i, l] = dot(b_ref[...], pack_right(g_ref[l]))
    inv = invariants_of(mom_ref.at[i])
    feat, dpre = silu_parts(dot(mixt_ref[...], pack_right(inv)))
    dpre_ref[i] = dpre
    head_ref[i] = feat[:, :ghost]
    tail_ref[i] = feat[:, atoms - ghost :]
    en_ref[i] = energy_rows(read_ref, feat)


def edge_back(k, edge_tile, sink, yb_ref, m_ref, dy_ref, dlen_ref, chans, atoms):
    for a0 in range(0, atoms, 128):
        y = [yb_ref[k, l, :, a0 : a0 + 128] for l in range(NL - 1)]
        y = [jnp.concatenate([v, v], axis=0) for v in y]
        acc = [jnp.zeros((8, 128), f32) for _ in range(NL)]
        for c0 in range(0, chans, 16):
            e = edge_tile(k, c0, a0)
            de = m_ref[0, c0 : c0 + 16, a0 : a0 + 128]
            for l in range(1, NL):
                dm = m_ref[l, c0 : c0 + 16, a0 : a0 + 128]
                de = de + dm * y[l - 1]
                p = e * dm
                acc[l] = acc[l] + (p[:8] + p[8:])
            p = sink(k, c0, a0, de)
            acc[0] = acc[0] + (p[:8] + p[8:])
        for l in range(1, NL):
            dy_ref[l - 1, k : k + 1, a0 : a0 + 128] = jnp.sum(acc[l], axis=0, keepdims=True)
        dlen_ref[k : k + 1, a0 : a0 + 128] = jnp.sum(acc[0], axis=0, keepdims=True)


@each_image
def radial_kernel(i, idx_ref, geo_ref, a_ref, b_ref, rad_ref, radl_ref, oh_ref):
    slots, _, atoms = rad_ref.shape[1:]
    for k in range(slots):
        oh_ref[i, :, k * atoms : (k + 1) * atoms] = one_hot(
            idx_ref[i, k : k + 1, :], oh_ref.shape[1]
        )
    for k0 in range(0, slots, GROUP):
        ks = range(k0, k0 + GROUP)
        hid, dsl = hidden_of(
            a_ref,
            [geo_ref[i, NL - 1, k : k + 1, :] for k in ks],
            [geo_ref[i, NL, k : k + 1, :] for k in ks],
        )
        rad = dot(b_ref[...], pack_right(hid))
        radl = dot(b_ref[...], pack_right(dsl))
        for k in ks:
            at = slice((k - k0) * atoms, (k - k0 + 1) * atoms)
            rad_ref[i, k] = rad[:, at]
            radl_ref[i, k] = radl[:, at]


@each_image
def second_kernel(
    i, head_ref, tail_ref, hlo_ref, hup_ref, ybs_ref, ohs_ref, rad_ref, radl_ref, mixt_ref,
    mix_ref, read_ref, dfh_ref, dft_ref, dlo_ref, dup_ref, dlen_ref, en_ref, q_ref, m_ref,
    hf_ref, dq_ref,
):
    slots, _, atoms = rad_ref.shape[1:]
    ghost = hlo_ref.shape[2]
    ch = hlo_ref.shape[1]
    yb_ref = ybs_ref.at[i]
    oh_ref = ohs_ref.at[i]
    for n, ref in enumerate((hlo_ref, head_ref, tail_ref, hup_ref)):
        hi, lo = split(ref[i])
        hf_ref[:ch, n * ghost : (n + 1) * ghost] = hi
        hf_ref[ch:, n * ghost : (n + 1) * ghost] = lo
    for k0 in range(0, slots, PULL):
        at = slice(k0 * atoms, (k0 + PULL) * atoms)
        got = dot(hf_ref[...], oh_ref[:, at])
        got = got[:ch] + got[ch:]
        for k in range(k0, k0 + PULL):
            q_ref[i, k] = got[:, (k - k0) * atoms : (k - k0 + 1) * atoms]

    def edge_tile(k, c0, a0):
        cs = pl.ds(c0, 16)
        return rad_ref[i, k, cs, a0 : a0 + 128] * q_ref[i, k, cs, a0 : a0 + 128]

    m = m_ref.at[i]
    moments_into(edge_tile, yb_ref, m, ch, slots, atoms)
    inv = invariants_of(m)
    feat, dpre = silu_parts(dot(mixt_ref[...], pack_right(inv)))
    en_ref[i] = energy_rows(read_ref, feat)
    dinv = dot(mix_ref[...], pack_right(wide(read_ref, atoms) * dpre))
    moment_grads_into(m, dinv, ch)
    for k in range(slots):
        for a0 in range(0, atoms, 128):
            ls = slice(a0, a0 + 128)
            y = [yb_ref[k, l, :, ls] for l in range(NL - 1)]
            y = [jnp.concatenate([v, v], axis=0) for v in y]
            acc = jnp.zeros((8, 128), f32)
            ks = slice(k * atoms + a0, k * atoms + a0 + 128)
            for c0 in range(0, ch, 16):
                cs = slice(c0, c0 + 16)
                de = m[0, cs, ls]
                for l in range(1, NL):
                    de = de + m[l, cs, ls] * y[l - 1]
                hi, lo = split(de * rad_ref[i, k, cs, ls])
                dq_ref[cs, ks] = hi
                dq_ref[ch + c0 : ch + c0 + 16, ks] = lo
                p = de * q_ref[i, k, cs, ls] * radl_ref[i, k, cs, ls]
                acc = acc + (p[:8] + p[8:])
            dlen_ref[i, k : k + 1, ls] = jnp.sum(acc, axis=0, keepdims=True)
    back = dot_nt(dq_ref[...], oh_ref[...])
    back = back[:ch] + back[ch:]
    dlo_ref[i] = back[:, :ghost]
    dfh_ref[i] = back[:, ghost : 2 * ghost]
    dft_ref[i] = back[:, 2 * ghost : 3 * ghost]
    dup_ref[i] = back[:, 3 * ghost :]


@each_image
def angular_kernel(i, rad_ref, q_ref, m_ref, dy_ref):
    slots, ch, atoms = rad_ref.shape[1:]
    for k in range(slots):
        for a0 in range(0, atoms, 128):
            ls = slice(a0, a0 + 128)
            acc = [jnp.zeros((8, 128), f32) for _ in range(NL)]
            for c0 in range(0, ch, 16):
                cs = slice(c0, c0 + 16)
                e = rad_ref[i, k, cs, ls] * q_ref[i, k, cs, ls]
                for l in range(1, NL):
                    p = e * m_ref[i, l, cs, ls]
                    acc[l] = acc[l] + (p[:8] + p[8:])
            for l in range(1, NL):
                dy_ref[i, l - 1, k : k + 1, ls] = jnp.sum(acc[l], axis=0, keepdims=True)


@each_image
def third_kernel(
    i, dfh_ref, dft_ref, rlo_ref, rup_ref, ybs_ref, ohs_ref, geo_ref, hid_ref, dsl_ref, mom_ref, dpre_ref,
    dy2_ref, dlen2_ref, bt_ref, mix_ref, read_ref,
    own_ref, flo_ref, fup_ref,
    m_ref, dg_ref, dy_ref, dlen_ref, doff_ref,
):
    slots, rh, atoms = hid_ref.shape[1:]
    ch, ghost = rlo_ref.shape[1:]
    extent = ohs_ref.shape[1]
    yb_ref = ybs_ref.at[i]
    cot = jnp.concatenate([dfh_ref[i] + rlo_ref[i], dft_ref[i] + rup_ref[i]], axis=1)
    dpre = (cot + wide(read_ref, atoms)) * dpre_ref[i]
    dinv = dot(mix_ref[...], pack_right(dpre))
    for l in range(NL):
        m_ref[l] = mom_ref[i, l]
    moment_grads_into(m_ref, dinv, ch)
    for l in range(NL):
        dg_ref[l] = dot(bt_ref[...], pack_right(m_ref[l]))

    def edge_tile(k, c0, a0):
        return hid_ref[i, k, pl.ds(c0, 16), a0 : a0 + 128]

    def sink(k, c0, a0, de):
        return de * dsl_ref[i, k, c0 : c0 + 16, a0 : a0 + 128]

    for k in range(slots):
        edge_back(k, edge_tile, sink, yb_ref, dg_ref, dy_ref, dlen_ref, rh, atoms)
    dy = [None] + [dy_ref[l] + dy2_ref[i, l] for l in range(NL - 1)]
    ux, uy, uz = [geo_ref[i, n] for n in range(3)]
    length = geo_ref[i, NL - 1]
    dux = dy[1] + uy * dy[4] + uz * dy[6] + ux * dy[7]
    duy = dy[2] + ux * dy[4] + uz * dy[5] - uy * dy[7]
    duz = dy[3] + uy * dy[5] + ux * dy[6] + RT3 * uz * dy[8]
    radial = dlen_ref[...] + dlen2_ref[i] - (dux * ux + duy * uy + duz * uz) / length
    doff = [du / length + radial * u for du, u in ((dux, ux), (duy, uy), (duz, uz))]
    centre = jnp.concatenate([jnp.sum(d, axis=0, keepdims=True) for d in doff], axis=0)
    for x in range(3):
        doff_ref[x] = doff[x]
    back = jnp.zeros((16, extent), f32)
    pad = jnp.zeros((5, atoms), f32)
    for k in range(slots):
        rows = jnp.concatenate([doff_ref[x, k : k + 1, :] for x in range(3)] + [pad], axis=0)
        hi = rows.astype(bf16).astype(f32)
        both = jnp.concatenate([hi, rows - hi], axis=0).astype(bf16)
        back = back + dot_nt(both, ohs_ref[i, :, k * atoms : (k + 1) * atoms])
    force = back[8:11] + back[:3]
    for n in range(own_ref.shape[1]):

        @pl.when(i == n)
        def _():
            own_ref[:, n, :] = centre - force[:, ghost : ghost + atoms]
            flo_ref[:, n, :] = -force[:, :ghost]
            fup_ref[:, n, :] = -force[:, ghost + atoms :]


def lane_row(values):
    lane = lax.broadcasted_iota(jnp.int32, (1, 128), 1)
    row = jnp.zeros((1, 128), f32)
    for n, v in enumerate(values):
        row = jnp.where(lane == n, v, row)
    return row


def total_of(x):
    return jnp.sum(jnp.sum(x, axis=1, keepdims=True), axis=0, keepdims=True)


def chain_of(pos_ref, before_ref, after_ref, start_ref, end_ref, chain):
    count = pos_ref.shape[1]
    me = lax.axis_index("image")
    before = jnp.where(me == 0, start_ref[...], before_ref[...])
    after = jnp.where(me == chain - 1, end_ref[...], after_ref[...])
    prev = [before] + [pos_ref[:, i, :] for i in range(count - 1)]
    nxt = [pos_ref[:, i, :] for i in range(1, count)] + [after]
    return prev, nxt


def partial_kernel(
    own_ref, rlo_ref, rup_ref, pos_ref, before_ref, after_ref, start_ref, end_ref,
    vel_ref, en1_ref, en2_ref, climb_ref, force_ref, send_ref, *, chain,
):
    count = pos_ref.shape[1]
    prev, nxt = chain_of(pos_ref, before_ref, after_ref, start_ref, end_ref, chain)
    values = []
    vel = jnp.zeros((1, 1), f32)
    for i in range(count):
        pos = pos_ref[:, i, :]
        force = own_ref[:, i, :] + jnp.concatenate([rlo_ref[:, i, :], rup_ref[:, i, :]], axis=1)
        force_ref[:, i, :] = force
        spread = nxt[i] - prev[i]
        ahead = nxt[i] - pos
        behind = pos - prev[i]
        values += [
            total_of(ahead * ahead),
            total_of(behind * behind),
            total_of(spread * spread),
            total_of(force * force),
            total_of(force * spread),
            total_of(en1_ref[i]) + total_of(en2_ref[i]),
        ]
        v = vel_ref[:, i, :]
        vel = vel + total_of(v * v)
    send_ref[...] = jnp.broadcast_to(lane_row(values + [vel, climb_ref[0].astype(f32)]), send_ref.shape)


def final_kernel(
    got_ref, force_ref, pos_ref, before_ref, after_ref, start_ref, end_ref,
    vel_ref, neb_ref, vnext_ref, pnext_ref, en_ref,
    *, chain, slabs,
):
    count = pos_ref.shape[1]
    atoms = pos_ref.shape[2]
    me = lax.axis_index("image")
    prev, nxt = chain_of(pos_ref, before_ref, after_ref, start_ref, end_ref, chain)
    rows = [
        jnp.sum(got_ref[g * slabs : (g + 1) * slabs, :], axis=0, keepdims=True)
        for g in range(chain)
    ]
    table = jnp.concatenate(rows, axis=0)
    climb = got_ref[0:1, 6 * count + 1 : 6 * count + 2]
    vel_sq = jnp.sum(table[:, 6 * count : 6 * count + 1], axis=0, keepdims=True)
    group = lax.broadcasted_iota(jnp.int32, (chain, 1), 0)
    force_sq = jnp.zeros((1, 1), f32)
    mine = []
    for i in range(count):
        ahead, behind, spread_sq, ff, fd, energy = [
            table[:, 6 * i + n : 6 * i + n + 1] for n in range(6)
        ]
        norm = 1.0 / jnp.sqrt(spread_sq + 1e-06)
        along = fd * norm
        climbing = jnp.where((group * count + i).astype(f32) == climb, 1.0, 0.0).astype(f32)
        spring = 5.0 * (jnp.sqrt(ahead) - jnp.sqrt(behind))
        coef = -(1.0 + climbing) * along + (1.0 - climbing) * spring
        scale = coef * norm
        part = ff + 2.0 * coef * along + scale * scale * spread_sq
        force_sq = force_sq + jnp.sum(part, axis=0, keepdims=True)
        here = group == me
        mine.append(jnp.sum(jnp.where(here, scale, 0.0), axis=0, keepdims=True))
        en_ref[i] = jnp.sum(jnp.where(here, energy, 0.0)) * (1.0 / (atoms * slabs))
    gain = 0.1 * jnp.sqrt(vel_sq / (force_sq + 1e-06))
    for i in range(count):
        neb = force_ref[:, i, :] + mine[i] * (nxt[i] - prev[i])
        neb_ref[:, i, :] = neb
        vnext = 0.9 * vel_ref[:, i, :] + gain * neb + 0.1 * neb
        vnext_ref[:, i, :] = vnext
        pnext_ref[:, i, :] = pos_ref[:, i, :] + 0.1 * vnext


def out(*shape):
    return jax.ShapeDtypeStruct(shape, f32)


def half(*shape):
    return jax.ShapeDtypeStruct(shape, bf16)


ANY = pl.BlockSpec(memory_space=pl.ANY)
VMEM = pl.BlockSpec(memory_space=pltpu.VMEM)
SMEM = pl.BlockSpec(memory_space=pltpu.SMEM)


def neighbours_of(cells, axis):
    count = lax.axis_size(axis)
    up = [(i, (i + 1) % count) for i in range(count)]
    down = [((i + 1) % count, i) for i in range(count)]
    to_below, to_above = cells
    return lax.ppermute(to_above, axis, up), lax.ppermute(to_below, axis, down)


def local(
    positions,
    velocity,
    start_state,
    end_state,
    neighbours,
    counts,
    climb_index,
    radial_a1,
    radial_b1,
    mix_first,
    read_first,
    radial_a2,
    radial_b2,
    mix_second,
    read_second,
):
    images, _, atoms = positions.shape
    slots = neighbours.shape[1]
    ghost = atoms // 2
    nb, rh = radial_a1.shape
    ch = radial_b1.shape[1]
    extent = atoms + 2 * ghost
    space = lax.axis_size("space")
    chain = lax.axis_size("image")
    params = pltpu.CompilerParams(vmem_limit_bytes=BIG_VMEM)
    small = pltpu.CompilerParams(vmem_limit_bytes=SMALL_VMEM)
    pos = positions.transpose(1, 0, 2)
    vel = velocity.transpose(1, 0, 2)

    plo, pup = neighbours_of((pos[:, :, :ghost], pos[:, :, ghost:]), "space")
    before = lax.ppermute(pos[:, images - 1], "image", [(i, i + 1) for i in range(chain - 1)])
    after = lax.ppermute(pos[:, 0], "image", [(i + 1, i) for i in range(chain - 1)])
    weights = (
        radial_a1, radial_b1, mix_first, read_first.reshape(1, ch),
        radial_a2, radial_b2, mix_second, read_second.reshape(1, ch),
    )
    idx, cnt, a1, b1, m1t, m1, b1t, r1, a2, b2, m2t, m2, r2 = pl.pallas_call(
        prep_kernel,
        in_specs=[pl.BlockSpec(memory_space=pltpu.HBM)] * 10,
        out_specs=[VMEM] * 13,
        out_shape=[
            jax.ShapeDtypeStruct(neighbours.shape, jnp.int32),
            jax.ShapeDtypeStruct(counts.shape, jnp.int32),
            half(rh, 3 * nb),
            half(ch, 3 * rh),
            half(ch, 9 * ch),
            half(3 * ch, 3 * ch),
            half(rh, 3 * ch),
            out(ch, 128),
            half(rh, 3 * nb),
            half(ch, 3 * rh),
            half(ch, 9 * ch),
            half(3 * ch, 3 * ch),
            out(ch, 128),
        ],
        scratch_shapes=[pltpu.VMEM(w.shape, f32) for w in weights]
        + [pltpu.SemaphoreType.DMA((10,))],
        compiler_params=small,
        cost_estimate=pl.CostEstimate(flops=4000000, bytes_accessed=4000000, transcendentals=0),
        name="prep",
    )(*[pltpu.with_memory_space_constraint(w, pltpu.HBM) for w in (neighbours, counts) + weights])
    geo_n = NL + 1

    head, tail, geo, hid, dsl, mom, dpre, en1, yb = pl.pallas_call(
        functools.partial(first_kernel, images=images),
        in_specs=[VMEM] * 3 + [ANY] * 2 + [VMEM] * 6,
        out_specs=[VMEM] * 9,
        out_shape=[
            out(images, ch, ghost),
            out(images, ch, ghost),
            out(images, geo_n, slots, atoms),
            out(images, slots, rh, atoms),
            out(images, slots, rh, atoms),
            out(images, NL, ch, atoms),
            out(images, ch, atoms),
            out(images, 8, 128),
            out(images, slots, NL - 1, 8, atoms),
        ],
        scratch_shapes=[pltpu.VMEM((NL, rh, atoms), f32)],
        compiler_params=params,
        name="first",
    )(pos, plo, pup, before, after, idx, cnt, a1, b1, m1t, r1)

    hlo, hup = neighbours_of((head, tail), "space")

    rad, radl, oh = pl.pallas_call(
        functools.partial(radial_kernel, images=images),
        in_specs=[VMEM] * 4,
        out_specs=[VMEM] * 3,
        out_shape=[out(images, slots, ch, atoms)] * 2 + [half(images, extent, slots * atoms)],
        compiler_params=small,
        cost_estimate=pl.CostEstimate(flops=1 << 30, bytes_accessed=1 << 23, transcendentals=1 << 20),
        name="radial",
    )(idx, geo, a2, b2)
    dfh, dft, dlo, dup, dlen2, en2, q, dm = pl.pallas_call(
        functools.partial(second_kernel, images=images),
        in_specs=[VMEM] * 11,
        out_specs=[VMEM] * 8,
        out_shape=[out(images, ch, ghost)] * 4
        + [
            out(images, slots, atoms),
            out(images, 8, 128),
            out(images, slots, ch, atoms),
            out(images, NL, ch, atoms),
        ],
        scratch_shapes=[
            pltpu.VMEM((2 * ch, extent), bf16),
            pltpu.VMEM((2 * ch, slots * atoms), bf16),
        ],
        compiler_params=params,
        name="second",
    )(head, tail, hlo, hup, yb, oh, rad, radl, m2t, m2, r2)

    rlo, rup = neighbours_of((dlo, dup), "space")
    dy2 = pl.pallas_call(
        functools.partial(angular_kernel, images=images),
        in_specs=[VMEM] * 3,
        out_specs=VMEM,
        out_shape=out(images, NL - 1, slots, atoms),
        compiler_params=small,
        cost_estimate=pl.CostEstimate(flops=1 << 30, bytes_accessed=1 << 23, transcendentals=0),
        name="angular",
    )(rad, q, dm)

    own, flo, fup = pl.pallas_call(
        functools.partial(third_kernel, images=images),
        in_specs=[VMEM] * 16,
        out_specs=[VMEM] * 3,
        out_shape=[out(3, images, atoms), out(3, images, ghost), out(3, images, ghost)],
        scratch_shapes=[
            pltpu.VMEM((NL, ch, atoms), f32),
            pltpu.VMEM((NL, rh, atoms), f32),
            pltpu.VMEM((NL - 1, slots, atoms), f32),
            pltpu.VMEM((slots, atoms), f32),
            pltpu.VMEM((3, slots, atoms), f32),
        ],
        compiler_params=params,
        name="third",
    )(dfh, dft, rlo, rup, yb, oh, geo, hid, dsl, mom, dpre, dy2, dlen2, b1t, m1, r1)

    glo, gup = neighbours_of((flo, fup), "space")

    rank = chain * space
    force, send = pl.pallas_call(
        functools.partial(partial_kernel, chain=chain),
        in_specs=[VMEM] * 11 + [SMEM],
        out_specs=[VMEM] * 2,
        out_shape=[out(3, images, atoms), out(rank, 128)],
        compiler_params=small,
        name="partial",
    )(own, glo, gup, pos, before, after, start_state, end_state, vel, en1, en2, climb_index)
    got = lax.all_to_all(
        send.reshape(rank, 1, 128), ("image", "space"), split_axis=0, concat_axis=0
    ).reshape(rank, 128)
    neb, vnext, pnext, energy = pl.pallas_call(
        functools.partial(final_kernel, chain=chain, slabs=space),
        in_specs=[VMEM] * 8,
        out_specs=[VMEM] * 3 + [SMEM],
        out_shape=[out(3, images, atoms)] * 3 + [out(images)],
        compiler_params=small,
        name="final",
    )(got, force, pos, before, after, start_state, end_state, vel)
    return (
        neb.transpose(1, 0, 2),
        vnext.transpose(1, 0, 2),
        pnext.transpose(1, 0, 2),
        energy,
    )


def solution(mesh):
    in_specs = (
        P("image", None, "space"),
        P("image", None, "space"),
        P(None, "space"),
        P(None, "space"),
        P("image", None, "space"),
        P("image", "space"),
        P(),
        P(),
        P(),
        P(),
        P(),
        P(),
        P(),
        P(),
        P(),
    )
    out_specs = (
        P("image", None, "space"),
        P("image", None, "space"),
        P("image", None, "space"),
        P("image"),
    )
    return jax.shard_map(local, mesh=mesh, in_specs=in_specs, out_specs=out_specs, check_vma=False)
```

```python
import functools
import math

import jax
import jax.numpy as jnp
from jax import lax
from jax.experimental import pallas as pl
from jax.experimental.pallas import tpu as pltpu
from jax.sharding import PartitionSpec as P

f32 = jnp.float32
bf16 = jnp.bfloat16
RT3 = math.sqrt(3.0)
NL = 9
GROUP_FIRST = 2
GROUP = 8
PULL = 8
BIG_VMEM = 16 << 20
SMALL_VMEM = 4 << 20


def split(x):
    hi = x.astype(bf16)
    lo = (x - hi.astype(f32)).astype(bf16)
    return hi, lo


def dot(a, b):
    return lax.dot_general(a, b, (((1,), (0,)), ((), ())), preferred_element_type=f32)


def dot_nt(a, b):
    return lax.dot_general(a, b, (((1,), (1,)), ((), ())), preferred_element_type=f32)


def pack_left(w):
    hi, lo = split(w)
    return jnp.concatenate([hi, hi, lo], axis=1)


def pack_right(x):
    hi, lo = split(x)
    return jnp.concatenate([hi, lo, hi], axis=0)


def one_hot(row, extent):
    step = 256
    wide = (step, row.shape[1])
    ids = lax.broadcasted_iota(jnp.int32, wide, 0).astype(f32).astype(bf16)
    zero, one = jnp.zeros(wide, bf16), jnp.ones(wide, bf16)
    parts = []
    for first in range(0, extent, step):
        here = jnp.broadcast_to((row - first).astype(f32), wide).astype(bf16)
        parts.append(jnp.where(ids == here, one, zero))
    return jnp.concatenate(parts, axis=0)


def lane_gather(row, idx):
    slots, atoms = idx.shape
    extent = row.shape[1]
    lane = idx & 127
    tile = idx >> 7
    blocks = [jnp.broadcast_to(row[:, t : t + 128], (8, 128)) for t in range(0, extent, 128)]
    out_rows = []
    for s0 in range(0, slots, 8):
        cells = []
        for a0 in range(0, atoms, 128):
            at = lane[s0 : s0 + 8, a0 : a0 + 128]
            which = tile[s0 : s0 + 8, a0 : a0 + 128]
            got = None
            for t, block in enumerate(blocks):
                v = jnp.take_along_axis(block, at, axis=1, mode="promise_in_bounds")
                got = v if got is None else jnp.where(which == t, v, got)
            cells.append(got)
        out_rows.append(jnp.concatenate(cells, axis=1))
    return jnp.concatenate(out_rows, axis=0)


def pick(block, i, axis):
    n = block.shape[axis]
    got = lax.index_in_dim(block, 0, axis, keepdims=False)
    for m in range(1, n):
        got = jnp.where(i == m, lax.index_in_dim(block, m, axis, keepdims=False), got)
    return got


def silu_parts(z):
    s = 0.5 + 0.5 * jnp.tanh(0.5 * z)
    h = z * s
    return h, s + h * (1.0 - s)


def basis_of(row):
    nb = 8
    centres = 0.5 * lax.broadcasted_iota(jnp.int32, (nb, row.shape[1]), 0).astype(f32)
    spread = row - centres
    basis = jnp.exp(-2.0 * spread * spread)
    return basis, -4.0 * spread * basis


def moments_into(edge_tile, yb_ref, m_ref, chans, slots, atoms):
    def tile(t, carry):
        c0 = pl.multiple_of(t * 16, 16)
        for a0 in range(0, atoms, 128):
            acc = [jnp.zeros((16, 128), f32) for _ in range(NL)]
            for k in range(slots):
                e = edge_tile(k, c0, a0)
                acc[0] = acc[0] + e
                for l in range(1, NL):
                    y = yb_ref[k, l - 1, :, a0 : a0 + 128]
                    acc[l] = acc[l] + e * jnp.concatenate([y, y], axis=0)
            for l in range(NL):
                m_ref[l, pl.ds(c0, 16), a0 : a0 + 128] = acc[l]
        return carry

    lax.fori_loop(0, chans // 16, tile, 0, unroll=True)


def store_yb(yb_ref, angular, slots, atoms):
    for k in range(slots):
        for l in range(NL - 1):
            yb_ref[k, l] = jnp.broadcast_to(angular[l][k : k + 1], (8, atoms))


def invariants_of(m_ref):
    m = [m_ref[l] for l in range(NL)]
    one = m[1] * m[1] + m[2] * m[2] + m[3] * m[3]
    two = m[4] * m[4] + m[5] * m[5] + m[6] * m[6] + m[7] * m[7] + m[8] * m[8]
    return jnp.concatenate([m[0], one, two], axis=0)


def moment_grads_into(m_ref, dinv, chans):
    m_ref[0] = dinv[:chans]
    d1 = 2.0 * dinv[chans : 2 * chans]
    d2 = 2.0 * dinv[2 * chans :]
    for l in range(1, NL):
        m_ref[l] = m_ref[l] * (d1 if l < 4 else d2)


def prep_kernel(*refs):
    n = 10
    hbm, outs, bufs, sems = refs[:n], refs[n : n + 13], refs[n + 13 : -1], refs[-1]
    (
        idx_out, cnt_out, a1_out, b1_out, m1t_out, m1_out, b1t_out, r1_out,
        a2_out, b2_out, m2t_out, m2_out, r2_out,
    ) = outs
    a1, b1, m1, r1, a2, b2, m2, r2 = bufs
    targets = (idx_out, cnt_out) + bufs
    copies = [pltpu.make_async_copy(h, t, sems.at[q]) for q, (h, t) in enumerate(zip(hbm, targets))]
    for c in copies:
        c.start()
    for c in copies:
        c.wait()
    a1_out[...] = pack_left(a1[...].T)
    b1_out[...] = pack_left(b1[...].T)
    m1t_out[...] = pack_left(m1[...].T)
    m1_out[...] = pack_left(m1[...])
    b1t_out[...] = pack_left(b1[...])
    r1_out[...] = jnp.broadcast_to(r1[...], r1_out.shape[::-1]).T
    a2_out[...] = pack_left(a2[...].T)
    b2_out[...] = pack_left(b2[...].T)
    m2t_out[...] = pack_left(m2[...].T)
    m2_out[...] = pack_left(m2[...])
    r2_out[...] = jnp.broadcast_to(r2[...], r2_out.shape[::-1]).T


def lanes(parts):
    return jnp.concatenate(parts, axis=1)


def hidden_of(a_ref, rows, lives):
    pairs = [basis_of(row) for row in rows]
    hid, ds = silu_parts(dot(a_ref[...], lanes([pack_right(p[0]) for p in pairs])))
    back = dot(a_ref[...], lanes([pack_right(p[1]) for p in pairs]))
    live = lanes(lives)
    return hid * live, ds * live * back


def energy_rows(read_ref, feat):
    ch, atoms = feat.shape
    read = read_ref[...]
    en = jnp.concatenate([read] * (atoms // 128), axis=1) * feat
    total = jnp.sum(en.reshape(ch // 8, 8, atoms), axis=0)
    return sum(total[:, a0 : a0 + 128] for a0 in range(0, atoms, 128))


def wide(read_ref, atoms):
    return jnp.concatenate([read_ref[...]] * (atoms // 128), axis=1)


def each_image(body):
    def kernel(*refs, images):
        def step(i, carry):
            body(i, *refs)
            return carry

        lax.fori_loop(0, images, step, 0)

    return kernel


@each_image
def first_kernel(
    i, pos_ref, plo_ref, pup_ref, before_ref, after_ref, idx_ref, cnt_ref, a_ref, b_ref, mixt_ref,
    read_ref, head_ref, tail_ref, geo_ref, hid_ref, dsl_ref, mom_ref, dpre_ref, en_ref, ybs_ref,
    g_ref,
):
    slots, atoms = idx_ref.shape[1:]
    yb_ref = ybs_ref.at[i]
    ghost = plo_ref.shape[2]
    idx = idx_ref[i]
    pos = pick(pos_ref[...], i, 1)
    plo = pick(plo_ref[...], i, 1)
    pup = pick(pup_ref[...], i, 1)
    ext = jnp.concatenate([plo, pos, pup], axis=1)
    off = [lane_gather(ext[x : x + 1], idx) - pos[x : x + 1] for x in range(3)]
    length = jnp.sqrt(off[0] * off[0] + off[1] * off[1] + off[2] * off[2] + 1.0)
    ux, uy, uz = [o / length for o in off]
    ids = lax.broadcasted_iota(jnp.int32, (slots, atoms), 0)
    cnt = pick(cnt_ref[...][None], i, 1)
    live = jnp.where(ids < cnt, 1.0 / slots, 0.0).astype(f32)
    angular = [
        ux,
        uy,
        uz,
        ux * uy,
        uy * uz,
        ux * uz,
        0.5 * (ux * ux - uy * uy),
        (3.0 * uz * uz - 1.0) / (2.0 * RT3),
    ]
    for l in range(NL - 1):
        geo_ref[i, l] = angular[l]
    geo_ref[i, NL - 1] = length
    geo_ref[i, NL] = live
    store_yb(yb_ref, angular, slots, atoms)
    for k0 in range(0, slots, GROUP_FIRST):
        ks = range(k0, k0 + GROUP_FIRST)
        hid, dsl = hidden_of(
            a_ref, [length[k : k + 1] for k in ks], [live[k : k + 1] for k in ks]
        )
        for k in ks:
            at = slice((k - k0) * atoms, (k - k0 + 1) * atoms)
            hid_ref[i, k] = hid[:, at]
            dsl_ref[i, k] = dsl[:, at]

    def hid_tile(k, c0, a0):
        return hid_ref[i, k, pl.ds(c0, 16), a0 : a0 + 128]

    moments_into(hid_tile, yb_ref, g_ref, hid_ref.shape[2], slots, atoms)
    for l in range(NL):
        mom_ref[i, l] = dot(b_ref[...], pack_right(g_ref[l]))
    inv = invariants_of(mom_ref.at[i])
    feat, dpre = silu_parts(dot(mixt_ref[...], pack_right(inv)))
    dpre_ref[i] = dpre
    head_ref[i] = feat[:, :ghost]
    tail_ref[i] = feat[:, atoms - ghost :]
    en_ref[i] = energy_rows(read_ref, feat)


def edge_back(k, edge_tile, sink, yb_ref, m_ref, dy_ref, dlen_ref, chans, atoms):
    for a0 in range(0, atoms, 128):
        y = [yb_ref[k, l, :, a0 : a0 + 128] for l in range(NL - 1)]
        y = [jnp.concatenate([v, v], axis=0) for v in y]
        acc = [jnp.zeros((8, 128), f32) for _ in range(NL)]
        for c0 in range(0, chans, 16):
            e = edge_tile(k, c0, a0)
            de = m_ref[0, c0 : c0 + 16, a0 : a0 + 128]
            for l in range(1, NL):
                dm = m_ref[l, c0 : c0 + 16, a0 : a0 + 128]
                de = de + dm * y[l - 1]
                p = e * dm
                acc[l] = acc[l] + (p[:8] + p[8:])
            p = sink(k, c0, a0, de)
            acc[0] = acc[0] + (p[:8] + p[8:])
        for l in range(1, NL):
            dy_ref[l - 1, k : k + 1, a0 : a0 + 128] = jnp.sum(acc[l], axis=0, keepdims=True)
        dlen_ref[k : k + 1, a0 : a0 + 128] = jnp.sum(acc[0], axis=0, keepdims=True)


@each_image
def radial_kernel(i, idx_ref, geo_ref, a_ref, b_ref, rad_ref, radl_ref, oh_ref):
    slots, _, atoms = rad_ref.shape[1:]
    for k in range(slots):
        oh_ref[i, :, k * atoms : (k + 1) * atoms] = one_hot(
            idx_ref[i, k : k + 1, :], oh_ref.shape[1]
        )
    for k0 in range(0, slots, GROUP):
        ks = range(k0, k0 + GROUP)
        hid, dsl = hidden_of(
            a_ref,
            [geo_ref[i, NL - 1, k : k + 1, :] for k in ks],
            [geo_ref[i, NL, k : k + 1, :] for k in ks],
        )
        rad = dot(b_ref[...], pack_right(hid))
        radl = dot(b_ref[...], pack_right(dsl))
        for k in ks:
            at = slice((k - k0) * atoms, (k - k0 + 1) * atoms)
            rad_ref[i, k] = rad[:, at]
            radl_ref[i, k] = radl[:, at]


@each_image
def second_kernel(
    i, head_ref, tail_ref, hlo_ref, hup_ref, ybs_ref, ohs_ref, rad_ref, radl_ref, mixt_ref,
    mix_ref, read_ref, dfh_ref, dft_ref, dlo_ref, dup_ref, dlen_ref, en_ref, q_ref, m_ref,
    hf_ref, dq_ref,
):
    slots, _, atoms = rad_ref.shape[1:]
    ghost = hlo_ref.shape[2]
    ch = hlo_ref.shape[1]
    yb_ref = ybs_ref.at[i]
    oh_ref = ohs_ref.at[i]
    for n, ref in enumerate((hlo_ref, head_ref, tail_ref, hup_ref)):
        hi, lo = split(ref[i])
        hf_ref[:ch, n * ghost : (n + 1) * ghost] = hi
        hf_ref[ch:, n * ghost : (n + 1) * ghost] = lo
    for k0 in range(0, slots, PULL):
        at = slice(k0 * atoms, (k0 + PULL) * atoms)
        got = dot(hf_ref[...], oh_ref[:, at])
        got = got[:ch] + got[ch:]
        for k in range(k0, k0 + PULL):
            q_ref[i, k] = got[:, (k - k0) * atoms : (k - k0 + 1) * atoms]

    def edge_tile(k, c0, a0):
        cs = pl.ds(c0, 16)
        return rad_ref[i, k, cs, a0 : a0 + 128] * q_ref[i, k, cs, a0 : a0 + 128]

    m = m_ref.at[i]
    moments_into(edge_tile, yb_ref, m, ch, slots, atoms)
    inv = invariants_of(m)
    feat, dpre = silu_parts(dot(mixt_ref[...], pack_right(inv)))
    en_ref[i] = energy_rows(read_ref, feat)
    dinv = dot(mix_ref[...], pack_right(wide(read_ref, atoms) * dpre))
    moment_grads_into(m, dinv, ch)
    for k in range(slots):
        for a0 in range(0, atoms, 128):
            ls = slice(a0, a0 + 128)
            y = [yb_ref[k, l, :, ls] for l in range(NL - 1)]
            y = [jnp.concatenate([v, v], axis=0) for v in y]
            acc = jnp.zeros((8, 128), f32)
            ks = slice(k * atoms + a0, k * atoms + a0 + 128)
            for c0 in range(0, ch, 16):
                cs = slice(c0, c0 + 16)
                de = m[0, cs, ls]
                for l in range(1, NL):
                    de = de + m[l, cs, ls] * y[l - 1]
                hi, lo = split(de * rad_ref[i, k, cs, ls])
                dq_ref[cs, ks] = hi
                dq_ref[ch + c0 : ch + c0 + 16, ks] = lo
                p = de * q_ref[i, k, cs, ls] * radl_ref[i, k, cs, ls]
                acc = acc + (p[:8] + p[8:])
            dlen_ref[i, k : k + 1, ls] = jnp.sum(acc, axis=0, keepdims=True)
    back = dot_nt(dq_ref[...], oh_ref[...])
    back = back[:ch] + back[ch:]
    dlo_ref[i] = back[:, :ghost]
    dfh_ref[i] = back[:, ghost : 2 * ghost]
    dft_ref[i] = back[:, 2 * ghost : 3 * ghost]
    dup_ref[i] = back[:, 3 * ghost :]


@each_image
def angular_kernel(i, rad_ref, q_ref, m_ref, dy_ref):
    slots, ch, atoms = rad_ref.shape[1:]
    for k in range(slots):
        for a0 in range(0, atoms, 128):
            ls = slice(a0, a0 + 128)
            acc = [jnp.zeros((8, 128), f32) for _ in range(NL)]
            for c0 in range(0, ch, 16):
                cs = slice(c0, c0 + 16)
                e = rad_ref[i, k, cs, ls] * q_ref[i, k, cs, ls]
                for l in range(1, NL):
                    p = e * m_ref[i, l, cs, ls]
                    acc[l] = acc[l] + (p[:8] + p[8:])
            for l in range(1, NL):
                dy_ref[i, l - 1, k : k + 1, ls] = jnp.sum(acc[l], axis=0, keepdims=True)


@each_image
def third_kernel(
    i, dfh_ref, dft_ref, rlo_ref, rup_ref, ybs_ref, ohs_ref, geo_ref, hid_ref, dsl_ref, mom_ref, dpre_ref,
    dy2_ref, dlen2_ref, bt_ref, mix_ref, read_ref,
    own_ref, flo_ref, fup_ref,
    m_ref, dg_ref, dy_ref, dlen_ref, doff_ref,
):
    slots, rh, atoms = hid_ref.shape[1:]
    ch, ghost = rlo_ref.shape[1:]
    extent = ohs_ref.shape[1]
    yb_ref = ybs_ref.at[i]
    cot = jnp.concatenate([dfh_ref[i] + rlo_ref[i], dft_ref[i] + rup_ref[i]], axis=1)
    dpre = (cot + wide(read_ref, atoms)) * dpre_ref[i]
    dinv = dot(mix_ref[...], pack_right(dpre))
    for l in range(NL):
        m_ref[l] = mom_ref[i, l]
    moment_grads_into(m_ref, dinv, ch)
    for l in range(NL):
        dg_ref[l] = dot(bt_ref[...], pack_right(m_ref[l]))

    def edge_tile(k, c0, a0):
        return hid_ref[i, k, pl.ds(c0, 16), a0 : a0 + 128]

    def sink(k, c0, a0, de):
        return de * dsl_ref[i, k, c0 : c0 + 16, a0 : a0 + 128]

    for k in range(slots):
        edge_back(k, edge_tile, sink, yb_ref, dg_ref, dy_ref, dlen_ref, rh, atoms)
    dy = [None] + [dy_ref[l] + dy2_ref[i, l] for l in range(NL - 1)]
    ux, uy, uz = [geo_ref[i, n] for n in range(3)]
    length = geo_ref[i, NL - 1]
    dux = dy[1] + uy * dy[4] + uz * dy[6] + ux * dy[7]
    duy = dy[2] + ux * dy[4] + uz * dy[5] - uy * dy[7]
    duz = dy[3] + uy * dy[5] + ux * dy[6] + RT3 * uz * dy[8]
    radial = dlen_ref[...] + dlen2_ref[i] - (dux * ux + duy * uy + duz * uz) / length
    doff = [du / length + radial * u for du, u in ((dux, ux), (duy, uy), (duz, uz))]
    centre = jnp.concatenate([jnp.sum(d, axis=0, keepdims=True) for d in doff], axis=0)
    for x in range(3):
        doff_ref[x] = doff[x]
    back = jnp.zeros((16, extent), f32)
    pad = jnp.zeros((5, atoms), f32)
    for k in range(slots):
        rows = jnp.concatenate([doff_ref[x, k : k + 1, :] for x in range(3)] + [pad], axis=0)
        hi = rows.astype(bf16).astype(f32)
        both = jnp.concatenate([hi, rows - hi], axis=0).astype(bf16)
        back = back + dot_nt(both, ohs_ref[i, :, k * atoms : (k + 1) * atoms])
    force = back[8:11] + back[:3]
    for n in range(own_ref.shape[1]):

        @pl.when(i == n)
        def _():
            own_ref[:, n, :] = centre - force[:, ghost : ghost + atoms]
            flo_ref[:, n, :] = -force[:, :ghost]
            fup_ref[:, n, :] = -force[:, ghost + atoms :]


def lane_row(values):
    lane = lax.broadcasted_iota(jnp.int32, (1, 128), 1)
    row = jnp.zeros((1, 128), f32)
    for n, v in enumerate(values):
        row = jnp.where(lane == n, v, row)
    return row


def total_of(x):
    return jnp.sum(jnp.sum(x, axis=1, keepdims=True), axis=0, keepdims=True)


def chain_of(pos_ref, before_ref, after_ref, start_ref, end_ref, chain):
    count = pos_ref.shape[1]
    me = lax.axis_index("image")
    before = jnp.where(me == 0, start_ref[...], before_ref[...])
    after = jnp.where(me == chain - 1, end_ref[...], after_ref[...])
    prev = [before] + [pos_ref[:, i, :] for i in range(count - 1)]
    nxt = [pos_ref[:, i, :] for i in range(1, count)] + [after]
    return prev, nxt


def partial_kernel(
    own_ref, rlo_ref, rup_ref, pos_ref, before_ref, after_ref, start_ref, end_ref,
    vel_ref, en1_ref, en2_ref, climb_ref, force_ref, send_ref, *, chain,
):
    count = pos_ref.shape[1]
    prev, nxt = chain_of(pos_ref, before_ref, after_ref, start_ref, end_ref, chain)
    values = []
    vel = jnp.zeros((1, 1), f32)
    for i in range(count):
        pos = pos_ref[:, i, :]
        force = own_ref[:, i, :] + jnp.concatenate([rlo_ref[:, i, :], rup_ref[:, i, :]], axis=1)
        force_ref[:, i, :] = force
        spread = nxt[i] - prev[i]
        ahead = nxt[i] - pos
        behind = pos - prev[i]
        values += [
            total_of(ahead * ahead),
            total_of(behind * behind),
            total_of(spread * spread),
            total_of(force * force),
            total_of(force * spread),
            total_of(en1_ref[i]) + total_of(en2_ref[i]),
        ]
        v = vel_ref[:, i, :]
        vel = vel + total_of(v * v)
    send_ref[...] = jnp.broadcast_to(lane_row(values + [vel, climb_ref[0].astype(f32)]), send_ref.shape)


def final_kernel(
    got_ref, force_ref, pos_ref, before_ref, after_ref, start_ref, end_ref,
    vel_ref, neb_ref, vnext_ref, pnext_ref, en_ref,
    *, chain, slabs,
):
    count = pos_ref.shape[1]
    atoms = pos_ref.shape[2]
    me = lax.axis_index("image")
    prev, nxt = chain_of(pos_ref, before_ref, after_ref, start_ref, end_ref, chain)
    rows = [
        jnp.sum(got_ref[g * slabs : (g + 1) * slabs, :], axis=0, keepdims=True)
        for g in range(chain)
    ]
    table = jnp.concatenate(rows, axis=0)
    climb = got_ref[0:1, 6 * count + 1 : 6 * count + 2]
    vel_sq = jnp.sum(table[:, 6 * count : 6 * count + 1], axis=0, keepdims=True)
    group = lax.broadcasted_iota(jnp.int32, (chain, 1), 0)
    force_sq = jnp.zeros((1, 1), f32)
    mine = []
    for i in range(count):
        ahead, behind, spread_sq, ff, fd, energy = [
            table[:, 6 * i + n : 6 * i + n + 1] for n in range(6)
        ]
        norm = 1.0 / jnp.sqrt(spread_sq + 1e-06)
        along = fd * norm
        climbing = jnp.where((group * count + i).astype(f32) == climb, 1.0, 0.0).astype(f32)
        spring = 5.0 * (jnp.sqrt(ahead) - jnp.sqrt(behind))
        coef = -(1.0 + climbing) * along + (1.0 - climbing) * spring
        scale = coef * norm
        part = ff + 2.0 * coef * along + scale * scale * spread_sq
        force_sq = force_sq + jnp.sum(part, axis=0, keepdims=True)
        here = group == me
        mine.append(jnp.sum(jnp.where(here, scale, 0.0), axis=0, keepdims=True))
        en_ref[i] = jnp.sum(jnp.where(here, energy, 0.0)) * (1.0 / (atoms * slabs))
    gain = 0.1 * jnp.sqrt(vel_sq / (force_sq + 1e-06))
    for i in range(count):
        neb = force_ref[:, i, :] + mine[i] * (nxt[i] - prev[i])
        neb_ref[:, i, :] = neb
        vnext = 0.9 * vel_ref[:, i, :] + gain * neb + 0.1 * neb
        vnext_ref[:, i, :] = vnext
        pnext_ref[:, i, :] = pos_ref[:, i, :] + 0.1 * vnext


def out(*shape):
    return jax.ShapeDtypeStruct(shape, f32)


def half(*shape):
    return jax.ShapeDtypeStruct(shape, bf16)


ANY = pl.BlockSpec(memory_space=pl.ANY)
VMEM = pl.BlockSpec(memory_space=pltpu.VMEM)
SMEM = pl.BlockSpec(memory_space=pltpu.SMEM)


def neighbours_of(cells, axis):
    count = lax.axis_size(axis)
    up = [(i, (i + 1) % count) for i in range(count)]
    down = [((i + 1) % count, i) for i in range(count)]
    to_below, to_above = cells
    return lax.ppermute(to_above, axis, up), lax.ppermute(to_below, axis, down)


def local(
    positions,
    velocity,
    start_state,
    end_state,
    neighbours,
    counts,
    climb_index,
    radial_a1,
    radial_b1,
    mix_first,
    read_first,
    radial_a2,
    radial_b2,
    mix_second,
    read_second,
):
    images, _, atoms = positions.shape
    slots = neighbours.shape[1]
    ghost = atoms // 2
    nb, rh = radial_a1.shape
    ch = radial_b1.shape[1]
    extent = atoms + 2 * ghost
    space = lax.axis_size("space")
    chain = lax.axis_size("image")
    params = pltpu.CompilerParams(vmem_limit_bytes=BIG_VMEM)
    small = pltpu.CompilerParams(vmem_limit_bytes=SMALL_VMEM)
    pos = positions.transpose(1, 0, 2)
    vel = velocity.transpose(1, 0, 2)

    plo, pup = neighbours_of((pos[:, :, :ghost], pos[:, :, ghost:]), "space")
    before = lax.ppermute(pos[:, images - 1], "image", [(i, i + 1) for i in range(chain - 1)])
    after = lax.ppermute(pos[:, 0], "image", [(i + 1, i) for i in range(chain - 1)])
    weights = (
        radial_a1, radial_b1, mix_first, read_first.reshape(1, ch),
        radial_a2, radial_b2, mix_second, read_second.reshape(1, ch),
    )
    idx, cnt, a1, b1, m1t, m1, b1t, r1, a2, b2, m2t, m2, r2 = pl.pallas_call(
        prep_kernel,
        in_specs=[pl.BlockSpec(memory_space=pltpu.HBM)] * 10,
        out_specs=[VMEM] * 13,
        out_shape=[
            jax.ShapeDtypeStruct(neighbours.shape, jnp.int32),
            jax.ShapeDtypeStruct(counts.shape, jnp.int32),
            half(rh, 3 * nb),
            half(ch, 3 * rh),
            half(ch, 9 * ch),
            half(3 * ch, 3 * ch),
            half(rh, 3 * ch),
            out(ch, 128),
            half(rh, 3 * nb),
            half(ch, 3 * rh),
            half(ch, 9 * ch),
            half(3 * ch, 3 * ch),
            out(ch, 128),
        ],
        scratch_shapes=[pltpu.VMEM(w.shape, f32) for w in weights]
        + [pltpu.SemaphoreType.DMA((10,))],
        compiler_params=small,
        cost_estimate=pl.CostEstimate(flops=4000000, bytes_accessed=4000000, transcendentals=0),
        name="prep",
    )(*[pltpu.with_memory_space_constraint(w, pltpu.HBM) for w in (neighbours, counts) + weights])
    geo_n = NL + 1

    head, tail, geo, hid, dsl, mom, dpre, en1, yb = pl.pallas_call(
        functools.partial(first_kernel, images=images),
        in_specs=[VMEM] * 3 + [ANY] * 2 + [VMEM] * 6,
        out_specs=[VMEM] * 9,
        out_shape=[
            out(images, ch, ghost),
            out(images, ch, ghost),
            out(images, geo_n, slots, atoms),
            out(images, slots, rh, atoms),
            out(images, slots, rh, atoms),
            out(images, NL, ch, atoms),
            out(images, ch, atoms),
            out(images, 8, 128),
            out(images, slots, NL - 1, 8, atoms),
        ],
        scratch_shapes=[pltpu.VMEM((NL, rh, atoms), f32)],
        compiler_params=params,
        name="first",
    )(pos, plo, pup, before, after, idx, cnt, a1, b1, m1t, r1)

    hlo, hup = neighbours_of((head, tail), "space")

    rad, radl, oh = pl.pallas_call(
        functools.partial(radial_kernel, images=images),
        in_specs=[VMEM] * 4,
        out_specs=[VMEM] * 3,
        out_shape=[out(images, slots, ch, atoms)] * 2 + [half(images, extent, slots * atoms)],
        compiler_params=small,
        cost_estimate=pl.CostEstimate(flops=1 << 30, bytes_accessed=1 << 23, transcendentals=1 << 20),
        name="radial",
    )(idx, geo, a2, b2)
    dfh, dft, dlo, dup, dlen2, en2, q, dm = pl.pallas_call(
        functools.partial(second_kernel, images=images),
        in_specs=[VMEM] * 11,
        out_specs=[VMEM] * 8,
        out_shape=[out(images, ch, ghost)] * 4
        + [
            out(images, slots, atoms),
            out(images, 8, 128),
            out(images, slots, ch, atoms),
            out(images, NL, ch, atoms),
        ],
        scratch_shapes=[
            pltpu.VMEM((2 * ch, extent), bf16),
            pltpu.VMEM((2 * ch, slots * atoms), bf16),
        ],
        compiler_params=params,
        name="second",
    )(head, tail, hlo, hup, yb, oh, rad, radl, m2t, m2, r2)

    rlo, rup = neighbours_of((dlo, dup), "space")
    dy2 = pl.pallas_call(
        functools.partial(angular_kernel, images=images),
        in_specs=[VMEM] * 3,
        out_specs=VMEM,
        out_shape=out(images, NL - 1, slots, atoms),
        compiler_params=small,
        cost_estimate=pl.CostEstimate(flops=1 << 30, bytes_accessed=1 << 23, transcendentals=0),
        name="angular",
    )(rad, q, dm)

    own, flo, fup = pl.pallas_call(
        functools.partial(third_kernel, images=images),
        in_specs=[VMEM] * 16,
        out_specs=[VMEM] * 3,
        out_shape=[out(3, images, atoms), out(3, images, ghost), out(3, images, ghost)],
        scratch_shapes=[
            pltpu.VMEM((NL, ch, atoms), f32),
            pltpu.VMEM((NL, rh, atoms), f32),
            pltpu.VMEM((NL - 1, slots, atoms), f32),
            pltpu.VMEM((slots, atoms), f32),
            pltpu.VMEM((3, slots, atoms), f32),
        ],
        compiler_params=params,
        name="third",
    )(dfh, dft, rlo, rup, yb, oh, geo, hid, dsl, mom, dpre, dy2, dlen2, b1t, m1, r1)

    glo, gup = neighbours_of((flo, fup), "space")

    rank = chain * space
    force, send = pl.pallas_call(
        functools.partial(partial_kernel, chain=chain),
        in_specs=[VMEM] * 11 + [SMEM],
        out_specs=[VMEM] * 2,
        out_shape=[out(3, images, atoms), out(rank, 128)],
        compiler_params=small,
        name="partial",
    )(own, glo, gup, pos, before, after, start_state, end_state, vel, en1, en2, climb_index)
    got = lax.all_to_all(
        send.reshape(rank, 1, 128), ("image", "space"), split_axis=0, concat_axis=0
    ).reshape(rank, 128)
    neb, vnext, pnext, energy = pl.pallas_call(
        functools.partial(final_kernel, chain=chain, slabs=space),
        in_specs=[VMEM] * 8,
        out_specs=[VMEM] * 3 + [SMEM],
        out_shape=[out(3, images, atoms)] * 3 + [out(images)],
        compiler_params=small,
        name="final",
    )(got, force, pos, before, after, start_state, end_state, vel)
    return (
        neb.transpose(1, 0, 2),
        vnext.transpose(1, 0, 2),
        pnext.transpose(1, 0, 2),
        energy,
    )


def solution(mesh):
    in_specs = (
        P("image", None, "space"),
        P("image", None, "space"),
        P(None, "space"),
        P(None, "space"),
        P("image", None, "space"),
        P("image", "space"),
        P(),
        P(),
        P(),
        P(),
        P(),
        P(),
        P(),
        P(),
        P(),
    )
    out_specs = (
        P("image", None, "space"),
        P("image", None, "space"),
        P("image", None, "space"),
        P("image"),
    )
    return jax.shard_map(local, mesh=mesh, in_specs=in_specs, out_specs=out_specs, check_vma=False)
```
